32 devices in a mesh: groups: 2 (over y), ctx: 16 (over z, x, core).
Axes of the slice: x: 2, y: 2, z: 4, core: 2. Of those that a mesh axis runs over, the one named last changes fastest.
Arguments:
- features: bfloat16 [12288, 5760], P(('groups', 'ctx')), parts along dimension 0, may hold values from -6 to 6
- positions: int32 [12288], P(('groups', 'ctx')), parts along dimension 0, may hold values from 0 to 4095, as said below
- counts: int32 [32], P(('groups', 'ctx')), parts along dimension 0, may hold values from 128 to 384, as said below
- conv_weight: float32 [3, 5760], replicated, may hold values from -3.5 to 3.5
- pole_rate: float32 [16, 1920], replicated, may hold values from 4.8828125e-05 to 0.15
- pole_residue: float32 [16, 1920], replicated, may hold values from -0.5 to 0.5
- skip_gain: float32 [1920], replicated, may hold values from 0.5 to 1.5
- out_weight: bfloat16 [1920, 1920], replicated, may hold values from -0.125 to 0.125
Outputs:
- block_out: bfloat16 [8192, 1920], P(('groups', 'ctx')), parts along dimension 0
The draws below stay inside these ranges and needn't reach their ends.
There are 2 independent parts, one for each index of `groups`. The reference program is written for one: setup_inputs(seed, part) draws one part's arguments, and reference() takes and returns one part's arrays. A program takes and returns all parts, laid end to end along the dimension named above; an argument that names none is the same for every part. Nothing has to cross between parts.
Inputs may be any that keep to these rules, and one draw needn't show every extreme that they name: Among the live slots of all sampler devices every position 0 to 4095 stands exactly once; the owner of a position is position // 256; at most 32 live slots of one sampler device have the same owner, and some sampler device has exactly 32 for some owner; slots that are not live hold arbitrary positions. The counts sum to 4096; at least one device has exactly 384 and at least one exactly 128.
All inputs are finite; a program needn't handle non-finite values.
Results may differ from the reference program's by a relative error of at most 0.0051.
Values may be sent and summed in bfloat16 or wider, within the bound.
A program may use at most 128 MiB of HBM per device.

```python
import math
import jax
import jax.numpy as jnp
from jax import lax

D = 1920
POLES = 16
KERNEL = 3
TOK_DEV = 256
SEQ = 4096
FEAT = 5760
CAP = 384
SLOTS = 6144
PAIR = 16
N_CTX = 16


def sender_layout(key):
    base = jax.random.fold_in(key, 7)
    keys = jax.random.split(base, 7)
    half_count = N_CTX // 2
    half_pair = PAIR // 2
    levels_half = jax.random.randint(keys[0], (half_count,), -half_pair, half_pair + 1)
    levels_half = levels_half.at[0].set(half_pair)
    order = jax.random.permutation(keys[1], N_CTX)
    levels = jnp.concatenate([levels_half, -levels_half])[order]
    first_perm = jax.random.permutation(keys[2], N_CTX)
    offset_shift = jax.random.randint(keys[3], (), 1, N_CTX)
    owner_ids = jnp.arange(N_CTX)
    second_perm = first_perm[(owner_ids - offset_shift) % N_CTX]
    first_hit = (first_perm[:, None] == owner_ids[None, :]).astype(jnp.int32)
    second_hit = (second_perm[:, None] == owner_ids[None, :]).astype(jnp.int32)
    matrix = PAIR + levels[:, None] + half_pair * (first_hit - second_hit)
    counts = TOK_DEV + N_CTX * levels
    inclusive = jnp.cumsum(matrix, axis=1)
    exclusive = inclusive - matrix
    earlier = jnp.cumsum(matrix, axis=0) - matrix
    slot_ids = jnp.arange(CAP)
    owners = jnp.sum((inclusive[:, None, :] <= slot_ids[None, :, None]).astype(jnp.int32), axis=2)
    owners = jnp.minimum(owners, N_CTX - 1)
    within = slot_ids[None, :] - jnp.take_along_axis(exclusive, owners, axis=1)
    index = jnp.clip(jnp.take_along_axis(earlier, owners, axis=1) + within, 0, TOK_DEV - 1)

    def owner_perm(sub_key):
        return jax.random.permutation(sub_key, TOK_DEV)
    perms = jax.vmap(owner_perm)(jax.random.split(keys[4], N_CTX))
    local = perms[owners, index]
    ordered = owners * TOK_DEV + local
    is_live = slot_ids[None, :] < counts[:, None]
    scores = jax.random.randint(keys[5], (N_CTX, CAP), 0, CAP) * CAP + slot_ids[None, :]
    scores = jnp.where(is_live, scores, CAP * CAP + slot_ids[None, :])
    shuffle = jnp.argsort(scores, axis=1, stable=True)
    placed_pos = jnp.take_along_axis(ordered, shuffle, axis=1)
    garbage = jax.random.randint(keys[6], (N_CTX, CAP), 0, SEQ)
    positions = jnp.where(is_live, placed_pos, garbage)
    return (positions.reshape(-1).astype(jnp.int32), counts.astype(jnp.int32))


def draw_positions(key, part):
    positions, counts = sender_layout(key)
    return positions


def draw_counts(key, part):
    positions, counts = sender_layout(key)
    return counts


def pole_table(key):
    base = jax.random.fold_in(key, 11)
    keys = jax.random.split(base, 4)
    share = 0.5
    slow = jax.random.bernoulli(keys[0], share, (POLES, D))
    slow_rate = jnp.exp(jax.random.uniform(keys[1], (POLES, D), jnp.float32, math.log(0.2), math.log(2.0))) / SEQ
    fast_rate = jnp.exp(jax.random.uniform(keys[2], (POLES, D), jnp.float32, math.log(0.04), math.log(0.15)))
    rate = jnp.where(slow, slow_rate, fast_rate)
    raw = jnp.clip(jax.random.normal(keys[3], (POLES, D), jnp.float32), -3.5, 3.5)
    residue = raw * jnp.sqrt(2.0 * rate + 2.0 / SEQ) * 0.25
    return (rate, residue)


def draw_pole_rate(key, part):
    rate, residue = pole_table(key)
    return rate


def draw_pole_residue(key, part):
    rate, residue = pole_table(key)
    return residue


def block_levels(key, extent, pieces, low, largest):
    level = 1.0
    for dim, blocks in pieces:
        heights = jax.random.uniform(jax.random.fold_in(jax.random.fold_in(key, 6), dim), (blocks,), jnp.float32, low / len(pieces), largest / len(pieces))
        level = level * jnp.repeat(jnp.exp(heights), extent[dim] // blocks).reshape((-1,) + (1,) * (len(extent) - 1 - dim))
    return level


def scatter_about(key, shape, width, bound, pieces=(), kind=jnp.bfloat16):
    gain = block_levels(key, shape, pieces, -0.22, 0.18) if pieces else 1.0
    values = jax.random.normal(key, shape, jnp.float32) * width * gain
    return jnp.minimum(jnp.maximum(values, -bound), bound).astype(kind)


def setup_inputs(seed: int = 0, part: int = 0) -> dict:
    seeds = jax.random.split(jax.random.key(seed), 9)
    part_keys = jax.random.split(jax.random.fold_in(seeds[8], part), 9)
    return {
        "features": scatter_about(part_keys[0], (SLOTS, FEAT), 1.0, 6.0, ((0, 16),)),
        "positions": draw_positions(jax.random.fold_in(jax.random.fold_in(seeds[8], part), 71), part),
        "counts": draw_counts(jax.random.fold_in(jax.random.fold_in(seeds[8], part), 71), part),
        "conv_weight": scatter_about(seeds[3], (KERNEL, FEAT), KERNEL ** -0.5, 3.5, (), jnp.float32),
        "pole_rate": draw_pole_rate(jax.random.fold_in(seeds[8], 71), part),
        "pole_residue": draw_pole_residue(jax.random.fold_in(seeds[8], 71), part),
        "skip_gain": jnp.clip(jax.random.uniform(seeds[6], (D,), jnp.float32, 0.5, 1.5), 0.5, 1.5),
        "out_weight": scatter_about(seeds[7], (D, D), D ** -0.5, 0.125),
    }


def reference(features, positions, counts, conv_weight, pole_rate, pole_residue, skip_gain, out_weight):
    seq_len = TOK_DEV * N_CTX
    slot_count = TOK_DEV * 3 // 2
    slot_ids = jnp.arange(slot_count).astype(jnp.int32)
    is_live = slot_ids[None, :] < counts[:, None]
    grid_pos = positions.reshape(N_CTX, slot_count)
    target = jnp.where(is_live, grid_pos, seq_len).reshape(-1).astype(jnp.int32)
    placed = jnp.zeros((seq_len + 1, 3 * D), jnp.bfloat16).at[target].set(features)[:seq_len]
    padded = jnp.concatenate([jnp.zeros((KERNEL - 1, 3 * D), jnp.bfloat16), placed], axis=0)
    featured = jnp.zeros((seq_len, 3 * D), jnp.float32)
    for tap in range(KERNEL):
        start = KERNEL - 1 - tap
        featured = featured + conv_weight[tap][None, :] * padded[start:start + seq_len].astype(jnp.float32)
    query_feat = featured[:, :D]
    key_feat = featured[:, D:2 * D]
    value_feat = featured[:, 2 * D:]
    product = key_feat * value_feat
    block_len = 64
    num_blocks = seq_len // block_len
    lag_steps = jnp.arange(block_len).astype(jnp.float32)
    powers = jnp.exp(-pole_rate[None] * lag_steps[:, None, None])
    filter_taps = jnp.einsum('jpc,pc->jc', powers, pole_residue, precision=lax.Precision.HIGHEST)
    lag_ids = jnp.arange(block_len).astype(jnp.int32)
    offsets = lag_ids[:, None] - lag_ids[None, :]
    toeplitz = jnp.where((offsets >= 0)[:, :, None], filter_taps[jnp.clip(offsets, 0, block_len - 1)], 0.0)
    end_weights = jnp.exp(-pole_rate[None] * (block_len - 1 - lag_steps)[:, None, None])
    inward = pole_residue[None] * jnp.exp(-pole_rate[None] * (lag_steps + 1.0)[:, None, None])
    decay_blk = jnp.exp(-pole_rate * float(block_len))

    def advance(running, blocked):
        inside = jnp.einsum('tsc,sc->tc', toeplitz, blocked, precision=lax.Precision.HIGHEST)
        from_state = jnp.einsum('tpc,pc->tc', inward, running, precision=lax.Precision.HIGHEST)
        update = jnp.einsum('spc,sc->pc', end_weights, blocked, precision=lax.Precision.HIGHEST)
        return decay_blk * running + update, inside + from_state

    start_state = jnp.zeros((POLES, D), jnp.float32)
    final_state, convolved = lax.scan(advance, start_state, product.reshape(num_blocks, block_len, D))
    filtered = skip_gain[None, :] * product + convolved.reshape(seq_len, D)
    gated = (query_feat * filtered).astype(jnp.bfloat16)
    return jnp.dot(gated, out_weight, preferred_element_type=jnp.float32).astype(jnp.bfloat16)
```

```python
import functools

import jax
import jax.numpy as jnp
from jax import lax
from jax.experimental import pallas as pl
from jax.experimental.pallas import tpu as pltpu
from jax.sharding import PartitionSpec as P

LANES = 128
ROWS = 8
MESH = pl.DeviceIdType.MESH
f32, bf16 = jnp.float32, jnp.bfloat16

block_len = 32


def from_behind(array, axis, by):
    count = lax.axis_size(axis)
    pairs = [(i, i + by) for i in range(count) if 0 <= i + by < count]
    return lax.ppermute(array, axis, pairs)


def plain_on_device(
    features, positions, counts, conv_weight, pole_rate, pole_residue, skip_gain, out_weight
):
    devices = lax.axis_size("ctx")
    slot_count = features.shape[0]
    feat_width = features.shape[1]
    channels = feat_width // 3
    tok_rows = 2 * slot_count // 3
    pair_cap = 2 * tok_rows // devices
    taps = conv_weight.shape[0]
    poles = pole_rate.shape[0]
    slot_ids = jnp.arange(slot_count, dtype=jnp.int32)
    is_live = slot_ids < counts[0]
    owners = jnp.where(is_live, positions // tok_rows, devices)
    same = jnp.logical_and(owners[:, None] == owners[None, :], slot_ids[None, :] < slot_ids[:, None])
    within = jnp.sum(same.astype(jnp.int32), axis=1)
    flat_index = jnp.where(is_live, owners * pair_cap + within, devices * pair_cap)
    outbox = (
        jnp.zeros((devices * pair_cap + 1, feat_width), features.dtype)
        .at[flat_index]
        .set(features)[:-1]
    )
    local_pos = (
        jnp.full((devices * pair_cap + 1,), -1, jnp.int32)
        .at[flat_index]
        .set(positions % tok_rows)[:-1]
    )
    outbox = outbox.reshape(devices, pair_cap, feat_width)
    local_pos = local_pos.reshape(devices, pair_cap)
    arrived, arrived_pos = (
        lax.all_to_all(outbox, "ctx", split_axis=0, concat_axis=0, tiled=True),
        lax.all_to_all(local_pos, "ctx", split_axis=0, concat_axis=0, tiled=True),
    )
    target = jnp.where(arrived_pos >= 0, arrived_pos, tok_rows).reshape(-1)
    placed = (
        jnp.zeros((tok_rows + 1, feat_width), features.dtype)
        .at[target]
        .set(arrived.reshape(-1, feat_width))[:-1]
    )
    rim_rows = from_behind(placed[tok_rows - (taps - 1) :], "ctx", 1)
    extended = jnp.concatenate([rim_rows, placed], axis=0)
    featured = jnp.zeros((tok_rows, feat_width), jnp.float32)
    for tap in range(taps):
        start = taps - 1 - tap
        featured = featured + conv_weight[tap][None, :] * extended[start : start + tok_rows].astype(
            jnp.float32
        )
    query_feat = featured[:, :channels]
    product = featured[:, channels : 2 * channels] * featured[:, 2 * channels :]
    num_blocks = tok_rows // block_len
    lag_steps = jnp.arange(block_len + 1).astype(jnp.float32)
    powers = jnp.exp(-pole_rate[None] * lag_steps[:, None, None])
    filter_taps = jnp.sum(powers[:block_len] * pole_residue[None], axis=1)
    blocked = product.reshape(num_blocks, block_len, channels)
    padded_blk = jnp.pad(blocked, ((0, 0), (block_len - 1, 0), (0, 0)))
    inside = jnp.zeros((num_blocks, block_len, channels), jnp.float32)
    for lag in range(block_len):
        first = block_len - 1 - lag
        inside = inside + filter_taps[lag][None, None, :] * padded_blk[:, first : first + block_len]
    blk_sums = jnp.zeros((num_blocks, poles, channels), jnp.float32)
    for row in range(block_len):
        blk_sums = blk_sums + powers[block_len - 1 - row][None] * blocked[:, row][:, None, :]
    decay_blk = powers[block_len]

    def advance(running, block_sum):
        return (decay_blk * running + block_sum, running)

    local_end, starts = lax.scan(advance, jnp.zeros((poles, channels), jnp.float32), blk_sums)
    decay_dev = jnp.exp(-pole_rate * float(tok_rows))

    def relay_step(counter, incoming):
        return from_behind(decay_dev * incoming + local_end, "ctx", 1)

    carry_in = lax.fori_loop(0, devices - 1, relay_step, jnp.zeros_like(local_end))
    block_starts = (jnp.arange(num_blocks) * block_len).astype(jnp.float32)
    block_decay = jnp.exp(-pole_rate[None] * block_starts[:, None, None])
    incoming = starts + block_decay * carry_in[None]
    inward = pole_residue[None] * powers[1:]
    from_state = jnp.zeros((num_blocks, block_len, channels), jnp.float32)
    for pole in range(poles):
        from_state = from_state + inward[:, pole][None] * incoming[:, pole][:, None, :]
    convolved = (inside + from_state).reshape(tok_rows, channels)
    filtered = skip_gain[None, :] * product + convolved
    gated_rows = (query_feat * filtered).astype(jnp.bfloat16)
    return jnp.dot(gated_rows, out_weight, preferred_element_type=jnp.float32).astype(jnp.bfloat16)

def col_tile(width):
    for tile in (384, 256, 128):
        if width % tile == 0:
            return tile
    return width


def scan_spans(n):
    spans, span = [], 1
    while span < n:
        spans.append(span)
        span *= 4
    return spans


def mega(
    n, cap, tok, up_front,
    counts, feats_hbm, pos, convw, rate, resid, skip, w_hbm, out,
    box_kv, box_q, arr_kv, arr_q, hot_s, place_s, prod, filt, gated, natural, state,
    feats, decay, rim_kv_out, rim_kv_in, rim_q_out, rim_q_in, own, acc, tx, rx, w_vmem,
    send_kv, recv_kv, send_q, recv_q, rim_sems, scan_send, scan_recv, self_sems, w_sem, f_sems,
):
    me = lax.axis_index("ctx")
    slots, feat = feats_hbm.shape
    ch = feat // 3
    poles = rate.shape[0]
    steps = tok // ROWS
    tile = col_tile(ch)
    rows = n * cap
    barrier = pltpu.get_barrier_semaphore()

    bits = (n - 1).bit_length()

    def mask_of(d):
        return sum(((d // (1 << b)) % 2) * (1 << (bits - 1 - b)) for b in range(bits))

    def peer_of(d):
        m = mask_of(d)
        return sum(((me // (1 << b) + m // (1 << b)) % 2) * (1 << b) for b in range(bits))

    def greet(d, c):
        pl.semaphore_signal(barrier, inc=1, device_id={"ctx": peer_of(d)}, device_id_type=MESH)
        return c

    lax.fori_loop(1, n, greet, 0)
    kv_cols = pl.ds(ch, 2 * ch)
    f_kv = pltpu.make_async_copy(feats_hbm.at[:, kv_cols], feats.at[:, kv_cols], f_sems.at[0])
    f_q = pltpu.make_async_copy(feats_hbm.at[:, pl.ds(0, ch)], feats.at[:, pl.ds(0, ch)], f_sems.at[1])
    f_kv.start()
    f_q.start()
    w_copy = pltpu.make_async_copy(w_hbm, w_vmem, w_sem)
    w_copy.start()

    p = pos[...].reshape(1, slots)
    shift = tok.bit_length() - 1
    live = lax.broadcasted_iota(jnp.int32, (1, slots), 1) < counts[0]
    owner = jnp.where(live, lax.shift_right_logical(p, shift), -1)
    local = lax.bitwise_and(p, tok - 1).astype(f32)
    mine = owner == lax.broadcasted_iota(jnp.int32, (n, slots), 0)
    tri = lax.broadcasted_iota(jnp.int32, (slots, slots), 0) <= lax.broadcasted_iota(
        jnp.int32, (slots, slots), 1
    )
    cum = jnp.dot(mine.astype(f32).astype(bf16), tri.astype(f32).astype(bf16), preferred_element_type=f32)
    rank = jnp.sum(jnp.where(mine, cum, 0.0), axis=0, keepdims=True) - 1.0
    flat = owner.astype(f32) * float(cap) + rank
    hit = lax.broadcasted_iota(jnp.int32, (rows, slots), 0).astype(f32) == flat
    hot_s[...] = hit.astype(f32).astype(bf16)
    marks = jnp.sum(jnp.where(hit, local + 1.0, 0.0), axis=1, keepdims=True) - 1.0
    box_kv[:, 2 * ch :] = jnp.broadcast_to(marks, (rows, LANES)).astype(bf16)

    def pack_kv(c, _):
        src = pl.ds(pl.multiple_of(ch + c * tile, LANES), tile)
        dst = pl.ds(pl.multiple_of(c * tile, LANES), tile)
        box_kv[:, dst] = jnp.dot(hot_s[...], feats[:, src], preferred_element_type=f32).astype(bf16)
        return _

    def pack_q(c, _):
        dst = pl.ds(pl.multiple_of(c * tile, LANES), tile)
        box_q[:, dst] = jnp.dot(hot_s[...], feats[:, dst], preferred_element_type=f32).astype(bf16)
        return _

    f_kv.wait()
    lax.fori_loop(0, 2 * ch // tile, pack_kv, 0)

    def slab(ref, k):
        return ref.at[pl.ds(pl.multiple_of(k * cap, cap), cap), :]

    def outgoing(box, arr, send, recv, d):
        to = peer_of(d)
        return pltpu.make_async_remote_copy(
            src_ref=slab(box, to), dst_ref=slab(arr, me), send_sem=send.at[d], recv_sem=recv.at[d],
            device_id={"ctx": to}, device_id_type=MESH,
        )

    def incoming(box, arr, send, recv, d):
        came = peer_of(d)
        return pltpu.make_async_remote_copy(
            src_ref=slab(box, came), dst_ref=slab(arr, came), send_sem=send.at[d], recv_sem=recv.at[d],
            device_id={"ctx": came}, device_id_type=MESH,
        )

    def start_kv(d, c):
        outgoing(box_kv, arr_kv, send_kv, recv_kv, d).start()
        return c

    def start_q(d, c):
        outgoing(box_q, arr_q, send_q, recv_q, d).start()
        return c

    def recv_kv_wait(d, c):
        incoming(box_kv, arr_kv, send_kv, recv_kv, d).wait_recv()
        return c

    def recv_q_wait(d, c):
        incoming(box_q, arr_q, send_q, recv_q, d).wait_recv()
        return c

    def send_waits(d, c):
        outgoing(box_kv, arr_kv, send_kv, recv_kv, d).wait_send()
        outgoing(box_q, arr_q, send_q, recv_q, d).wait_send()
        return c

    pl.semaphore_wait(barrier, n - 1)
    lax.fori_loop(1, n, start_kv, 0)
    own_kv = pltpu.make_async_copy(slab(box_kv, me), slab(arr_kv, me), self_sems.at[0])
    own_kv.start()
    f_q.wait()
    lax.fori_loop(0, ch // tile, pack_q, 0)
    own_q = pltpu.make_async_copy(slab(box_q, me), slab(arr_q, me), self_sems.at[1])
    own_q.start()
    lax.fori_loop(1, 1 + up_front, start_q, 0)
    decay[...] = jnp.exp(-rate[...])

    own_kv.wait()
    lax.fori_loop(1, n, recv_kv_wait, 0)

    ext = tok + 2 * ROWS
    came_pos = jnp.transpose(arr_kv[:, 2 * ch :].astype(f32))[0:1, :]
    row = lax.broadcasted_iota(jnp.int32, (ext, 1), 0)
    want = lax.bitwise_and(row, ROWS - 1) * steps + lax.shift_right_logical(row, 3) - 2
    want = jnp.where(want < 0, -100, want).astype(f32)
    place_s[...] = (want == came_pos).astype(f32).astype(bf16)
    rim_row = lax.broadcasted_iota(jnp.int32, (16, 1), 0)
    rim_want = jnp.where(rim_row < 2, rim_row + tok - 2, -100).astype(f32)
    rim_hot = (rim_want == came_pos).astype(f32).astype(bf16)

    def rim_copy(src, dst, k, to):
        return pltpu.make_async_remote_copy(
            src_ref=src, dst_ref=dst, send_sem=rim_sems.at[2 * k], recv_sem=rim_sems.at[2 * k + 1],
            device_id={"ctx": to}, device_id_type=MESH,
        )

    after, before = lax.rem(me + 1, n), lax.rem(me + n - 1, n)

    def rim_kv_tile(c, _):
        cols = pl.ds(pl.multiple_of(c * tile, LANES), tile)
        rim_kv_out[:, cols] = jnp.dot(rim_hot, arr_kv[:, cols], preferred_element_type=f32).astype(bf16)
        return _

    def rim_q_tile(c, _):
        cols = pl.ds(pl.multiple_of(c * tile, LANES), tile)
        rim_q_out[:, cols] = jnp.dot(rim_hot, arr_q[:, cols], preferred_element_type=f32).astype(bf16)
        return _

    lax.fori_loop(0, 2 * ch // tile, rim_kv_tile, 0)
    rim_kv = rim_copy(rim_kv_out, rim_kv_in, 0, after)
    rim_kv.start()
    spans = scan_spans(n)
    cuts = [1]
    for share in PACE:
        cuts.append(min(n, cuts[-1] + share * (n - 1) // 15))
    lax.fori_loop(cuts[1], cuts[2], start_q, 0)
    rim_copy(rim_kv_out, rim_kv_in, 0, before).wait_recv()

    sub = lax.broadcasted_iota(jnp.int32, (ROWS, 1), 0)
    first = jnp.logical_and(sub == 0, me > 0)

    def featured(arr, at, w_at, rim, rim_at):
        x = jnp.dot(place_s[...], arr[:, pl.ds(pl.multiple_of(at, LANES), tile)], preferred_element_type=f32)
        w = convw[:, pl.ds(pl.multiple_of(w_at, LANES), tile)]
        y = w[0:1] * x[2 * ROWS :] + w[1:2] * x[ROWS : ROWS + tok] + w[2:3] * x[:tok]
        if rim is None:
            return y
        edge = rim[:, pl.ds(pl.multiple_of(rim_at, LANES), tile)].astype(f32)
        top = jnp.where(first, w[1:2] * edge[1:2] + w[2:3] * edge[0:1], 0.0)
        nxt = jnp.where(first, w[2:3] * edge[1:2], 0.0)
        return jnp.concatenate([y[:ROWS] + top, y[ROWS : 2 * ROWS] + nxt, y[2 * ROWS :]], axis=0)

    def product_tile(c, _):
        at = c * tile
        k = featured(arr_kv, at, ch + at, rim_kv_in, at)
        v = featured(arr_kv, ch + at, 2 * ch + at, rim_kv_in, ch + at)
        prod[:, pl.ds(pl.multiple_of(at, LANES), tile)] = k * v
        return _

    lax.fori_loop(0, ch // tile, product_tile, 0)
    lax.fori_loop(cuts[2], cuts[3], start_q, 0)

    def spread(ref, k, cols):
        return jnp.broadcast_to(ref[k : k + 1, cols], (ROWS, LANES))

    later = ((ROWS - 1 - sub) * steps).astype(f32)

    def total(terms):
        while len(terms) > 1:
            terms = [a + b for a, b in zip(terms[::2], terms[1::2])] + terms[len(terms) // 2 * 2 :]
        return terms[0]

    def local_tile(c, _):
        cols = pl.ds(pl.multiple_of(c * LANES, LANES), LANES)
        dec = [spread(decay, k, cols) for k in range(poles)]
        res = [spread(resid, k, cols) for k in range(poles)]
        gain = jnp.broadcast_to(skip[pl.ds(pl.multiple_of(c * LANES, LANES), LANES)].reshape(1, LANES), (ROWS, LANES))

        def step(i, st):
            at = pl.ds(pl.multiple_of(i * ROWS, ROWS), ROWS)
            x = prod[at, cols]
            st = tuple(d * s + x for d, s in zip(dec, st))
            filt[at, cols] = gain * x + total([r * s for r, s in zip(res, st)])
            return st

        zero = jnp.zeros((ROWS, LANES), f32)
        st = lax.fori_loop(0, steps, step, (zero,) * poles, unroll=2)
        for k in range(poles):
            state[k, :, cols] = st[k]
            fade = jnp.exp(-rate[k : k + 1, cols] * later)
            own[k : k + 1, cols] = jnp.sum(fade * st[k], axis=0, keepdims=True)
        return _

    half = ch // LANES // 2
    lax.fori_loop(0, half, local_tile, 0)
    lax.fori_loop(cuts[3], cuts[4], start_q, 0)
    lax.fori_loop(half, ch // LANES, local_tile, 0)

    def scan_copy(k, j, to):
        return pltpu.make_async_remote_copy(
            src_ref=tx.at[k], dst_ref=rx.at[3 * k + j - 1], send_sem=scan_send.at[3 * k + j - 1],
            recv_sem=scan_recv.at[3 * k + j - 1], device_id={"ctx": to}, device_id_type=MESH,
        )

    def scan_moves(k, send, act):
        span = spans[k]
        for j in range(1, 4):
            if j * span < n:
                to = me + j * span if send else me - j * span
                act(scan_copy(k, j, lax.rem(to + n, n)))

    acc[0] = jnp.zeros((poles, ch), f32)
    for k, span in enumerate(spans):
        tx[k] = own[...].astype(bf16)
        scan_moves(k, True, lambda copy: copy.start())
        stop = n if k == len(spans) - 1 or 5 + k >= len(cuts) else cuts[5 + k]
        lax.fori_loop(cuts[4 + k] if 4 + k < len(cuts) else n, stop, start_q, 0)
        scan_moves(k, False, lambda copy: copy.wait_recv())
        for j in range(1, 4):
            if j * span < n:
                got = jnp.where(me >= j * span, rx[3 * k + j - 1].astype(f32), 0.0)
                acc[0] = acc[0] + jnp.exp(-rate[...] * float(tok * (j * span - 1))) * got
                if k < len(spans) - 1:
                    own[...] = own[...] + jnp.exp(-rate[...] * float(tok * j * span)) * got

    def carry_tile(c, _):
        cols = pl.ds(pl.multiple_of(c * LANES, LANES), LANES)
        dec = [spread(decay, k, cols) for k in range(poles)]
        start = []
        for k in range(poles):
            r = rate[k : k + 1, cols]
            x = jnp.where(sub == 0, acc[0, k : k + 1, cols], pltpu.roll(state[k, :, cols], 1, 0))
            for by in (1, 2, 4):
                fade = jnp.exp(-r * float(steps * by))
                x = x + jnp.where(sub >= by, fade * pltpu.roll(x, by, 0), 0.0)
            start.append(resid[k : k + 1, cols] * x)

        def step(i, g):
            at = pl.ds(pl.multiple_of(i * ROWS, ROWS), ROWS)
            g = tuple(d * s for d, s in zip(dec, g))
            filt[at, cols] = filt[at, cols] + total(list(g))
            return g

        lax.fori_loop(0, steps, step, tuple(start), unroll=2)
        return _

    lax.fori_loop(0, ch // LANES, carry_tile, 0)

    own_q.wait()
    lax.fori_loop(1, n, recv_q_wait, 0)
    lax.fori_loop(0, ch // tile, rim_q_tile, 0)
    rim_q = rim_copy(rim_q_out, rim_q_in, 1, after)
    rim_q.start()

    def query_tile(c, _):
        at = c * tile
        prod[:, pl.ds(pl.multiple_of(at, LANES), tile)] = featured(arr_q, at, at, None, at)
        return _

    lax.fori_loop(0, ch // tile, query_tile, 0)
    rim_copy(rim_q_out, rim_q_in, 1, before).wait_recv()
    edge = rim_q_in[...].astype(f32)
    w1, w2 = convw[1:2, 0:ch], convw[2:3, 0:ch]
    prod[0:ROWS, :] = prod[0:ROWS, :] + jnp.where(first, w1 * edge[1:2] + w2 * edge[0:1], 0.0)
    prod[ROWS : 2 * ROWS, :] = prod[ROWS : 2 * ROWS, :] + jnp.where(first, w2 * edge[1:2], 0.0)

    nat = lax.broadcasted_iota(jnp.int32, (tok, 1), 0)
    seat = lax.bitwise_and(nat, steps - 1) * ROWS + lax.shift_right_logical(nat, steps.bit_length() - 1)
    order = (seat == lax.broadcasted_iota(jnp.int32, (tok, tok), 1)).astype(f32).astype(bf16)

    def gate_tile(c, _):
        cols = pl.ds(pl.multiple_of(c * tile, LANES), tile)
        rows_g = (prod[:, cols] * filt[:, cols]).astype(bf16)
        natural[:, cols] = jnp.dot(order, rows_g, preferred_element_type=f32).astype(bf16)
        return _

    lax.fori_loop(0, ch // tile, gate_tile, 0)
    w_copy.wait()

    def out_tile(c, _):
        cols = pl.ds(pl.multiple_of(c * tile, LANES), tile)
        out[:, cols] = jnp.dot(natural[...], w_vmem[:, cols], preferred_element_type=f32).astype(bf16)
        return _

    lax.fori_loop(0, ch // tile, out_tile, 0)

    lax.fori_loop(1, n, send_waits, 0)
    rim_kv.wait_send()
    rim_q.wait_send()
    for k in range(len(spans)):
        scan_moves(k, True, lambda copy: copy.wait_send())


def swift(
    n, groups, cap, base, tok,
    counts, feats_hbm, pos, convw, rate, resid, skip, w_hbm, out, most,
    box_kv, box_q, arr_kv, arr_q, mark_out, mark_in, group_out, group_in,
    hot_s, place_s, prod, filt, natural, state,
    feats, decay, rim_kv_out, rim_kv_in, rim_q_out, rim_q_in, own, acc, tx, rx, w_vmem,
    send_kv, recv_kv, send_q, recv_q, send_m, recv_m, send_g, recv_g,
    over_send_kv, over_recv_kv, over_send_q, over_recv_q, raw,
    rim_sems, scan_send, scan_recv, self_sems, w_sem, f_sems,
):
    me = lax.axis_index("ctx")
    group = lax.axis_index("groups")
    slots, feat = feats_hbm.shape
    ch = feat // 3
    poles = rate.shape[0]
    steps = tok // ROWS
    tile = col_tile(ch)
    rows = n * cap
    over = cap - base
    half_n = n // 2
    barrier = pltpu.get_barrier_semaphore()
    bits = (n - 1).bit_length()

    def flip(a, m):
        return sum(((a // (1 << b) + m // (1 << b)) % 2) * (1 << b) for b in range(bits))

    def greet(m, c):
        pl.semaphore_signal(barrier, inc=1, device_id={"ctx": flip(me, m)}, device_id_type=MESH)
        return c

    lax.fori_loop(1, n, greet, 0)
    for g in range(1, groups):
        pl.semaphore_signal(barrier, inc=1, device_id={"groups": lax.rem(group + g, groups)}, device_id_type=MESH)
    kv_cols = pl.ds(ch, 2 * ch)
    f_kv = pltpu.make_async_copy(feats_hbm.at[:, kv_cols], feats.at[:, kv_cols], f_sems.at[0])
    f_q = pltpu.make_async_copy(feats_hbm.at[:, pl.ds(0, ch)], feats.at[:, pl.ds(0, ch)], f_sems.at[1])
    f_kv.start()
    f_q.start()
    w_copy = pltpu.make_async_copy(w_hbm, w_vmem, w_sem)
    w_copy.start()

    p = pos[...].reshape(1, slots)
    shift = tok.bit_length() - 1
    live = lax.broadcasted_iota(jnp.int32, (1, slots), 1) < counts[0]
    owner = jnp.where(live, lax.shift_right_logical(p, shift), -1)
    local = lax.bitwise_and(p, tok - 1).astype(f32)
    mine = owner == lax.broadcasted_iota(jnp.int32, (n, slots), 0)
    tri = lax.broadcasted_iota(jnp.int32, (slots, slots), 0) <= lax.broadcasted_iota(
        jnp.int32, (slots, slots), 1
    )
    tri = tri.astype(f32).astype(bf16)
    cum = jnp.dot(mine.astype(f32).astype(bf16), tri, preferred_element_type=f32)
    rank = jnp.sum(jnp.where(mine, cum, 0.0), axis=0, keepdims=True) - 1.0
    direct = jnp.logical_and(live, rank < float(base))
    beyond = jnp.logical_and(live, rank >= float(base)).astype(f32)
    bump = jnp.dot(jnp.broadcast_to(beyond, (16, slots)).astype(bf16), tri, preferred_element_type=f32)[0:1]
    late = jnp.where(beyond > 0.0, bump - 1.0, -1.0)
    apart = lax.bitwise_xor(owner, me)
    flat = jnp.where(direct, apart.astype(f32) * float(cap) + rank, -1.0)
    spare = jnp.where(late >= 0.0, late + float(base), -1.0)
    hot_row = lax.broadcasted_iota(jnp.int32, (rows, slots), 0)
    hit = jnp.logical_or(hot_row.astype(f32) == flat, lax.bitwise_and(hot_row, cap - 1).astype(f32) == spare)
    hot_s[...] = hit.astype(f32).astype(bf16)

    def pack_rows(box, first, c0):
        def pack(c, _):
            at = pl.ds(pl.multiple_of(first, rows // 2), rows // 2)
            src = pl.ds(pl.multiple_of(c0 + c * tile, LANES), tile)
            dst = pl.ds(pl.multiple_of(c * tile, LANES), tile)
            box[at, dst] = jnp.dot(hot_s[at, :], feats[:, src], preferred_element_type=f32).astype(bf16)
            return _

        return pack

    def slab(ref, k, size):
        return ref.at[pl.ds(pl.multiple_of(k * cap, cap), size), :]

    def over_rows(ref, k):
        return ref.at[pl.ds(pl.multiple_of(k * cap + base, ROWS), over), :]

    def direct_copy(which, m, size, came):
        box, arr, send, recv = which
        to = flip(me, m)
        return pltpu.make_async_remote_copy(
            src_ref=slab(box, m, size), dst_ref=slab(arr, to if came else me, size), send_sem=send.at[m],
            recv_sem=recv.at[m], device_id={"ctx": to}, device_id_type=MESH,
        )

    def to_mirror(which, came):
        box, arr, send, recv = which
        to = flip(me, half_n)
        return pltpu.make_async_remote_copy(
            src_ref=over_rows(box, half_n), dst_ref=over_rows(arr, to if came else me), send_sem=send.at[0],
            recv_sem=recv.at[0], device_id={"ctx": to}, device_id_type=MESH,
        )

    def forward(which, m, came):
        box, arr, send, recv = which
        to = flip(me, m)
        rows_of = over_rows(arr, flip(to if came else me, half_n))
        return pltpu.make_async_remote_copy(
            src_ref=rows_of, dst_ref=rows_of, send_sem=send.at[m], recv_sem=recv.at[m],
            device_id={"ctx": to}, device_id_type=MESH,
        )

    kv_direct = (box_kv, arr_kv, send_kv, recv_kv)
    q_direct = (box_q, arr_q, send_q, recv_q)
    kv_over = (box_kv, arr_kv, over_send_kv, over_recv_kv)
    q_over = (box_q, arr_q, over_send_q, over_recv_q)

    def each(first, last, make, act):
        def one(m, c):
            act(make(m))
            return c

        lax.fori_loop(first, last, one, 0)

    def start(copy):
        copy.start()

    def arrive(copy):
        copy.wait_recv()

    def sent(copy):
        copy.wait_send()

    def near(which, came=False):
        return lambda m: direct_copy(which, m, cap, came)

    def far(which, came=False):
        return lambda m: direct_copy(which, m, base, came)

    def spread_over(which, came=False):
        return lambda m: forward(which, m, came)

    def marks_to(m, to, came):
        return pltpu.make_async_remote_copy(
            src_ref=mark_out.at[to], dst_ref=mark_in.at[came], send_sem=send_m.at[m], recv_sem=recv_m.at[m],
            device_id={"ctx": to}, device_id_type=MESH,
        )

    def start_marks(m, c):
        marks_to(m, flip(me, m), me).start()
        return c

    def recv_marks(m, c):
        marks_to(m, flip(me, m), flip(me, m)).wait_recv()
        return c

    f_kv.wait()
    lax.fori_loop(0, 2 * ch // tile, pack_rows(box_kv, rows // 2, ch), 0)
    pl.semaphore_wait(barrier, n - 1 + groups - 1)
    to_mirror(kv_over, False).start()
    each(half_n, n, far(kv_direct), start)
    lax.fori_loop(0, 2 * ch // tile, pack_rows(box_kv, 0, ch), 0)
    each(1, half_n, near(kv_direct), start)
    own_kv = pltpu.make_async_copy(slab(box_kv, 0, cap), slab(arr_kv, me, cap), self_sems.at[0])
    own_kv.start()

    seats = (lax.broadcasted_iota(jnp.int32, (LANES, slots), 0) - lax.rem(me * cap, LANES)).astype(f32)
    in_slab = jnp.logical_and(seats >= 0.0, seats < float(cap))
    at_base = jnp.logical_and(direct, seats == rank)
    at_over = jnp.logical_and(in_slab, jnp.logical_and(late >= 0.0, seats - float(base) == late))
    last_dims = (((1,), (1,)), ((), ()))
    sub16 = lax.broadcasted_iota(jnp.int32, (16, slots), 0)
    two = jnp.where(sub16 == 0, local + 1.0, jnp.where(sub16 == 1, owner.astype(f32), 0.0)).astype(bf16)
    tell = lax.dot_general(
        jnp.where(mine, local + 1.0, 0.0).astype(bf16), at_base.astype(f32).astype(bf16), last_dims,
        preferred_element_type=f32,
    )
    tell = jnp.where(tell > 0.0, tell + (lax.broadcasted_iota(jnp.int32, (n, LANES), 0) * tok).astype(f32), 0.0)
    extra = lax.dot_general(two, at_over.astype(f32).astype(bf16), last_dims, preferred_element_type=f32)
    tell = tell + (extra[0:1] + extra[1:2] * float(tok))
    held = jnp.broadcast_to(jnp.sum(beyond, axis=1, keepdims=True), (1, LANES))
    for k in range(n):
        mark_out[k, 0:1, :] = tell[k : k + 1, :]
        mark_out[k, 1:2, :] = held
    mark_in[me] = mark_out[me]
    lax.fori_loop(1, n, start_marks, 0)

    to_mirror(kv_over, True).wait_recv()
    each(1, half_n, spread_over(kv_over), start)

    f_q.wait()
    lax.fori_loop(0, ch // tile, pack_rows(box_q, rows // 2, 0), 0)
    to_mirror(q_over, False).start()
    lax.fori_loop(0, ch // tile, pack_rows(box_q, 0, 0), 0)
    own_q = pltpu.make_async_copy(slab(box_q, 0, cap), slab(arr_q, me, cap), self_sems.at[1])
    own_q.start()
    decay[...] = jnp.exp(-rate[...])

    lax.fori_loop(1, n, recv_marks, 0)
    lanes_of = [
        sum(mark_in[k, 0:1, :] for k in range(g * (LANES // cap), (g + 1) * (LANES // cap)))
        for g in range(rows // LANES)
    ]
    came_pos = jnp.concatenate(lanes_of, axis=1) - 1.0
    worst = mark_in[0, 1:2, :]
    for k in range(1, n):
        worst = jnp.maximum(worst, mark_in[k, 1:2, :])
    group_out[...] = jnp.broadcast_to(worst, (ROWS, LANES))

    def group_copy(g, to):
        return pltpu.make_async_remote_copy(
            src_ref=group_out, dst_ref=group_in.at[g], send_sem=send_g.at[g], recv_sem=recv_g.at[g],
            device_id={"groups": to}, device_id_type=MESH,
        )

    for g in range(1, groups):
        group_copy(g, lax.rem(group + g, groups)).start()

    ext = tok + 2 * ROWS
    row = lax.broadcasted_iota(jnp.int32, (ext, 1), 0)
    want = lax.bitwise_and(row, ROWS - 1) * steps + lax.shift_right_logical(row, 3) - 2
    want = jnp.where(want < 0, -100, want + me * tok).astype(f32)
    place_s[...] = (want == came_pos).astype(f32).astype(bf16)
    rim_row = lax.broadcasted_iota(jnp.int32, (16, 1), 0)
    rim_want = jnp.where(rim_row < 2, rim_row + me * tok + tok - 2, -100).astype(f32)
    rim_hot = (rim_want == came_pos).astype(f32).astype(bf16)

    to_mirror(q_over, True).wait_recv()
    each(1, half_n, spread_over(q_over), start)
    own_kv.wait()
    each(1, half_n, near(kv_direct, True), arrive)
    each(1, half_n, near(q_direct), start)
    each(1, half_n, spread_over(kv_over, True), arrive)
    cuts = [half_n]
    for share in FLOW:
        cuts.append(min(n, cuts[-1] + share * half_n // 8))
    each(half_n, cuts[0] + n - cuts[1], far(kv_direct, True), arrive)
    ahead = cuts[1] - half_n

    def kv_then_q(m, c):
        far(kv_direct, True)(m).wait_recv()
        far(q_direct)(m - n + cuts[1]).start()
        return c

    lax.fori_loop(n - ahead, n, kv_then_q, 0)

    def rim_copy(src, dst, k, to):
        return pltpu.make_async_remote_copy(
            src_ref=src, dst_ref=dst, send_sem=rim_sems.at[2 * k], recv_sem=rim_sems.at[2 * k + 1],
            device_id={"ctx": to}, device_id_type=MESH,
        )

    after, before = lax.rem(me + 1, n), lax.rem(me + n - 1, n)

    def rim_tile(arr, rim):
        def fill(c, _):
            cols = pl.ds(pl.multiple_of(c * tile, LANES), tile)
            rim[:, cols] = jnp.dot(rim_hot, arr[:, cols], preferred_element_type=f32).astype(bf16)
            return _

        return fill

    lax.fori_loop(0, 2 * ch // tile, rim_tile(arr_kv, rim_kv_out), 0)
    rim_kv = rim_copy(rim_kv_out, rim_kv_in, 0, after)
    rim_kv.start()
    spans = scan_spans(n)

    sub = lax.broadcasted_iota(jnp.int32, (ROWS, 1), 0)
    first = jnp.logical_and(sub == 0, me > 0)

    def featured(arr, at, w_at):
        x = jnp.dot(place_s[...], arr[:, pl.ds(pl.multiple_of(at, LANES), tile)], preferred_element_type=f32)
        w = convw[:, pl.ds(pl.multiple_of(w_at, LANES), tile)]
        return w[0:1] * x[2 * ROWS :] + w[1:2] * x[ROWS : ROWS + tok] + w[2:3] * x[:tok]

    def product_tile(c, _):
        at = c * tile
        k = featured(arr_kv, at, ch + at)
        v = featured(arr_kv, ch + at, 2 * ch + at)
        raw[:, pl.ds(pl.multiple_of(at, LANES), tile)] = k[: 2 * ROWS]
        raw[:, pl.ds(pl.multiple_of(ch + at, LANES), tile)] = v[: 2 * ROWS]
        prod[:, pl.ds(pl.multiple_of(at, LANES), tile)] = k * v
        return _

    lax.fori_loop(0, ch // tile, product_tile, 0)
    each(cuts[1], cuts[2], far(q_direct), start)
    rim_copy(rim_kv_out, rim_kv_in, 0, before).wait_recv()

    def edge_tile(c, _):
        def with_edge(at):
            cols = pl.ds(pl.multiple_of(at, LANES), tile)
            w = convw[:, pl.ds(pl.multiple_of(ch + at, LANES), tile)]
            edge = rim_kv_in[:, cols].astype(f32)
            top = jnp.where(first, w[1:2] * edge[1:2] + w[2:3] * edge[0:1], 0.0)
            nxt = jnp.where(first, w[2:3] * edge[1:2], 0.0)
            return jnp.concatenate([raw[0:ROWS, cols] + top, raw[ROWS:, cols] + nxt], axis=0)

        at = c * tile
        prod[0 : 2 * ROWS, pl.ds(pl.multiple_of(at, LANES), tile)] = with_edge(at) * with_edge(ch + at)
        return _

    lax.fori_loop(0, ch // tile, edge_tile, 0)

    def spread(ref, k, cols):
        return jnp.broadcast_to(ref[k : k + 1, cols], (ROWS, LANES))

    later = ((ROWS - 1 - sub) * steps).astype(f32)

    def total(terms):
        while len(terms) > 1:
            terms = [a + b for a, b in zip(terms[::2], terms[1::2])] + terms[len(terms) // 2 * 2 :]
        return terms[0]

    def local_tile(c, _):
        cols = pl.ds(pl.multiple_of(c * LANES, LANES), LANES)
        dec = [spread(decay, k, cols) for k in range(poles)]
        res = [spread(resid, k, cols) for k in range(poles)]
        gain = jnp.broadcast_to(skip[pl.ds(pl.multiple_of(c * LANES, LANES), LANES)].reshape(1, LANES), (ROWS, LANES))

        def step(i, st):
            at = pl.ds(pl.multiple_of(i * ROWS, ROWS), ROWS)
            x = prod[at, cols]
            st = tuple(d * s + x for d, s in zip(dec, st))
            filt[at, cols] = gain * x + total([r * s for r, s in zip(res, st)])
            return st

        zero = jnp.zeros((ROWS, LANES), f32)
        st = lax.fori_loop(0, steps, step, (zero,) * poles, unroll=2)
        for k in range(poles):
            state[k, :, cols] = st[k]
            fade = jnp.exp(-rate[k : k + 1, cols] * later)
            own[k : k + 1, cols] = jnp.sum(fade * st[k], axis=0, keepdims=True)
        return _

    middle = (ch // LANES + 1) // 2
    parts = [(0, middle), (middle, ch // LANES)]

    def scan_copy(part, k, j, to):
        cols = pl.ds(part[0] * LANES, (part[1] - part[0]) * LANES)
        at = (3 * k + j - 1) * len(parts) + parts.index(part)
        return pltpu.make_async_remote_copy(
            src_ref=tx.at[k, :, cols], dst_ref=rx.at[3 * k + j - 1, :, cols], send_sem=scan_send.at[at],
            recv_sem=scan_recv.at[at], device_id={"ctx": to}, device_id_type=MESH,
        )

    def scan_moves(part, k, send, act):
        span = spans[k]
        for j in range(1, 4):
            if j * span < n:
                to = me + j * span if send else me - j * span
                act(scan_copy(part, k, j, lax.rem(to + n, n)))

    def scan_start(part, k):
        cols = pl.ds(part[0] * LANES, (part[1] - part[0]) * LANES)
        tx[k, :, cols] = own[:, cols].astype(bf16)
        scan_moves(part, k, True, start)

    def scan_take(part, k):
        span = spans[k]
        cols = pl.ds(part[0] * LANES, (part[1] - part[0]) * LANES)
        scan_moves(part, k, False, arrive)
        r = rate[:, cols]
        for j in range(1, 4):
            if j * span < n:
                got = jnp.where(me >= j * span, rx[3 * k + j - 1, :, cols].astype(f32), 0.0)
                acc[0, :, cols] = acc[0, :, cols] + jnp.exp(-r * float(tok * (j * span - 1))) * got
                if k < len(spans) - 1:
                    own[:, cols] = own[:, cols] + jnp.exp(-r * float(tok * j * span)) * got

    acc[0] = jnp.zeros((poles, ch), f32)
    for part in parts:
        lax.fori_loop(part[0], part[1], local_tile, 0)
        scan_start(part, 0)
    each(cuts[2], cuts[3], far(q_direct), start)
    for k in range(len(spans) - 1):
        for part in parts:
            scan_take(part, k)
            scan_start(part, k + 1)
    each(cuts[3], n, far(q_direct), start)

    def carry_tile(c, _):
        cols = pl.ds(pl.multiple_of(c * LANES, LANES), LANES)
        dec = [spread(decay, k, cols) for k in range(poles)]
        start = []
        for k in range(poles):
            r = rate[k : k + 1, cols]
            x = jnp.where(sub == 0, acc[0, k : k + 1, cols], pltpu.roll(state[k, :, cols], 1, 0))
            for by in (1, 2, 4):
                fade = jnp.exp(-r * float(steps * by))
                x = x + jnp.where(sub >= by, fade * pltpu.roll(x, by, 0), 0.0)
            start.append(resid[k : k + 1, cols] * x)

        def step(i, g):
            at = pl.ds(pl.multiple_of(i * ROWS, ROWS), ROWS)
            g = tuple(d * s for d, s in zip(dec, g))
            filt[at, cols] = filt[at, cols] + total(list(g))
            return g

        lax.fori_loop(0, steps, step, tuple(start), unroll=2)
        return _

    for part in parts:
        scan_take(part, len(spans) - 1)
        lax.fori_loop(part[0], part[1], carry_tile, 0)
    top_of = worst
    for g in range(1, groups):
        group_copy(g, lax.rem(group + groups - g, groups)).wait_recv()
        top_of = jnp.maximum(top_of, group_in[g, 0:1, :])
    most[...] = jnp.broadcast_to(top_of, (ROWS, LANES))
    w_copy.wait()

    own_q.wait()
    each(1, half_n, near(q_direct, True), arrive)
    each(1, half_n, spread_over(q_over, True), arrive)
    each(half_n, n, far(q_direct, True), arrive)
    lax.fori_loop(0, ch // tile, rim_tile(arr_q, rim_q_out), 0)
    rim_q = rim_copy(rim_q_out, rim_q_in, 1, after)
    rim_q.start()

    def query_tile(c, _):
        at = c * tile
        prod[:, pl.ds(pl.multiple_of(at, LANES), tile)] = featured(arr_q, at, at)
        return _

    lax.fori_loop(0, ch // tile, query_tile, 0)
    rim_copy(rim_q_out, rim_q_in, 1, before).wait_recv()
    edge = rim_q_in[...].astype(f32)
    w1, w2 = convw[1:2, 0:ch], convw[2:3, 0:ch]
    prod[0:ROWS, :] = prod[0:ROWS, :] + jnp.where(first, w1 * edge[1:2] + w2 * edge[0:1], 0.0)
    prod[ROWS : 2 * ROWS, :] = prod[ROWS : 2 * ROWS, :] + jnp.where(first, w2 * edge[1:2], 0.0)

    nat = lax.broadcasted_iota(jnp.int32, (tok, 1), 0)
    seat = lax.bitwise_and(nat, steps - 1) * ROWS + lax.shift_right_logical(nat, steps.bit_length() - 1)
    order = (seat == lax.broadcasted_iota(jnp.int32, (tok, tok), 1)).astype(f32).astype(bf16)

    def gate_tile(c, _):
        cols = pl.ds(pl.multiple_of(c * tile, LANES), tile)
        rows_g = (prod[:, cols] * filt[:, cols]).astype(bf16)
        natural[:, cols] = jnp.dot(order, rows_g, preferred_element_type=f32).astype(bf16)
        return _

    lax.fori_loop(0, ch // tile, gate_tile, 0)

    def out_tile(c, _):
        cols = pl.ds(pl.multiple_of(c * tile, LANES), tile)
        out[:, cols] = jnp.dot(natural[...], w_vmem[:, cols], preferred_element_type=f32).astype(bf16)
        return _

    lax.fori_loop(0, ch // tile, out_tile, 0)

    for which in (kv_direct, q_direct):
        each(1, half_n, near(which), sent)
        each(half_n, n, far(which), sent)
    for which in (kv_over, q_over):
        to_mirror(which, False).wait_send()
        each(1, half_n, spread_over(which), sent)
    each(1, n, lambda m: marks_to(m, flip(me, m), me), sent)
    for g in range(1, groups):
        group_copy(g, lax.rem(group + g, groups)).wait_send()
    rim_kv.wait_send()
    rim_q.wait_send()
    for k in range(len(spans)):
        for part in parts:
            scan_moves(part, k, True, sent)


def swift_call(n, groups, cap, base, tok, args):
    counts, features, positions, conv_weight, pole_rate, pole_residue, skip_gain, out_weight = args
    slots, feat = features.shape
    ch = feat // 3
    poles = pole_rate.shape[0]
    rows = n * cap
    stages = len(scan_spans(n))
    whole = pl.BlockSpec(memory_space=pltpu.VMEM)
    dma = pltpu.SemaphoreType.DMA
    vmem = pltpu.VMEM
    return pl.pallas_call(
        functools.partial(swift, n, groups, cap, base, tok),
        out_shape=(jax.ShapeDtypeStruct((tok, ch), bf16), jax.ShapeDtypeStruct((ROWS, LANES), f32)),
        in_specs=[pl.BlockSpec(memory_space=pltpu.SMEM), pl.BlockSpec(memory_space=pl.ANY)]
        + [whole] * 5 + [pl.BlockSpec(memory_space=pl.ANY)],
        out_specs=(whole, whole),
        scratch_shapes=[
            vmem((rows, 2 * ch), bf16),
            vmem((rows, ch), bf16),
            vmem((rows, 2 * ch), bf16),
            vmem((rows, ch), bf16),
            vmem((n, 2, LANES), f32),
            vmem((n, 2, LANES), f32),
            vmem((ROWS, LANES), f32),
            vmem((groups, ROWS, LANES), f32),
            vmem((rows, slots), bf16),
            vmem((tok + 2 * ROWS, rows), bf16),
            vmem((tok, ch), f32),
            vmem((tok, ch), f32),
            vmem((tok, ch), bf16),
            vmem((poles, ROWS, ch), f32),
            vmem((slots, feat), bf16),
            vmem((poles, ch), f32),
            vmem((16, 2 * ch), bf16),
            vmem((16, 2 * ch), bf16),
            vmem((16, ch), bf16),
            vmem((16, ch), bf16),
            vmem((poles, ch), f32),
            vmem((1, poles, ch), f32),
            vmem((stages, poles, ch), bf16),
            vmem((3 * stages, poles, ch), bf16),
            vmem(out_weight.shape, bf16),
        ]
        + [dma((n,))] * 6
        + [dma((groups,))] * 2
        + [dma((n,))] * 4
        + [vmem((2 * ROWS, 2 * ch), f32)]
        + [dma((4,)), dma((6 * stages,)), dma((6 * stages,)), dma((2,)), dma, dma((2,))],
        compiler_params=pltpu.CompilerParams(
            collective_id=1, has_side_effects=True, vmem_limit_bytes=60 << 20
        ),
        name="hyena_direct",
    )(*args)


def mega_call(n, cap, tok, args):
    counts, features, positions, conv_weight, pole_rate, pole_residue, skip_gain, out_weight = args
    slots, feat = features.shape
    ch = feat // 3
    poles = pole_rate.shape[0]
    rows = n * cap
    stages = len(scan_spans(n))
    whole = pl.BlockSpec(memory_space=pltpu.VMEM)
    dma = pltpu.SemaphoreType.DMA
    return pl.pallas_call(
        functools.partial(mega, n, cap, tok, PACE[0] * (n - 1) // 15),
        out_shape=jax.ShapeDtypeStruct((tok, ch), bf16),
        in_specs=[pl.BlockSpec(memory_space=pltpu.SMEM), pl.BlockSpec(memory_space=pl.ANY)]
        + [whole] * 5 + [pl.BlockSpec(memory_space=pl.ANY)],
        out_specs=whole,
        scratch_shapes=[
            pltpu.VMEM((rows, 2 * ch + LANES), bf16),
            pltpu.VMEM((rows, ch), bf16),
            pltpu.VMEM((rows, 2 * ch + LANES), bf16),
            pltpu.VMEM((rows, ch), bf16),
            pltpu.VMEM((rows, slots), bf16),
            pltpu.VMEM((tok + 2 * ROWS, rows), bf16),
            pltpu.VMEM((tok, ch), f32),
            pltpu.VMEM((tok, ch), f32),
            pltpu.VMEM((16, LANES), bf16),
            pltpu.VMEM((tok, ch), bf16),
            pltpu.VMEM((poles, ROWS, ch), f32),
            pltpu.VMEM((slots, feat), bf16),
            pltpu.VMEM((poles, ch), f32),
            pltpu.VMEM((16, 2 * ch), bf16),
            pltpu.VMEM((16, 2 * ch), bf16),
            pltpu.VMEM((16, ch), bf16),
            pltpu.VMEM((16, ch), bf16),
            pltpu.VMEM((poles, ch), f32),
            pltpu.VMEM((1, poles, ch), f32),
            pltpu.VMEM((stages, poles, ch), bf16),
            pltpu.VMEM((3 * stages, poles, ch), bf16),
            pltpu.VMEM(out_weight.shape, bf16),
            dma((n,)), dma((n,)), dma((n,)), dma((n,)), dma((4,)), dma((3 * stages,)), dma((3 * stages,)),
            dma((2,)), dma, dma((2,)),
        ],
        compiler_params=pltpu.CompilerParams(
            collective_id=0, has_side_effects=True, vmem_limit_bytes=60 << 20
        ),
        name="hyena",
    )(*args)


def on_device(
    features, positions, counts, conv_weight, pole_rate, pole_residue, skip_gain, out_weight
):
    n = lax.axis_size("ctx")
    groups = lax.axis_size("groups")
    slots, feat = features.shape
    ch = feat // 3
    tok = 2 * slots // 3
    cap = 2 * tok // n
    if cap % 16 or tok & (tok - 1) or tok > 256 or conv_weight.shape[0] != 3 or ch % LANES or n & (n - 1) or n < 4:
        return plain_on_device(
            features, positions, counts, conv_weight, pole_rate, pole_residue, skip_gain, out_weight
        )
    args = (counts, features, positions, conv_weight, pole_rate, pole_residue, skip_gain, out_weight)
    base = slots // n
    if base % ROWS or cap - base > 16 or LANES % cap:
        return mega_call(n, cap, tok, args)
    done, most = swift_call(n, groups, cap, base, tok, args)
    return lax.cond(most[0, 0] > float(cap - base), lambda d: mega_call(n, cap, tok, args), lambda d: d, done)


PACE = (2, 1, 1, 2, 2)
FLOW = (3, 1, 2)


def solution(mesh):
    return jax.shard_map(
        on_device,
        mesh=mesh,
        in_specs=(
            P(("groups", "ctx"), None),
            P(("groups", "ctx")),
            P(("groups", "ctx")),
            P(),
            P(),
            P(),
            P(),
            P(),
        ),
        out_specs=P(("groups", "ctx"), None),
        check_vma=False,
    )
```

```python
import functools

import jax
import jax.numpy as jnp
from jax import lax
from jax.experimental import pallas as pl
from jax.experimental.pallas import tpu as pltpu
from jax.sharding import PartitionSpec as P

LANES = 128
ROWS = 8
MESH = pl.DeviceIdType.MESH
f32, bf16 = jnp.float32, jnp.bfloat16

block_len = 32


def from_behind(array, axis, by):
    count = lax.axis_size(axis)
    pairs = [(i, i + by) for i in range(count) if 0 <= i + by < count]
    return lax.ppermute(array, axis, pairs)


def plain_on_device(
    features, positions, counts, conv_weight, pole_rate, pole_residue, skip_gain, out_weight
):
    devices = lax.axis_size("ctx")
    slot_count = features.shape[0]
    feat_width = features.shape[1]
    channels = feat_width // 3
    tok_rows = 2 * slot_count // 3
    pair_cap = 2 * tok_rows // devices
    taps = conv_weight.shape[0]
    poles = pole_rate.shape[0]
    slot_ids = jnp.arange(slot_count, dtype=jnp.int32)
    is_live = slot_ids < counts[0]
    owners = jnp.where(is_live, positions // tok_rows, devices)
    same = jnp.logical_and(owners[:, None] == owners[None, :], slot_ids[None, :] < slot_ids[:, None])
    within = jnp.sum(same.astype(jnp.int32), axis=1)
    flat_index = jnp.where(is_live, owners * pair_cap + within, devices * pair_cap)
    outbox = (
        jnp.zeros((devices * pair_cap + 1, feat_width), features.dtype)
        .at[flat_index]
        .set(features)[:-1]
    )
    local_pos = (
        jnp.full((devices * pair_cap + 1,), -1, jnp.int32)
        .at[flat_index]
        .set(positions % tok_rows)[:-1]
    )
    outbox = outbox.reshape(devices, pair_cap, feat_width)
    local_pos = local_pos.reshape(devices, pair_cap)
    arrived, arrived_pos = (
        lax.all_to_all(outbox, "ctx", split_axis=0, concat_axis=0, tiled=True),
        lax.all_to_all(local_pos, "ctx", split_axis=0, concat_axis=0, tiled=True),
    )
    target = jnp.where(arrived_pos >= 0, arrived_pos, tok_rows).reshape(-1)
    placed = (
        jnp.zeros((tok_rows + 1, feat_width), features.dtype)
        .at[target]
        .set(arrived.reshape(-1, feat_width))[:-1]
    )
    rim_rows = from_behind(placed[tok_rows - (taps - 1) :], "ctx", 1)
    extended = jnp.concatenate([rim_rows, placed], axis=0)
    featured = jnp.zeros((tok_rows, feat_width), jnp.float32)
    for tap in range(taps):
        start = taps - 1 - tap
        featured = featured + conv_weight[tap][None, :] * extended[start : start + tok_rows].astype(
            jnp.float32
        )
    query_feat = featured[:, :channels]
    product = featured[:, channels : 2 * channels] * featured[:, 2 * channels :]
    num_blocks = tok_rows // block_len
    lag_steps = jnp.arange(block_len + 1).astype(jnp.float32)
    powers = jnp.exp(-pole_rate[None] * lag_steps[:, None, None])
    filter_taps = jnp.sum(powers[:block_len] * pole_residue[None], axis=1)
    blocked = product.reshape(num_blocks, block_len, channels)
    padded_blk = jnp.pad(blocked, ((0, 0), (block_len - 1, 0), (0, 0)))
    inside = jnp.zeros((num_blocks, block_len, channels), jnp.float32)
    for lag in range(block_len):
        first = block_len - 1 - lag
        inside = inside + filter_taps[lag][None, None, :] * padded_blk[:, first : first + block_len]
    blk_sums = jnp.zeros((num_blocks, poles, channels), jnp.float32)
    for row in range(block_len):
        blk_sums = blk_sums + powers[block_len - 1 - row][None] * blocked[:, row][:, None, :]
    decay_blk = powers[block_len]

    def advance(running, block_sum):
        return (decay_blk * running + block_sum, running)

    local_end, starts = lax.scan(advance, jnp.zeros((poles, channels), jnp.float32), blk_sums)
    decay_dev = jnp.exp(-pole_rate * float(tok_rows))

    def relay_step(counter, incoming):
        return from_behind(decay_dev * incoming + local_end, "ctx", 1)

    carry_in = lax.fori_loop(0, devices - 1, relay_step, jnp.zeros_like(local_end))
    block_starts = (jnp.arange(num_blocks) * block_len).astype(jnp.float32)
    block_decay = jnp.exp(-pole_rate[None] * block_starts[:, None, None])
    incoming = starts + block_decay * carry_in[None]
    inward = pole_residue[None] * powers[1:]
    from_state = jnp.zeros((num_blocks, block_len, channels), jnp.float32)
    for pole in range(poles):
        from_state = from_state + inward[:, pole][None] * incoming[:, pole][:, None, :]
    convolved = (inside + from_state).reshape(tok_rows, channels)
    filtered = skip_gain[None, :] * product + convolved
    gated_rows = (query_feat * filtered).astype(jnp.bfloat16)
    return jnp.dot(gated_rows, out_weight, preferred_element_type=jnp.float32).astype(jnp.bfloat16)

def col_tile(width):
    for tile in (384, 256, 128):
        if width % tile == 0:
            return tile
    return width


def scan_spans(n):
    spans, span = [], 1
    while span < n:
        spans.append(span)
        span *= 4
    return spans


def mega(
    n, cap, tok, up_front,
    counts, feats_hbm, pos, convw, rate, resid, skip, w_hbm, out,
    box_kv, box_q, arr_kv, arr_q, hot_s, place_s, prod, filt, gated, natural, state,
    feats, decay, rim_kv_out, rim_kv_in, rim_q_out, rim_q_in, own, acc, tx, rx, w_vmem,
    send_kv, recv_kv, send_q, recv_q, rim_sems, scan_send, scan_recv, self_sems, w_sem, f_sems,
):
    me = lax.axis_index("ctx")
    slots, feat = feats_hbm.shape
    ch = feat // 3
    poles = rate.shape[0]
    steps = tok // ROWS
    tile = col_tile(ch)
    rows = n * cap
    barrier = pltpu.get_barrier_semaphore()

    bits = (n - 1).bit_length()

    def mask_of(d):
        return sum(((d // (1 << b)) % 2) * (1 << (bits - 1 - b)) for b in range(bits))

    def peer_of(d):
        m = mask_of(d)
        return sum(((me // (1 << b) + m // (1 << b)) % 2) * (1 << b) for b in range(bits))

    def greet(d, c):
        pl.semaphore_signal(barrier, inc=1, device_id={"ctx": peer_of(d)}, device_id_type=MESH)
        return c

    lax.fori_loop(1, n, greet, 0)
    kv_cols = pl.ds(ch, 2 * ch)
    f_kv = pltpu.make_async_copy(feats_hbm.at[:, kv_cols], feats.at[:, kv_cols], f_sems.at[0])
    f_q = pltpu.make_async_copy(feats_hbm.at[:, pl.ds(0, ch)], feats.at[:, pl.ds(0, ch)], f_sems.at[1])
    f_kv.start()
    f_q.start()
    w_copy = pltpu.make_async_copy(w_hbm, w_vmem, w_sem)
    w_copy.start()

    p = pos[...].reshape(1, slots)
    shift = tok.bit_length() - 1
    live = lax.broadcasted_iota(jnp.int32, (1, slots), 1) < counts[0]
    owner = jnp.where(live, lax.shift_right_logical(p, shift), -1)
    local = lax.bitwise_and(p, tok - 1).astype(f32)
    mine = owner == lax.broadcasted_iota(jnp.int32, (n, slots), 0)
    tri = lax.broadcasted_iota(jnp.int32, (slots, slots), 0) <= lax.broadcasted_iota(
        jnp.int32, (slots, slots), 1
    )
    cum = jnp.dot(mine.astype(f32).astype(bf16), tri.astype(f32).astype(bf16), preferred_element_type=f32)
    rank = jnp.sum(jnp.where(mine, cum, 0.0), axis=0, keepdims=True) - 1.0
    flat = owner.astype(f32) * float(cap) + rank
    hit = lax.broadcasted_iota(jnp.int32, (rows, slots), 0).astype(f32) == flat
    hot_s[...] = hit.astype(f32).astype(bf16)
    marks = jnp.sum(jnp.where(hit, local + 1.0, 0.0), axis=1, keepdims=True) - 1.0
    box_kv[:, 2 * ch :] = jnp.broadcast_to(marks, (rows, LANES)).astype(bf16)

    def pack_kv(c, _):
        src = pl.ds(pl.multiple_of(ch + c * tile, LANES), tile)
        dst = pl.ds(pl.multiple_of(c * tile, LANES), tile)
        box_kv[:, dst] = jnp.dot(hot_s[...], feats[:, src], preferred_element_type=f32).astype(bf16)
        return _

    def pack_q(c, _):
        dst = pl.ds(pl.multiple_of(c * tile, LANES), tile)
        box_q[:, dst] = jnp.dot(hot_s[...], feats[:, dst], preferred_element_type=f32).astype(bf16)
        return _

    f_kv.wait()
    lax.fori_loop(0, 2 * ch // tile, pack_kv, 0)

    def slab(ref, k):
        return ref.at[pl.ds(pl.multiple_of(k * cap, cap), cap), :]

    def outgoing(box, arr, send, recv, d):
        to = peer_of(d)
        return pltpu.make_async_remote_copy(
            src_ref=slab(box, to), dst_ref=slab(arr, me), send_sem=send.at[d], recv_sem=recv.at[d],
            device_id={"ctx": to}, device_id_type=MESH,
        )

    def incoming(box, arr, send, recv, d):
        came = peer_of(d)
        return pltpu.make_async_remote_copy(
            src_ref=slab(box, came), dst_ref=slab(arr, came), send_sem=send.at[d], recv_sem=recv.at[d],
            device_id={"ctx": came}, device_id_type=MESH,
        )

    def start_kv(d, c):
        outgoing(box_kv, arr_kv, send_kv, recv_kv, d).start()
        return c

    def start_q(d, c):
        outgoing(box_q, arr_q, send_q, recv_q, d).start()
        return c

    def recv_kv_wait(d, c):
        incoming(box_kv, arr_kv, send_kv, recv_kv, d).wait_recv()
        return c

    def recv_q_wait(d, c):
        incoming(box_q, arr_q, send_q, recv_q, d).wait_recv()
        return c

    def send_waits(d, c):
        outgoing(box_kv, arr_kv, send_kv, recv_kv, d).wait_send()
        outgoing(box_q, arr_q, send_q, recv_q, d).wait_send()
        return c

    pl.semaphore_wait(barrier, n - 1)
    lax.fori_loop(1, n, start_kv, 0)
    own_kv = pltpu.make_async_copy(slab(box_kv, me), slab(arr_kv, me), self_sems.at[0])
    own_kv.start()
    f_q.wait()
    lax.fori_loop(0, ch // tile, pack_q, 0)
    own_q = pltpu.make_async_copy(slab(box_q, me), slab(arr_q, me), self_sems.at[1])
    own_q.start()
    lax.fori_loop(1, 1 + up_front, start_q, 0)
    decay[...] = jnp.exp(-rate[...])

    own_kv.wait()
    lax.fori_loop(1, n, recv_kv_wait, 0)

    ext = tok + 2 * ROWS
    came_pos = jnp.transpose(arr_kv[:, 2 * ch :].astype(f32))[0:1, :]
    row = lax.broadcasted_iota(jnp.int32, (ext, 1), 0)
    want = lax.bitwise_and(row, ROWS - 1) * steps + lax.shift_right_logical(row, 3) - 2
    want = jnp.where(want < 0, -100, want).astype(f32)
    place_s[...] = (want == came_pos).astype(f32).astype(bf16)
    rim_row = lax.broadcasted_iota(jnp.int32, (16, 1), 0)
    rim_want = jnp.where(rim_row < 2, rim_row + tok - 2, -100).astype(f32)
    rim_hot = (rim_want == came_pos).astype(f32).astype(bf16)

    def rim_copy(src, dst, k, to):
        return pltpu.make_async_remote_copy(
            src_ref=src, dst_ref=dst, send_sem=rim_sems.at[2 * k], recv_sem=rim_sems.at[2 * k + 1],
            device_id={"ctx": to}, device_id_type=MESH,
        )

    after, before = lax.rem(me + 1, n), lax.rem(me + n - 1, n)

    def rim_kv_tile(c, _):
        cols = pl.ds(pl.multiple_of(c * tile, LANES), tile)
        rim_kv_out[:, cols] = jnp.dot(rim_hot, arr_kv[:, cols], preferred_element_type=f32).astype(bf16)
        return _

    def rim_q_tile(c, _):
        cols = pl.ds(pl.multiple_of(c * tile, LANES), tile)
        rim_q_out[:, cols] = jnp.dot(rim_hot, arr_q[:, cols], preferred_element_type=f32).astype(bf16)
        return _

    lax.fori_loop(0, 2 * ch // tile, rim_kv_tile, 0)
    rim_kv = rim_copy(rim_kv_out, rim_kv_in, 0, after)
    rim_kv.start()
    spans = scan_spans(n)
    cuts = [1]
    for share in PACE:
        cuts.append(min(n, cuts[-1] + share * (n - 1) // 15))
    lax.fori_loop(cuts[1], cuts[2], start_q, 0)
    rim_copy(rim_kv_out, rim_kv_in, 0, before).wait_recv()

    sub = lax.broadcasted_iota(jnp.int32, (ROWS, 1), 0)
    first = jnp.logical_and(sub == 0, me > 0)

    def featured(arr, at, w_at, rim, rim_at):
        x = jnp.dot(place_s[...], arr[:, pl.ds(pl.multiple_of(at, LANES), tile)], preferred_element_type=f32)
        w = convw[:, pl.ds(pl.multiple_of(w_at, LANES), tile)]
        y = w[0:1] * x[2 * ROWS :] + w[1:2] * x[ROWS : ROWS + tok] + w[2:3] * x[:tok]
        if rim is None:
            return y
        edge = rim[:, pl.ds(pl.multiple_of(rim_at, LANES), tile)].astype(f32)
        top = jnp.where(first, w[1:2] * edge[1:2] + w[2:3] * edge[0:1], 0.0)
        nxt = jnp.where(first, w[2:3] * edge[1:2], 0.0)
        return jnp.concatenate([y[:ROWS] + top, y[ROWS : 2 * ROWS] + nxt, y[2 * ROWS :]], axis=0)

    def product_tile(c, _):
        at = c * tile
        k = featured(arr_kv, at, ch + at, rim_kv_in, at)
        v = featured(arr_kv, ch + at, 2 * ch + at, rim_kv_in, ch + at)
        prod[:, pl.ds(pl.multiple_of(at, LANES), tile)] = k * v
        return _

    lax.fori_loop(0, ch // tile, product_tile, 0)
    lax.fori_loop(cuts[2], cuts[3], start_q, 0)

    def spread(ref, k, cols):
        return jnp.broadcast_to(ref[k : k + 1, cols], (ROWS, LANES))

    later = ((ROWS - 1 - sub) * steps).astype(f32)

    def total(terms):
        while len(terms) > 1:
            terms = [a + b for a, b in zip(terms[::2], terms[1::2])] + terms[len(terms) // 2 * 2 :]
        return terms[0]

    def local_tile(c, _):
        cols = pl.ds(pl.multiple_of(c * LANES, LANES), LANES)
        dec = [spread(decay, k, cols) for k in range(poles)]
        res = [spread(resid, k, cols) for k in range(poles)]
        gain = jnp.broadcast_to(skip[pl.ds(pl.multiple_of(c * LANES, LANES), LANES)].reshape(1, LANES), (ROWS, LANES))

        def step(i, st):
            at = pl.ds(pl.multiple_of(i * ROWS, ROWS), ROWS)
            x = prod[at, cols]
            st = tuple(d * s + x for d, s in zip(dec, st))
            filt[at, cols] = gain * x + total([r * s for r, s in zip(res, st)])
            return st

        zero = jnp.zeros((ROWS, LANES), f32)
        st = lax.fori_loop(0, steps, step, (zero,) * poles, unroll=2)
        for k in range(poles):
            state[k, :, cols] = st[k]
            fade = jnp.exp(-rate[k : k + 1, cols] * later)
            own[k : k + 1, cols] = jnp.sum(fade * st[k], axis=0, keepdims=True)
        return _

    half = ch // LANES // 2
    lax.fori_loop(0, half, local_tile, 0)
    lax.fori_loop(cuts[3], cuts[4], start_q, 0)
    lax.fori_loop(half, ch // LANES, local_tile, 0)

    def scan_copy(k, j, to):
        return pltpu.make_async_remote_copy(
            src_ref=tx.at[k], dst_ref=rx.at[3 * k + j - 1], send_sem=scan_send.at[3 * k + j - 1],
            recv_sem=scan_recv.at[3 * k + j - 1], device_id={"ctx": to}, device_id_type=MESH,
        )

    def scan_moves(k, send, act):
        span = spans[k]
        for j in range(1, 4):
            if j * span < n:
                to = me + j * span if send else me - j * span
                act(scan_copy(k, j, lax.rem(to + n, n)))

    acc[0] = jnp.zeros((poles, ch), f32)
    for k, span in enumerate(spans):
        tx[k] = own[...].astype(bf16)
        scan_moves(k, True, lambda copy: copy.start())
        stop = n if k == len(spans) - 1 or 5 + k >= len(cuts) else cuts[5 + k]
        lax.fori_loop(cuts[4 + k] if 4 + k < len(cuts) else n, stop, start_q, 0)
        scan_moves(k, False, lambda copy: copy.wait_recv())
        for j in range(1, 4):
            if j * span < n:
                got = jnp.where(me >= j * span, rx[3 * k + j - 1].astype(f32), 0.0)
                acc[0] = acc[0] + jnp.exp(-rate[...] * float(tok * (j * span - 1))) * got
                if k < len(spans) - 1:
                    own[...] = own[...] + jnp.exp(-rate[...] * float(tok * j * span)) * got

    def carry_tile(c, _):
        cols = pl.ds(pl.multiple_of(c * LANES, LANES), LANES)
        dec = [spread(decay, k, cols) for k in range(poles)]
        start = []
        for k in range(poles):
            r = rate[k : k + 1, cols]
            x = jnp.where(sub == 0, acc[0, k : k + 1, cols], pltpu.roll(state[k, :, cols], 1, 0))
            for by in (1, 2, 4):
                fade = jnp.exp(-r * float(steps * by))
                x = x + jnp.where(sub >= by, fade * pltpu.roll(x, by, 0), 0.0)
            start.append(resid[k : k + 1, cols] * x)

        def step(i, g):
            at = pl.ds(pl.multiple_of(i * ROWS, ROWS), ROWS)
            g = tuple(d * s for d, s in zip(dec, g))
            filt[at, cols] = filt[at, cols] + total(list(g))
            return g

        lax.fori_loop(0, steps, step, tuple(start), unroll=2)
        return _

    lax.fori_loop(0, ch // LANES, carry_tile, 0)

    own_q.wait()
    lax.fori_loop(1, n, recv_q_wait, 0)
    lax.fori_loop(0, ch // tile, rim_q_tile, 0)
    rim_q = rim_copy(rim_q_out, rim_q_in, 1, after)
    rim_q.start()

    def query_tile(c, _):
        at = c * tile
        prod[:, pl.ds(pl.multiple_of(at, LANES), tile)] = featured(arr_q, at, at, None, at)
        return _

    lax.fori_loop(0, ch // tile, query_tile, 0)
    rim_copy(rim_q_out, rim_q_in, 1, before).wait_recv()
    edge = rim_q_in[...].astype(f32)
    w1, w2 = convw[1:2, 0:ch], convw[2:3, 0:ch]
    prod[0:ROWS, :] = prod[0:ROWS, :] + jnp.where(first, w1 * edge[1:2] + w2 * edge[0:1], 0.0)
    prod[ROWS : 2 * ROWS, :] = prod[ROWS : 2 * ROWS, :] + jnp.where(first, w2 * edge[1:2], 0.0)

    nat = lax.broadcasted_iota(jnp.int32, (tok, 1), 0)
    seat = lax.bitwise_and(nat, steps - 1) * ROWS + lax.shift_right_logical(nat, steps.bit_length() - 1)
    order = (seat == lax.broadcasted_iota(jnp.int32, (tok, tok), 1)).astype(f32).astype(bf16)

    def gate_tile(c, _):
        cols = pl.ds(pl.multiple_of(c * tile, LANES), tile)
        rows_g = (prod[:, cols] * filt[:, cols]).astype(bf16)
        natural[:, cols] = jnp.dot(order, rows_g, preferred_element_type=f32).astype(bf16)
        return _

    lax.fori_loop(0, ch // tile, gate_tile, 0)
    w_copy.wait()

    def out_tile(c, _):
        cols = pl.ds(pl.multiple_of(c * tile, LANES), tile)
        out[:, cols] = jnp.dot(natural[...], w_vmem[:, cols], preferred_element_type=f32).astype(bf16)
        return _

    lax.fori_loop(0, ch // tile, out_tile, 0)

    lax.fori_loop(1, n, send_waits, 0)
    rim_kv.wait_send()
    rim_q.wait_send()
    for k in range(len(spans)):
        scan_moves(k, True, lambda copy: copy.wait_send())


def swift(
    n, groups, cap, base, tok,
    counts, feats_hbm, pos, convw, rate, resid, skip, w_hbm, out, most,
    box_kv, box_q, arr_kv, arr_q, mark_out, mark_in, group_out, group_in,
    hot_s, place_s, prod, filt, gated, natural, state,
    feats, decay, rim_kv_out, rim_kv_in, rim_q_out, rim_q_in, own, acc, tx, rx, w_vmem,
    send_kv, recv_kv, send_q, recv_q, send_m, recv_m, send_g, recv_g,
    over_send_kv, over_recv_kv, over_send_q, over_recv_q, raw, ending, inward, hops, leaps,
    rim_sems, scan_send, scan_recv, self_sems, w_sem, f_sems,
):
    me = lax.axis_index("ctx")
    group = lax.axis_index("groups")
    slots, feat = feats_hbm.shape
    ch = feat // 3
    poles = rate.shape[0]
    steps = tok // ROWS
    tile = col_tile(ch)
    rows = n * cap
    over = cap - base
    half_n = n // 2
    barrier = pltpu.get_barrier_semaphore()
    bits = (n - 1).bit_length()

    def flip(a, m):
        return sum(((a // (1 << b) + m // (1 << b)) % 2) * (1 << b) for b in range(bits))

    def greet(m, c):
        pl.semaphore_signal(barrier, inc=1, device_id={"ctx": flip(me, m)}, device_id_type=MESH)
        return c

    lax.fori_loop(1, n, greet, 0)
    for g in range(1, groups):
        pl.semaphore_signal(barrier, inc=1, device_id={"groups": lax.rem(group + g, groups)}, device_id_type=MESH)
    kv_cols = pl.ds(ch, 2 * ch)
    f_kv = pltpu.make_async_copy(feats_hbm.at[:, kv_cols], feats.at[:, kv_cols], f_sems.at[0])
    f_q = pltpu.make_async_copy(feats_hbm.at[:, pl.ds(0, ch)], feats.at[:, pl.ds(0, ch)], f_sems.at[1])
    f_kv.start()
    f_q.start()
    w_copy = pltpu.make_async_copy(w_hbm, w_vmem, w_sem)
    w_copy.start()

    p = pos[...].reshape(1, slots)
    shift = tok.bit_length() - 1
    live = lax.broadcasted_iota(jnp.int32, (1, slots), 1) < counts[0]
    owner = jnp.where(live, lax.shift_right_logical(p, shift), -1)
    local = lax.bitwise_and(p, tok - 1).astype(f32)
    mine = owner == lax.broadcasted_iota(jnp.int32, (n, slots), 0)
    tri = lax.broadcasted_iota(jnp.int32, (slots, slots), 0) <= lax.broadcasted_iota(
        jnp.int32, (slots, slots), 1
    )
    tri = tri.astype(f32).astype(bf16)
    cum = jnp.dot(mine.astype(f32).astype(bf16), tri, preferred_element_type=f32)
    rank = jnp.sum(jnp.where(mine, cum, 0.0), axis=0, keepdims=True) - 1.0
    direct = jnp.logical_and(live, rank < float(base))
    beyond = jnp.logical_and(live, rank >= float(base)).astype(f32)
    bump = jnp.dot(jnp.broadcast_to(beyond, (16, slots)).astype(bf16), tri, preferred_element_type=f32)[0:1]
    late = jnp.where(beyond > 0.0, bump - 1.0, -1.0)
    apart = lax.bitwise_xor(owner, me)
    flat = jnp.where(direct, apart.astype(f32) * float(cap) + rank, -1.0)
    spare = jnp.where(late >= 0.0, late + float(base), -1.0)
    hot_row = lax.broadcasted_iota(jnp.int32, (rows, slots), 0)
    hit = jnp.logical_or(hot_row.astype(f32) == flat, lax.bitwise_and(hot_row, cap - 1).astype(f32) == spare)
    hot_s[...] = hit.astype(f32).astype(bf16)

    def pack_rows(box, first, c0):
        def pack(c, _):
            at = pl.ds(pl.multiple_of(first, rows // 2), rows // 2)
            src = pl.ds(pl.multiple_of(c0 + c * tile, LANES), tile)
            dst = pl.ds(pl.multiple_of(c * tile, LANES), tile)
            box[at, dst] = jnp.dot(hot_s[at, :], feats[:, src], preferred_element_type=f32).astype(bf16)
            return _

        return pack

    def slab(ref, k, size):
        return ref.at[pl.ds(pl.multiple_of(k * cap, cap), size), :]

    def over_rows(ref, k):
        return ref.at[pl.ds(pl.multiple_of(k * cap + base, ROWS), over), :]

    def direct_copy(which, m, size, came):
        box, arr, send, recv = which
        to = flip(me, m)
        return pltpu.make_async_remote_copy(
            src_ref=slab(box, m, size), dst_ref=slab(arr, to if came else me, size), send_sem=send.at[m],
            recv_sem=recv.at[m], device_id={"ctx": to}, device_id_type=MESH,
        )

    def to_mirror(which, came):
        box, arr, send, recv = which
        to = flip(me, half_n)
        return pltpu.make_async_remote_copy(
            src_ref=over_rows(box, half_n), dst_ref=over_rows(arr, to if came else me), send_sem=send.at[0],
            recv_sem=recv.at[0], device_id={"ctx": to}, device_id_type=MESH,
        )

    def forward(which, m, came):
        box, arr, send, recv = which
        to = flip(me, m)
        rows_of = over_rows(arr, flip(to if came else me, half_n))
        return pltpu.make_async_remote_copy(
            src_ref=rows_of, dst_ref=rows_of, send_sem=send.at[m], recv_sem=recv.at[m],
            device_id={"ctx": to}, device_id_type=MESH,
        )

    kv_direct = (box_kv, arr_kv, send_kv, recv_kv)
    q_direct = (box_q, arr_q, send_q, recv_q)
    kv_over = (box_kv, arr_kv, over_send_kv, over_recv_kv)
    q_over = (box_q, arr_q, over_send_q, over_recv_q)

    def each(first, last, make, act):
        def one(m, c):
            act(make(m))
            return c

        lax.fori_loop(first, last, one, 0)

    def start(copy):
        copy.start()

    def arrive(copy):
        copy.wait_recv()

    def sent(copy):
        copy.wait_send()

    def near(which, came=False):
        return lambda m: direct_copy(which, m, cap, came)

    def far(which, came=False):
        return lambda m: direct_copy(which, m, base, came)

    def spread_over(which, came=False):
        return lambda m: forward(which, m, came)

    def marks_to(m, to, came):
        return pltpu.make_async_remote_copy(
            src_ref=mark_out.at[to], dst_ref=mark_in.at[came], send_sem=send_m.at[m], recv_sem=recv_m.at[m],
            device_id={"ctx": to}, device_id_type=MESH,
        )

    def start_marks(m, c):
        marks_to(m, flip(me, m), me).start()
        return c

    def recv_marks(m, c):
        marks_to(m, flip(me, m), flip(me, m)).wait_recv()
        return c

    f_kv.wait()
    lax.fori_loop(0, 2 * ch // tile, pack_rows(box_kv, rows // 2, ch), 0)
    pl.semaphore_wait(barrier, n - 1 + groups - 1)
    to_mirror(kv_over, False).start()
    each(half_n, n, far(kv_direct), start)
    lax.fori_loop(0, 2 * ch // tile, pack_rows(box_kv, 0, ch), 0)
    each(1, half_n, near(kv_direct), start)
    own_kv = pltpu.make_async_copy(slab(box_kv, 0, cap), slab(arr_kv, me, cap), self_sems.at[0])
    own_kv.start()

    seats = (lax.broadcasted_iota(jnp.int32, (LANES, slots), 0) - lax.rem(me * cap, LANES)).astype(f32)
    in_slab = jnp.logical_and(seats >= 0.0, seats < float(cap))
    at_base = jnp.logical_and(direct, seats == rank)
    at_over = jnp.logical_and(in_slab, jnp.logical_and(late >= 0.0, seats - float(base) == late))
    last_dims = (((1,), (1,)), ((), ()))
    sub16 = lax.broadcasted_iota(jnp.int32, (16, slots), 0)
    two = jnp.where(sub16 == 0, local + 1.0, jnp.where(sub16 == 1, owner.astype(f32), 0.0)).astype(bf16)
    tell = lax.dot_general(
        jnp.where(mine, local + 1.0, 0.0).astype(bf16), at_base.astype(f32).astype(bf16), last_dims,
        preferred_element_type=f32,
    )
    tell = jnp.where(tell > 0.0, tell + (lax.broadcasted_iota(jnp.int32, (n, LANES), 0) * tok).astype(f32), 0.0)
    extra = lax.dot_general(two, at_over.astype(f32).astype(bf16), last_dims, preferred_element_type=f32)
    tell = tell + (extra[0:1] + extra[1:2] * float(tok))
    held = jnp.broadcast_to(jnp.sum(beyond, axis=1, keepdims=True), (1, LANES))
    for k in range(n):
        mark_out[k, 0:1, :] = tell[k : k + 1, :]
        mark_out[k, 1:2, :] = held
    mark_in[me] = mark_out[me]
    lax.fori_loop(1, n, start_marks, 0)

    to_mirror(kv_over, True).wait_recv()
    each(1, half_n, spread_over(kv_over), start)

    f_q.wait()
    lax.fori_loop(0, ch // tile, pack_rows(box_q, rows // 2, 0), 0)
    to_mirror(q_over, False).start()
    lax.fori_loop(0, ch // tile, pack_rows(box_q, 0, 0), 0)
    own_q = pltpu.make_async_copy(slab(box_q, 0, cap), slab(arr_q, me, cap), self_sems.at[1])
    own_q.start()
    decay[...] = jnp.exp(-rate[...])
    spans = scan_spans(n)
    sub = lax.broadcasted_iota(jnp.int32, (ROWS, 1), 0)
    first = jnp.logical_and(sub == 0, me > 0)
    later = ((ROWS - 1 - sub) * steps).astype(f32)
    segment = (sub * steps).astype(f32)
    leap_of = {}
    for k, span in enumerate(spans):
        for j in range(1, 4):
            if j * span < n:
                for lag in (j * span - 1,) + ((j * span,) if k < len(spans) - 1 else ()):
                    leap_of.setdefault(lag, len(leap_of))
    for lag, at in leap_of.items():
        leaps[at] = jnp.exp(-rate[...] * float(tok * lag))
    for at, by in enumerate((1, 2, 4)):
        hops[at] = jnp.exp(-rate[...] * float(steps * by))

    def fades_of(k, _):
        r = rate[pl.ds(k, 1), :]
        ending[k] = jnp.exp(-r * later)
        inward[k] = resid[pl.ds(k, 1), :] * jnp.exp(-r * segment)
        return _

    lax.fori_loop(0, poles, fades_of, 0)

    lax.fori_loop(1, n, recv_marks, 0)
    lanes_of = [
        sum(mark_in[k, 0:1, :] for k in range(g * (LANES // cap), (g + 1) * (LANES // cap)))
        for g in range(rows // LANES)
    ]
    came_pos = jnp.concatenate(lanes_of, axis=1) - 1.0
    worst = mark_in[0, 1:2, :]
    for k in range(1, n):
        worst = jnp.maximum(worst, mark_in[k, 1:2, :])
    group_out[...] = jnp.broadcast_to(worst, (ROWS, LANES))

    def group_copy(g, to):
        return pltpu.make_async_remote_copy(
            src_ref=group_out, dst_ref=group_in.at[g], send_sem=send_g.at[g], recv_sem=recv_g.at[g],
            device_id={"groups": to}, device_id_type=MESH,
        )

    for g in range(1, groups):
        group_copy(g, lax.rem(group + g, groups)).start()

    ext = tok + 2 * ROWS
    row = lax.broadcasted_iota(jnp.int32, (ext, 1), 0)
    want = lax.bitwise_and(row, ROWS - 1) * steps + lax.shift_right_logical(row, 3) - 2
    want = jnp.where(want < 0, -100, want + me * tok).astype(f32)
    place_s[...] = (want == came_pos).astype(f32).astype(bf16)
    rim_row = lax.broadcasted_iota(jnp.int32, (16, 1), 0)
    rim_want = jnp.where(rim_row < 2, rim_row + me * tok + tok - 2, -100).astype(f32)
    rim_hot = (rim_want == came_pos).astype(f32).astype(bf16)

    to_mirror(q_over, True).wait_recv()
    each(1, half_n, spread_over(q_over), start)
    own_kv.wait()
    each(1, half_n, near(kv_direct, True), arrive)
    each(1, half_n, near(q_direct), start)
    each(1, half_n, spread_over(kv_over, True), arrive)
    cuts = [half_n]
    for share in FLOW:
        cuts.append(min(n, cuts[-1] + share * half_n // 8))
    each(half_n, cuts[0] + n - cuts[1], far(kv_direct, True), arrive)
    ahead = cuts[1] - half_n

    def kv_then_q(m, c):
        far(kv_direct, True)(m).wait_recv()
        far(q_direct)(m - n + cuts[1]).start()
        return c

    lax.fori_loop(n - ahead, n, kv_then_q, 0)

    def rim_copy(src, dst, k, to):
        return pltpu.make_async_remote_copy(
            src_ref=src, dst_ref=dst, send_sem=rim_sems.at[2 * k], recv_sem=rim_sems.at[2 * k + 1],
            device_id={"ctx": to}, device_id_type=MESH,
        )

    after, before = lax.rem(me + 1, n), lax.rem(me + n - 1, n)

    def rim_tile(arr, rim):
        def fill(c, _):
            cols = pl.ds(pl.multiple_of(c * tile, LANES), tile)
            rim[:, cols] = jnp.dot(rim_hot, arr[:, cols], preferred_element_type=f32).astype(bf16)
            return _

        return fill

    lax.fori_loop(0, 2 * ch // tile, rim_tile(arr_kv, rim_kv_out), 0)
    rim_kv = rim_copy(rim_kv_out, rim_kv_in, 0, after)
    rim_kv.start()

    def featured(arr, at, w_at):
        x = jnp.dot(place_s[...], arr[:, pl.ds(pl.multiple_of(at, LANES), tile)], preferred_element_type=f32)
        w = convw[:, pl.ds(pl.multiple_of(w_at, LANES), tile)]
        return w[0:1] * x[2 * ROWS :] + w[1:2] * x[ROWS : ROWS + tok] + w[2:3] * x[:tok]

    def product_tile(c, _):
        at = c * tile
        k = featured(arr_kv, at, ch + at)
        v = featured(arr_kv, ch + at, 2 * ch + at)
        raw[:, pl.ds(pl.multiple_of(at, LANES), tile)] = k[: 2 * ROWS]
        raw[:, pl.ds(pl.multiple_of(ch + at, LANES), tile)] = v[: 2 * ROWS]
        prod[:, pl.ds(pl.multiple_of(at, LANES), tile)] = k * v
        return _

    lax.fori_loop(0, ch // tile, product_tile, 0)
    each(cuts[1], cuts[2], far(q_direct), start)
    rim_copy(rim_kv_out, rim_kv_in, 0, before).wait_recv()

    def edge_tile(c, _):
        def with_edge(at):
            cols = pl.ds(pl.multiple_of(at, LANES), tile)
            w = convw[:, pl.ds(pl.multiple_of(ch + at, LANES), tile)]
            edge = rim_kv_in[:, cols].astype(f32)
            top = jnp.where(first, w[1:2] * edge[1:2] + w[2:3] * edge[0:1], 0.0)
            nxt = jnp.where(first, w[2:3] * edge[1:2], 0.0)
            return jnp.concatenate([raw[0:ROWS, cols] + top, raw[ROWS:, cols] + nxt], axis=0)

        at = c * tile
        prod[0 : 2 * ROWS, pl.ds(pl.multiple_of(at, LANES), tile)] = with_edge(at) * with_edge(ch + at)
        return _

    lax.fori_loop(0, ch // tile, edge_tile, 0)

    def spread(ref, k, cols):
        return jnp.broadcast_to(ref[k : k + 1, cols], (ROWS, LANES))

    def total(terms):
        while len(terms) > 1:
            terms = [a + b for a, b in zip(terms[::2], terms[1::2])] + terms[len(terms) // 2 * 2 :]
        return terms[0]

    def local_tile(c, _):
        cols = pl.ds(pl.multiple_of(c * LANES, LANES), LANES)
        dec = [spread(decay, k, cols) for k in range(poles)]
        res = [spread(resid, k, cols) for k in range(poles)]
        gain = jnp.broadcast_to(skip[pl.ds(pl.multiple_of(c * LANES, LANES), LANES)].reshape(1, LANES), (ROWS, LANES))

        def step(i, st):
            at = pl.ds(pl.multiple_of(i * ROWS, ROWS), ROWS)
            x = prod[at, cols]
            st = tuple(d * s + x for d, s in zip(dec, st))
            filt[at, cols] = gain * x + total([r * s for r, s in zip(res, st)])
            return st

        zero = jnp.zeros((ROWS, LANES), f32)
        st = lax.fori_loop(0, steps, step, (zero,) * poles, unroll=4)
        for k in range(poles):
            state[k, :, cols] = st[k]
            own[k : k + 1, cols] = jnp.sum(ending[k, :, cols] * st[k], axis=0, keepdims=True)
        return _

    def prefix_tile(c, _):
        cols = pl.ds(pl.multiple_of(c * LANES, LANES), LANES)
        for k in range(poles):
            x = jnp.where(sub == 0, 0.0, pltpu.roll(state[k, :, cols], 1, 0))
            for at, by in enumerate((1, 2, 4)):
                x = x + jnp.where(sub >= by, hops[at, k : k + 1, cols] * pltpu.roll(x, by, 0), 0.0)
            state[k, :, cols] = resid[k : k + 1, cols] * x
        return _

    middle = (ch // LANES + 1) // 2
    parts = [(0, middle), (middle, ch // LANES)]

    def scan_copy(part, k, j, to):
        cols = pl.ds(part[0] * LANES, (part[1] - part[0]) * LANES)
        at = (3 * k + j - 1) * len(parts) + parts.index(part)
        return pltpu.make_async_remote_copy(
            src_ref=tx.at[k, :, cols], dst_ref=rx.at[3 * k + j - 1, :, cols], send_sem=scan_send.at[at],
            recv_sem=scan_recv.at[at], device_id={"ctx": to}, device_id_type=MESH,
        )

    def scan_moves(part, k, send, act):
        span = spans[k]
        for j in range(1, 4):
            if j * span < n:
                to = me + j * span if send else me - j * span
                act(scan_copy(part, k, j, lax.rem(to + n, n)))

    def scan_start(part, k):
        cols = pl.ds(part[0] * LANES, (part[1] - part[0]) * LANES)
        tx[k, :, cols] = own[:, cols].astype(bf16)
        scan_moves(part, k, True, start)

    def scan_take(part, k):
        span = spans[k]
        cols = pl.ds(part[0] * LANES, (part[1] - part[0]) * LANES)
        scan_moves(part, k, False, arrive)
        for j in range(1, 4):
            if j * span < n:
                got = jnp.where(me >= j * span, rx[3 * k + j - 1, :, cols].astype(f32), 0.0)
                acc[0, :, cols] = acc[0, :, cols] + leaps[leap_of[j * span - 1], :, cols] * got
                if k < len(spans) - 1:
                    own[:, cols] = own[:, cols] + leaps[leap_of[j * span], :, cols] * got

    acc[0] = jnp.zeros((poles, ch), f32)
    for part in parts:
        lax.fori_loop(part[0], part[1], local_tile, 0)
        scan_start(part, 0)
    each(cuts[2], cuts[3], far(q_direct), start)
    lax.fori_loop(0, ch // LANES, prefix_tile, 0)
    for k in range(len(spans) - 1):
        for part in parts:
            scan_take(part, k)
            scan_start(part, k + 1)
    each(cuts[3], n, far(q_direct), start)

    def carry_tile(c, _):
        cols = pl.ds(pl.multiple_of(c * LANES, LANES), LANES)
        dec = [spread(decay, k, cols) for k in range(poles)]
        begin = tuple(
            state[k, :, cols] + inward[k, :, cols] * acc[0, k : k + 1, cols] for k in range(poles)
        )

        def step(i, g):
            at = pl.ds(pl.multiple_of(i * ROWS, ROWS), ROWS)
            g = tuple(d * s for d, s in zip(dec, g))
            filt[at, cols] = filt[at, cols] + total(list(g))
            return g

        lax.fori_loop(0, steps, step, begin, unroll=4)
        return _

    for part in parts:
        scan_take(part, len(spans) - 1)
        lax.fori_loop(part[0], part[1], carry_tile, 0)
    top_of = worst
    for g in range(1, groups):
        group_copy(g, lax.rem(group + groups - g, groups)).wait_recv()
        top_of = jnp.maximum(top_of, group_in[g, 0:1, :])
    most[0] = jnp.max(top_of).astype(jnp.int32)
    w_copy.wait()

    own_q.wait()
    each(1, half_n, near(q_direct, True), arrive)
    each(1, half_n, spread_over(q_over, True), arrive)
    each(half_n, n, far(q_direct, True), arrive)
    lax.fori_loop(0, ch // tile, rim_tile(arr_q, rim_q_out), 0)
    rim_q = rim_copy(rim_q_out, rim_q_in, 1, after)
    rim_q.start()

    def gate_tile(c, _):
        at = c * tile
        cols = pl.ds(pl.multiple_of(at, LANES), tile)
        y = featured(arr_q, at, at)
        raw[:, cols] = y[: 2 * ROWS]
        gated[:, cols] = (y * filt[:, cols]).astype(bf16)
        return _

    lax.fori_loop(0, ch // tile, gate_tile, 0)
    rim_copy(rim_q_out, rim_q_in, 1, before).wait_recv()
    edge = rim_q_in[...].astype(f32)
    w1, w2 = convw[1:2, 0:ch], convw[2:3, 0:ch]
    top = jnp.where(first, w1 * edge[1:2] + w2 * edge[0:1], 0.0)
    nxt = jnp.where(first, w2 * edge[1:2], 0.0)
    begun = raw[:, 0:ch] + jnp.concatenate([top, nxt], axis=0)
    gated[0 : 2 * ROWS, :] = (begun * filt[0 : 2 * ROWS, :]).astype(bf16)

    nat = lax.broadcasted_iota(jnp.int32, (tok, 1), 0)
    seat = lax.bitwise_and(nat, steps - 1) * ROWS + lax.shift_right_logical(nat, steps.bit_length() - 1)
    order = (seat == lax.broadcasted_iota(jnp.int32, (tok, tok), 1)).astype(f32).astype(bf16)

    def order_tile(c, _):
        cols = pl.ds(pl.multiple_of(c * tile, LANES), tile)
        natural[:, cols] = jnp.dot(order, gated[:, cols], preferred_element_type=f32).astype(bf16)
        return _

    lax.fori_loop(0, ch // tile, order_tile, 0)

    def out_tile(c, _):
        cols = pl.ds(pl.multiple_of(c * tile, LANES), tile)
        out[:, cols] = jnp.dot(natural[...], w_vmem[:, cols], preferred_element_type=f32).astype(bf16)
        return _

    lax.fori_loop(0, ch // tile, out_tile, 0)

    for which in (kv_direct, q_direct):
        each(1, half_n, near(which), sent)
        each(half_n, n, far(which), sent)
    for which in (kv_over, q_over):
        to_mirror(which, False).wait_send()
        each(1, half_n, spread_over(which), sent)
    each(1, n, lambda m: marks_to(m, flip(me, m), me), sent)
    for g in range(1, groups):
        group_copy(g, lax.rem(group + g, groups)).wait_send()
    rim_kv.wait_send()
    rim_q.wait_send()
    for k in range(len(spans)):
        for part in parts:
            scan_moves(part, k, True, sent)


def swift_call(n, groups, cap, base, tok, args):
    counts, features, positions, conv_weight, pole_rate, pole_residue, skip_gain, out_weight = args
    slots, feat = features.shape
    ch = feat // 3
    poles = pole_rate.shape[0]
    rows = n * cap
    stages = len(scan_spans(n))
    whole = pl.BlockSpec(memory_space=pltpu.VMEM)
    dma = pltpu.SemaphoreType.DMA
    vmem = pltpu.VMEM
    return pl.pallas_call(
        functools.partial(swift, n, groups, cap, base, tok),
        out_shape=(jax.ShapeDtypeStruct((tok, ch), bf16), jax.ShapeDtypeStruct((1,), jnp.int32)),
        in_specs=[pl.BlockSpec(memory_space=pltpu.SMEM), pl.BlockSpec(memory_space=pl.ANY)]
        + [whole] * 5 + [pl.BlockSpec(memory_space=pl.ANY)],
        out_specs=(whole, pl.BlockSpec(memory_space=pltpu.SMEM)),
        scratch_shapes=[
            vmem((rows, 2 * ch), bf16),
            vmem((rows, ch), bf16),
            vmem((rows, 2 * ch), bf16),
            vmem((rows, ch), bf16),
            vmem((n, 2, LANES), f32),
            vmem((n, 2, LANES), f32),
            vmem((ROWS, LANES), f32),
            vmem((groups, ROWS, LANES), f32),
            vmem((rows, slots), bf16),
            vmem((tok + 2 * ROWS, rows), bf16),
            vmem((tok, ch), f32),
            vmem((tok, ch), f32),
            vmem((tok, ch), bf16),
            vmem((tok, ch), bf16),
            vmem((poles, ROWS, ch), f32),
            vmem((slots, feat), bf16),
            vmem((poles, ch), f32),
            vmem((16, 2 * ch), bf16),
            vmem((16, 2 * ch), bf16),
            vmem((16, ch), bf16),
            vmem((16, ch), bf16),
            vmem((poles, ch), f32),
            vmem((1, poles, ch), f32),
            vmem((stages, poles, ch), bf16),
            vmem((3 * stages, poles, ch), bf16),
            vmem(out_weight.shape, bf16),
        ]
        + [dma((n,))] * 6
        + [dma((groups,))] * 2
        + [dma((n,))] * 4
        + [
            vmem((2 * ROWS, 2 * ch), f32),
            vmem((poles, ROWS, ch), f32),
            vmem((poles, ROWS, ch), f32),
            vmem((3, poles, ch), f32),
            vmem((6 * stages, poles, ch), f32),
        ]
        + [dma((4,)), dma((6 * stages,)), dma((6 * stages,)), dma((2,)), dma, dma((2,))],
        compiler_params=pltpu.CompilerParams(
            collective_id=1, has_side_effects=True, vmem_limit_bytes=60 << 20
        ),
        name="hyena_direct",
    )(*args)


def mega_call(n, cap, tok, args):
    counts, features, positions, conv_weight, pole_rate, pole_residue, skip_gain, out_weight = args
    slots, feat = features.shape
    ch = feat // 3
    poles = pole_rate.shape[0]
    rows = n * cap
    stages = len(scan_spans(n))
    whole = pl.BlockSpec(memory_space=pltpu.VMEM)
    dma = pltpu.SemaphoreType.DMA
    return pl.pallas_call(
        functools.partial(mega, n, cap, tok, PACE[0] * (n - 1) // 15),
        out_shape=jax.ShapeDtypeStruct((tok, ch), bf16),
        in_specs=[pl.BlockSpec(memory_space=pltpu.SMEM), pl.BlockSpec(memory_space=pl.ANY)]
        + [whole] * 5 + [pl.BlockSpec(memory_space=pl.ANY)],
        out_specs=whole,
        scratch_shapes=[
            pltpu.VMEM((rows, 2 * ch + LANES), bf16),
            pltpu.VMEM((rows, ch), bf16),
            pltpu.VMEM((rows, 2 * ch + LANES), bf16),
            pltpu.VMEM((rows, ch), bf16),
            pltpu.VMEM((rows, slots), bf16),
            pltpu.VMEM((tok + 2 * ROWS, rows), bf16),
            pltpu.VMEM((tok, ch), f32),
            pltpu.VMEM((tok, ch), f32),
            pltpu.VMEM((16, LANES), bf16),
            pltpu.VMEM((tok, ch), bf16),
            pltpu.VMEM((poles, ROWS, ch), f32),
            pltpu.VMEM((slots, feat), bf16),
            pltpu.VMEM((poles, ch), f32),
            pltpu.VMEM((16, 2 * ch), bf16),
            pltpu.VMEM((16, 2 * ch), bf16),
            pltpu.VMEM((16, ch), bf16),
            pltpu.VMEM((16, ch), bf16),
            pltpu.VMEM((poles, ch), f32),
            pltpu.VMEM((1, poles, ch), f32),
            pltpu.VMEM((stages, poles, ch), bf16),
            pltpu.VMEM((3 * stages, poles, ch), bf16),
            pltpu.VMEM(out_weight.shape, bf16),
            dma((n,)), dma((n,)), dma((n,)), dma((n,)), dma((4,)), dma((3 * stages,)), dma((3 * stages,)),
            dma((2,)), dma, dma((2,)),
        ],
        compiler_params=pltpu.CompilerParams(
            collective_id=0, has_side_effects=True, vmem_limit_bytes=60 << 20
        ),
        name="hyena",
    )(*args)


def on_device(
    features, positions, counts, conv_weight, pole_rate, pole_residue, skip_gain, out_weight
):
    n = lax.axis_size("ctx")
    groups = lax.axis_size("groups")
    slots, feat = features.shape
    ch = feat // 3
    tok = 2 * slots // 3
    cap = 2 * tok // n
    if cap % 16 or tok & (tok - 1) or tok > 256 or conv_weight.shape[0] != 3 or ch % LANES or n & (n - 1) or n < 4:
        return plain_on_device(
            features, positions, counts, conv_weight, pole_rate, pole_residue, skip_gain, out_weight
        )
    args = (counts, features, positions, conv_weight, pole_rate, pole_residue, skip_gain, out_weight)
    base = slots // n
    if base % ROWS or cap - base > 16 or LANES % cap:
        return mega_call(n, cap, tok, args)
    done, most = swift_call(n, groups, cap, base, tok, args)
    return lax.cond(most[0] > cap - base, lambda d: mega_call(n, cap, tok, args), lambda d: d, done)


PACE = (2, 1, 1, 2, 2)
FLOW = (4, 2, 1)


def solution(mesh):
    return jax.shard_map(
        on_device,
        mesh=mesh,
        in_specs=(
            P(("groups", "ctx"), None),
            P(("groups", "ctx")),
            P(("groups", "ctx")),
            P(),
            P(),
            P(),
            P(),
            P(),
        ),
        out_specs=P(("groups", "ctx"), None),
        check_vma=False,
    )
```

```python
import functools

import jax
import jax.numpy as jnp
from jax import lax
from jax.experimental import pallas as pl
from jax.experimental.pallas import tpu as pltpu
from jax.sharding import PartitionSpec as P

LANES = 128
ROWS = 8
MESH = pl.DeviceIdType.MESH
f32, bf16 = jnp.float32, jnp.bfloat16

block_len = 32


def from_behind(array, axis, by):
    count = lax.axis_size(axis)
    pairs = [(i, i + by) for i in range(count) if 0 <= i + by < count]
    return lax.ppermute(array, axis, pairs)


def plain_on_device(
    features, positions, counts, conv_weight, pole_rate, pole_residue, skip_gain, out_weight
):
    devices = lax.axis_size("ctx")
    slot_count = features.shape[0]
    feat_width = features.shape[1]
    channels = feat_width // 3
    tok_rows = 2 * slot_count // 3
    pair_cap = 2 * tok_rows // devices
    taps = conv_weight.shape[0]
    poles = pole_rate.shape[0]
    slot_ids = jnp.arange(slot_count, dtype=jnp.int32)
    is_live = slot_ids < counts[0]
    owners = jnp.where(is_live, positions // tok_rows, devices)
    same = jnp.logical_and(owners[:, None] == owners[None, :], slot_ids[None, :] < slot_ids[:, None])
    within = jnp.sum(same.astype(jnp.int32), axis=1)
    flat_index = jnp.where(is_live, owners * pair_cap + within, devices * pair_cap)
    outbox = (
        jnp.zeros((devices * pair_cap + 1, feat_width), features.dtype)
        .at[flat_index]
        .set(features)[:-1]
    )
    local_pos = (
        jnp.full((devices * pair_cap + 1,), -1, jnp.int32)
        .at[flat_index]
        .set(positions % tok_rows)[:-1]
    )
    outbox = outbox.reshape(devices, pair_cap, feat_width)
    local_pos = local_pos.reshape(devices, pair_cap)
    arrived, arrived_pos = (
        lax.all_to_all(outbox, "ctx", split_axis=0, concat_axis=0, tiled=True),
        lax.all_to_all(local_pos, "ctx", split_axis=0, concat_axis=0, tiled=True),
    )
    target = jnp.where(arrived_pos >= 0, arrived_pos, tok_rows).reshape(-1)
    placed = (
        jnp.zeros((tok_rows + 1, feat_width), features.dtype)
        .at[target]
        .set(arrived.reshape(-1, feat_width))[:-1]
    )
    rim_rows = from_behind(placed[tok_rows - (taps - 1) :], "ctx", 1)
    extended = jnp.concatenate([rim_rows, placed], axis=0)
    featured = jnp.zeros((tok_rows, feat_width), jnp.float32)
    for tap in range(taps):
        start = taps - 1 - tap
        featured = featured + conv_weight[tap][None, :] * extended[start : start + tok_rows].astype(
            jnp.float32
        )
    query_feat = featured[:, :channels]
    product = featured[:, channels : 2 * channels] * featured[:, 2 * channels :]
    num_blocks = tok_rows // block_len
    lag_steps = jnp.arange(block_len + 1).astype(jnp.float32)
    powers = jnp.exp(-pole_rate[None] * lag_steps[:, None, None])
    filter_taps = jnp.sum(powers[:block_len] * pole_residue[None], axis=1)
    blocked = product.reshape(num_blocks, block_len, channels)
    padded_blk = jnp.pad(blocked, ((0, 0), (block_len - 1, 0), (0, 0)))
    inside = jnp.zeros((num_blocks, block_len, channels), jnp.float32)
    for lag in range(block_len):
        first = block_len - 1 - lag
        inside = inside + filter_taps[lag][None, None, :] * padded_blk[:, first : first + block_len]
    blk_sums = jnp.zeros((num_blocks, poles, channels), jnp.float32)
    for row in range(block_len):
        blk_sums = blk_sums + powers[block_len - 1 - row][None] * blocked[:, row][:, None, :]
    decay_blk = powers[block_len]

    def advance(running, block_sum):
        return (decay_blk * running + block_sum, running)

    local_end, starts = lax.scan(advance, jnp.zeros((poles, channels), jnp.float32), blk_sums)
    decay_dev = jnp.exp(-pole_rate * float(tok_rows))

    def relay_step(counter, incoming):
        return from_behind(decay_dev * incoming + local_end, "ctx", 1)

    carry_in = lax.fori_loop(0, devices - 1, relay_step, jnp.zeros_like(local_end))
    block_starts = (jnp.arange(num_blocks) * block_len).astype(jnp.float32)
    block_decay = jnp.exp(-pole_rate[None] * block_starts[:, None, None])
    incoming = starts + block_decay * carry_in[None]
    inward = pole_residue[None] * powers[1:]
    from_state = jnp.zeros((num_blocks, block_len, channels), jnp.float32)
    for pole in range(poles):
        from_state = from_state + inward[:, pole][None] * incoming[:, pole][:, None, :]
    convolved = (inside + from_state).reshape(tok_rows, channels)
    filtered = skip_gain[None, :] * product + convolved
    gated_rows = (query_feat * filtered).astype(jnp.bfloat16)
    return jnp.dot(gated_rows, out_weight, preferred_element_type=jnp.float32).astype(jnp.bfloat16)

def col_tile(width):
    for tile in (384, 256, 128):
        if width % tile == 0:
            return tile
    return width


def scan_spans(n):
    spans, span = [], 1
    while span < n:
        spans.append(span)
        span *= 4
    return spans


def mega(
    n, cap, tok, up_front,
    counts, feats_hbm, pos, convw, rate, resid, skip, w_hbm, out,
    box_kv, box_q, arr_kv, arr_q, hot_s, place_s, prod, filt, gated, natural, state,
    feats, decay, rim_kv_out, rim_kv_in, rim_q_out, rim_q_in, own, acc, tx, rx, w_vmem,
    send_kv, recv_kv, send_q, recv_q, rim_sems, scan_send, scan_recv, self_sems, w_sem, f_sems,
):
    me = lax.axis_index("ctx")
    slots, feat = feats_hbm.shape
    ch = feat // 3
    poles = rate.shape[0]
    steps = tok // ROWS
    tile = col_tile(ch)
    rows = n * cap
    barrier = pltpu.get_barrier_semaphore()

    bits = (n - 1).bit_length()

    def mask_of(d):
        return sum(((d // (1 << b)) % 2) * (1 << (bits - 1 - b)) for b in range(bits))

    def peer_of(d):
        m = mask_of(d)
        return sum(((me // (1 << b) + m // (1 << b)) % 2) * (1 << b) for b in range(bits))

    def greet(d, c):
        pl.semaphore_signal(barrier, inc=1, device_id={"ctx": peer_of(d)}, device_id_type=MESH)
        return c

    lax.fori_loop(1, n, greet, 0)
    kv_cols = pl.ds(ch, 2 * ch)
    f_kv = pltpu.make_async_copy(feats_hbm.at[:, kv_cols], feats.at[:, kv_cols], f_sems.at[0])
    f_q = pltpu.make_async_copy(feats_hbm.at[:, pl.ds(0, ch)], feats.at[:, pl.ds(0, ch)], f_sems.at[1])
    f_kv.start()
    f_q.start()
    w_copy = pltpu.make_async_copy(w_hbm, w_vmem, w_sem)
    w_copy.start()

    p = pos[...].reshape(1, slots)
    shift = tok.bit_length() - 1
    live = lax.broadcasted_iota(jnp.int32, (1, slots), 1) < counts[0]
    owner = jnp.where(live, lax.shift_right_logical(p, shift), -1)
    local = lax.bitwise_and(p, tok - 1).astype(f32)
    mine = owner == lax.broadcasted_iota(jnp.int32, (n, slots), 0)
    tri = lax.broadcasted_iota(jnp.int32, (slots, slots), 0) <= lax.broadcasted_iota(
        jnp.int32, (slots, slots), 1
    )
    cum = jnp.dot(mine.astype(f32).astype(bf16), tri.astype(f32).astype(bf16), preferred_element_type=f32)
    rank = jnp.sum(jnp.where(mine, cum, 0.0), axis=0, keepdims=True) - 1.0
    flat = owner.astype(f32) * float(cap) + rank
    hit = lax.broadcasted_iota(jnp.int32, (rows, slots), 0).astype(f32) == flat
    hot_s[...] = hit.astype(f32).astype(bf16)
    marks = jnp.sum(jnp.where(hit, local + 1.0, 0.0), axis=1, keepdims=True) - 1.0
    box_kv[:, 2 * ch :] = jnp.broadcast_to(marks, (rows, LANES)).astype(bf16)

    def pack_kv(c, _):
        src = pl.ds(pl.multiple_of(ch + c * tile, LANES), tile)
        dst = pl.ds(pl.multiple_of(c * tile, LANES), tile)
        box_kv[:, dst] = jnp.dot(hot_s[...], feats[:, src], preferred_element_type=f32).astype(bf16)
        return _

    def pack_q(c, _):
        dst = pl.ds(pl.multiple_of(c * tile, LANES), tile)
        box_q[:, dst] = jnp.dot(hot_s[...], feats[:, dst], preferred_element_type=f32).astype(bf16)
        return _

    f_kv.wait()
    lax.fori_loop(0, 2 * ch // tile, pack_kv, 0)

    def slab(ref, k):
        return ref.at[pl.ds(pl.multiple_of(k * cap, cap), cap), :]

    def outgoing(box, arr, send, recv, d):
        to = peer_of(d)
        return pltpu.make_async_remote_copy(
            src_ref=slab(box, to), dst_ref=slab(arr, me), send_sem=send.at[d], recv_sem=recv.at[d],
            device_id={"ctx": to}, device_id_type=MESH,
        )

    def incoming(box, arr, send, recv, d):
        came = peer_of(d)
        return pltpu.make_async_remote_copy(
            src_ref=slab(box, came), dst_ref=slab(arr, came), send_sem=send.at[d], recv_sem=recv.at[d],
            device_id={"ctx": came}, device_id_type=MESH,
        )

    def start_kv(d, c):
        outgoing(box_kv, arr_kv, send_kv, recv_kv, d).start()
        return c

    def start_q(d, c):
        outgoing(box_q, arr_q, send_q, recv_q, d).start()
        return c

    def recv_kv_wait(d, c):
        incoming(box_kv, arr_kv, send_kv, recv_kv, d).wait_recv()
        return c

    def recv_q_wait(d, c):
        incoming(box_q, arr_q, send_q, recv_q, d).wait_recv()
        return c

    def send_waits(d, c):
        outgoing(box_kv, arr_kv, send_kv, recv_kv, d).wait_send()
        outgoing(box_q, arr_q, send_q, recv_q, d).wait_send()
        return c

    pl.semaphore_wait(barrier, n - 1)
    lax.fori_loop(1, n, start_kv, 0)
    own_kv = pltpu.make_async_copy(slab(box_kv, me), slab(arr_kv, me), self_sems.at[0])
    own_kv.start()
    f_q.wait()
    lax.fori_loop(0, ch // tile, pack_q, 0)
    own_q = pltpu.make_async_copy(slab(box_q, me), slab(arr_q, me), self_sems.at[1])
    own_q.start()
    lax.fori_loop(1, 1 + up_front, start_q, 0)
    decay[...] = jnp.exp(-rate[...])

    own_kv.wait()
    lax.fori_loop(1, n, recv_kv_wait, 0)

    ext = tok + 2 * ROWS
    came_pos = jnp.transpose(arr_kv[:, 2 * ch :].astype(f32))[0:1, :]
    row = lax.broadcasted_iota(jnp.int32, (ext, 1), 0)
    want = lax.bitwise_and(row, ROWS - 1) * steps + lax.shift_right_logical(row, 3) - 2
    want = jnp.where(want < 0, -100, want).astype(f32)
    place_s[...] = (want == came_pos).astype(f32).astype(bf16)
    rim_row = lax.broadcasted_iota(jnp.int32, (16, 1), 0)
    rim_want = jnp.where(rim_row < 2, rim_row + tok - 2, -100).astype(f32)
    rim_hot = (rim_want == came_pos).astype(f32).astype(bf16)

    def rim_copy(src, dst, k, to):
        return pltpu.make_async_remote_copy(
            src_ref=src, dst_ref=dst, send_sem=rim_sems.at[2 * k], recv_sem=rim_sems.at[2 * k + 1],
            device_id={"ctx": to}, device_id_type=MESH,
        )

    after, before = lax.rem(me + 1, n), lax.rem(me + n - 1, n)

    def rim_kv_tile(c, _):
        cols = pl.ds(pl.multiple_of(c * tile, LANES), tile)
        rim_kv_out[:, cols] = jnp.dot(rim_hot, arr_kv[:, cols], preferred_element_type=f32).astype(bf16)
        return _

    def rim_q_tile(c, _):
        cols = pl.ds(pl.multiple_of(c * tile, LANES), tile)
        rim_q_out[:, cols] = jnp.dot(rim_hot, arr_q[:, cols], preferred_element_type=f32).astype(bf16)
        return _

    lax.fori_loop(0, 2 * ch // tile, rim_kv_tile, 0)
    rim_kv = rim_copy(rim_kv_out, rim_kv_in, 0, after)
    rim_kv.start()
    spans = scan_spans(n)
    cuts = [1]
    for share in PACE:
        cuts.append(min(n, cuts[-1] + share * (n - 1) // 15))
    lax.fori_loop(cuts[1], cuts[2], start_q, 0)
    rim_copy(rim_kv_out, rim_kv_in, 0, before).wait_recv()

    sub = lax.broadcasted_iota(jnp.int32, (ROWS, 1), 0)
    first = jnp.logical_and(sub == 0, me > 0)

    def featured(arr, at, w_at, rim, rim_at):
        x = jnp.dot(place_s[...], arr[:, pl.ds(pl.multiple_of(at, LANES), tile)], preferred_element_type=f32)
        w = convw[:, pl.ds(pl.multiple_of(w_at, LANES), tile)]
        y = w[0:1] * x[2 * ROWS :] + w[1:2] * x[ROWS : ROWS + tok] + w[2:3] * x[:tok]
        if rim is None:
            return y
        edge = rim[:, pl.ds(pl.multiple_of(rim_at, LANES), tile)].astype(f32)
        top = jnp.where(first, w[1:2] * edge[1:2] + w[2:3] * edge[0:1], 0.0)
        nxt = jnp.where(first, w[2:3] * edge[1:2], 0.0)
        return jnp.concatenate([y[:ROWS] + top, y[ROWS : 2 * ROWS] + nxt, y[2 * ROWS :]], axis=0)

    def product_tile(c, _):
        at = c * tile
        k = featured(arr_kv, at, ch + at, rim_kv_in, at)
        v = featured(arr_kv, ch + at, 2 * ch + at, rim_kv_in, ch + at)
        prod[:, pl.ds(pl.multiple_of(at, LANES), tile)] = k * v
        return _

    lax.fori_loop(0, ch // tile, product_tile, 0)
    lax.fori_loop(cuts[2], cuts[3], start_q, 0)

    def spread(ref, k, cols):
        return jnp.broadcast_to(ref[k : k + 1, cols], (ROWS, LANES))

    later = ((ROWS - 1 - sub) * steps).astype(f32)

    def total(terms):
        while len(terms) > 1:
            terms = [a + b for a, b in zip(terms[::2], terms[1::2])] + terms[len(terms) // 2 * 2 :]
        return terms[0]

    def local_tile(c, _):
        cols = pl.ds(pl.multiple_of(c * LANES, LANES), LANES)
        dec = [spread(decay, k, cols) for k in range(poles)]
        res = [spread(resid, k, cols) for k in range(poles)]
        gain = jnp.broadcast_to(skip[pl.ds(pl.multiple_of(c * LANES, LANES), LANES)].reshape(1, LANES), (ROWS, LANES))

        def step(i, st):
            at = pl.ds(pl.multiple_of(i * ROWS, ROWS), ROWS)
            x = prod[at, cols]
            st = tuple(d * s + x for d, s in zip(dec, st))
            filt[at, cols] = gain * x + total([r * s for r, s in zip(res, st)])
            return st

        zero = jnp.zeros((ROWS, LANES), f32)
        st = lax.fori_loop(0, steps, step, (zero,) * poles, unroll=2)
        for k in range(poles):
            state[k, :, cols] = st[k]
            fade = jnp.exp(-rate[k : k + 1, cols] * later)
            own[k : k + 1, cols] = jnp.sum(fade * st[k], axis=0, keepdims=True)
        return _

    half = ch // LANES // 2
    lax.fori_loop(0, half, local_tile, 0)
    lax.fori_loop(cuts[3], cuts[4], start_q, 0)
    lax.fori_loop(half, ch // LANES, local_tile, 0)

    def scan_copy(k, j, to):
        return pltpu.make_async_remote_copy(
            src_ref=tx.at[k], dst_ref=rx.at[3 * k + j - 1], send_sem=scan_send.at[3 * k + j - 1],
            recv_sem=scan_recv.at[3 * k + j - 1], device_id={"ctx": to}, device_id_type=MESH,
        )

    def scan_moves(k, send, act):
        span = spans[k]
        for j in range(1, 4):
            if j * span < n:
                to = me + j * span if send else me - j * span
                act(scan_copy(k, j, lax.rem(to + n, n)))

    acc[0] = jnp.zeros((poles, ch), f32)
    for k, span in enumerate(spans):
        tx[k] = own[...].astype(bf16)
        scan_moves(k, True, lambda copy: copy.start())
        stop = n if k == len(spans) - 1 or 5 + k >= len(cuts) else cuts[5 + k]
        lax.fori_loop(cuts[4 + k] if 4 + k < len(cuts) else n, stop, start_q, 0)
        scan_moves(k, False, lambda copy: copy.wait_recv())
        for j in range(1, 4):
            if j * span < n:
                got = jnp.where(me >= j * span, rx[3 * k + j - 1].astype(f32), 0.0)
                acc[0] = acc[0] + jnp.exp(-rate[...] * float(tok * (j * span - 1))) * got
                if k < len(spans) - 1:
                    own[...] = own[...] + jnp.exp(-rate[...] * float(tok * j * span)) * got

    def carry_tile(c, _):
        cols = pl.ds(pl.multiple_of(c * LANES, LANES), LANES)
        dec = [spread(decay, k, cols) for k in range(poles)]
        start = []
        for k in range(poles):
            r = rate[k : k + 1, cols]
            x = jnp.where(sub == 0, acc[0, k : k + 1, cols], pltpu.roll(state[k, :, cols], 1, 0))
            for by in (1, 2, 4):
                fade = jnp.exp(-r * float(steps * by))
                x = x + jnp.where(sub >= by, fade * pltpu.roll(x, by, 0), 0.0)
            start.append(resid[k : k + 1, cols] * x)

        def step(i, g):
            at = pl.ds(pl.multiple_of(i * ROWS, ROWS), ROWS)
            g = tuple(d * s for d, s in zip(dec, g))
            filt[at, cols] = filt[at, cols] + total(list(g))
            return g

        lax.fori_loop(0, steps, step, tuple(start), unroll=2)
        return _

    lax.fori_loop(0, ch // LANES, carry_tile, 0)

    own_q.wait()
    lax.fori_loop(1, n, recv_q_wait, 0)
    lax.fori_loop(0, ch // tile, rim_q_tile, 0)
    rim_q = rim_copy(rim_q_out, rim_q_in, 1, after)
    rim_q.start()

    def query_tile(c, _):
        at = c * tile
        prod[:, pl.ds(pl.multiple_of(at, LANES), tile)] = featured(arr_q, at, at, None, at)
        return _

    lax.fori_loop(0, ch // tile, query_tile, 0)
    rim_copy(rim_q_out, rim_q_in, 1, before).wait_recv()
    edge = rim_q_in[...].astype(f32)
    w1, w2 = convw[1:2, 0:ch], convw[2:3, 0:ch]
    prod[0:ROWS, :] = prod[0:ROWS, :] + jnp.where(first, w1 * edge[1:2] + w2 * edge[0:1], 0.0)
    prod[ROWS : 2 * ROWS, :] = prod[ROWS : 2 * ROWS, :] + jnp.where(first, w2 * edge[1:2], 0.0)

    nat = lax.broadcasted_iota(jnp.int32, (tok, 1), 0)
    seat = lax.bitwise_and(nat, steps - 1) * ROWS + lax.shift_right_logical(nat, steps.bit_length() - 1)
    order = (seat == lax.broadcasted_iota(jnp.int32, (tok, tok), 1)).astype(f32).astype(bf16)

    def gate_tile(c, _):
        cols = pl.ds(pl.multiple_of(c * tile, LANES), tile)
        rows_g = (prod[:, cols] * filt[:, cols]).astype(bf16)
        natural[:, cols] = jnp.dot(order, rows_g, preferred_element_type=f32).astype(bf16)
        return _

    lax.fori_loop(0, ch // tile, gate_tile, 0)
    w_copy.wait()

    def out_tile(c, _):
        cols = pl.ds(pl.multiple_of(c * tile, LANES), tile)
        out[:, cols] = jnp.dot(natural[...], w_vmem[:, cols], preferred_element_type=f32).astype(bf16)
        return _

    lax.fori_loop(0, ch // tile, out_tile, 0)

    lax.fori_loop(1, n, send_waits, 0)
    rim_kv.wait_send()
    rim_q.wait_send()
    for k in range(len(spans)):
        scan_moves(k, True, lambda copy: copy.wait_send())


def swift(
    n, groups, cap, base, tok,
    counts, feats_hbm, pos, convw, rate, resid, skip, w_hbm, out, most,
    box_a, box_b, box_q, arr_a, arr_b, arr_q, mark_out, mark_in, group_out, group_in,
    hot_s, place_s, prod, filt, gated, natural, state,
    feats, decay, rims_out, rims_in, own, acc, totals, rate4, tx, rx, w_vmem,
    sends, recvs, over_sends, over_recvs, send_m, recv_m, send_g, recv_g, raw, ending, inward, hops, leaps,
    rim_sems, scan_send, scan_recv, self_sems, w_sem, f_sems,
):
    me = lax.axis_index("ctx")
    group = lax.axis_index("groups")
    slots, feat = feats_hbm.shape
    ch = feat // 3
    poles = rate.shape[0]
    steps = tok // ROWS
    tile = col_tile(ch)
    rows = n * cap
    over = cap - base
    half_n = n // 2
    tiles = ch // tile
    lead = (tiles + 1) // 2
    parts = [(0, lead), (lead, tiles)]
    barrier = pltpu.get_barrier_semaphore()
    bits = (n - 1).bit_length()

    def flip(a, m):
        return sum(((a // (1 << b) + m // (1 << b)) % 2) * (1 << b) for b in range(bits))

    def greet(m, c):
        pl.semaphore_signal(barrier, inc=1, device_id={"ctx": flip(me, m)}, device_id_type=MESH)
        return c

    lax.fori_loop(1, n, greet, 0)
    for g in range(1, groups):
        pl.semaphore_signal(barrier, inc=1, device_id={"groups": lax.rem(group + g, groups)}, device_id_type=MESH)
    kv_cols = pl.ds(ch, 2 * ch)
    f_kv = pltpu.make_async_copy(feats_hbm.at[:, kv_cols], feats.at[:, kv_cols], f_sems.at[0])
    f_q = pltpu.make_async_copy(feats_hbm.at[:, pl.ds(0, ch)], feats.at[:, pl.ds(0, ch)], f_sems.at[1])
    f_kv.start()
    f_q.start()
    w_copy = pltpu.make_async_copy(w_hbm, w_vmem, w_sem)
    w_copy.start()

    p = pos[...].reshape(1, slots)
    shift = tok.bit_length() - 1
    live = lax.broadcasted_iota(jnp.int32, (1, slots), 1) < counts[0]
    owner = jnp.where(live, lax.shift_right_logical(p, shift), -1)
    local = lax.bitwise_and(p, tok - 1).astype(f32)
    mine = owner == lax.broadcasted_iota(jnp.int32, (n, slots), 0)
    tri = lax.broadcasted_iota(jnp.int32, (slots, slots), 0) <= lax.broadcasted_iota(
        jnp.int32, (slots, slots), 1
    )
    tri = tri.astype(f32).astype(bf16)
    cum = jnp.dot(mine.astype(f32).astype(bf16), tri, preferred_element_type=f32)
    rank = jnp.sum(jnp.where(mine, cum, 0.0), axis=0, keepdims=True) - 1.0
    direct = jnp.logical_and(live, rank < float(base))
    beyond = jnp.logical_and(live, rank >= float(base)).astype(f32)
    bump = jnp.dot(jnp.broadcast_to(beyond, (16, slots)).astype(bf16), tri, preferred_element_type=f32)[0:1]
    late = jnp.where(beyond > 0.0, bump - 1.0, -1.0)
    apart = lax.bitwise_xor(owner, me)
    flat = jnp.where(direct, apart.astype(f32) * float(cap) + rank, -1.0)
    spare = jnp.where(late >= 0.0, late + float(base), -1.0)
    hot_row = lax.broadcasted_iota(jnp.int32, (rows, slots), 0)
    hit = jnp.logical_or(hot_row.astype(f32) == flat, lax.bitwise_and(hot_row, cap - 1).astype(f32) == spare)
    hot_s[...] = hit.astype(f32).astype(bf16)

    def pack_rows(box, first, count, source):
        def pack(c, _):
            at = pl.ds(first, rows // 2)
            src = pl.ds(pl.multiple_of(source(c), LANES), tile)
            dst = pl.ds(pl.multiple_of(c * tile, LANES), tile)
            box[at, dst] = jnp.dot(hot_s[at, :], feats[:, src], preferred_element_type=f32).astype(bf16)
            return _

        lax.fori_loop(0, count, pack, 0)

    def pack_kv(i, first):
        t0, t1 = parts[i]
        count = t1 - t0
        pack_rows(boxes[i], first, 2 * count, lambda c: ch + (c // count) * ch + (t0 + c % count) * tile)

    boxes = (box_a, box_b, box_q)
    arrs = (arr_a, arr_b, arr_q)

    def slab(ref, k, size):
        return ref.at[pl.ds(pl.multiple_of(k * cap, cap), size), :]

    def over_rows(ref, k):
        return ref.at[pl.ds(pl.multiple_of(k * cap + base, ROWS), over), :]

    def direct_copy(which, m, size, came):
        box, arr, send, recv = boxes[which], arrs[which], sends.at[which], recvs.at[which]
        to = flip(me, m)
        return pltpu.make_async_remote_copy(
            src_ref=slab(box, m, size), dst_ref=slab(arr, to if came else me, size), send_sem=send.at[m],
            recv_sem=recv.at[m], device_id={"ctx": to}, device_id_type=MESH,
        )

    def to_mirror(which, came):
        box, arr, send, recv = boxes[which], arrs[which], over_sends.at[which], over_recvs.at[which]
        to = flip(me, half_n)
        return pltpu.make_async_remote_copy(
            src_ref=over_rows(box, half_n), dst_ref=over_rows(arr, to if came else me), send_sem=send.at[0],
            recv_sem=recv.at[0], device_id={"ctx": to}, device_id_type=MESH,
        )

    def forward(which, m, came):
        arr, send, recv = arrs[which], over_sends.at[which], over_recvs.at[which]
        to = flip(me, m)
        rows_of = over_rows(arr, flip(to if came else me, half_n))
        return pltpu.make_async_remote_copy(
            src_ref=rows_of, dst_ref=rows_of, send_sem=send.at[m], recv_sem=recv.at[m],
            device_id={"ctx": to}, device_id_type=MESH,
        )

    in_a, in_b, in_q = 0, 1, 2

    def each(first, last, make, act):
        def one(m, c):
            act(make(m))
            return c

        lax.fori_loop(first, last, one, 0)

    def start(copy):
        copy.start()

    def arrive(copy):
        copy.wait_recv()

    def sent(copy):
        copy.wait_send()

    def near(which, came=False):
        return lambda m: direct_copy(which, m, cap, came)

    def far(which, came=False):
        return lambda m: direct_copy(which, m, base, came)

    def spread_over(which, came=False):
        return lambda m: forward(which, m, came)

    def marks_to(m, to, came):
        return pltpu.make_async_remote_copy(
            src_ref=mark_out.at[to], dst_ref=mark_in.at[came], send_sem=send_m.at[m], recv_sem=recv_m.at[m],
            device_id={"ctx": to}, device_id_type=MESH,
        )

    def start_marks(m, c):
        marks_to(m, flip(me, m), me).start()
        return c

    def recv_marks(m, c):
        marks_to(m, flip(me, m), flip(me, m)).wait_recv()
        return c

    def own_copy(i):
        return pltpu.make_async_copy(slab(boxes[i], 0, cap), slab(arrs[i], me, cap), self_sems.at[i])

    f_kv.wait()
    pack_kv(in_a, rows // 2)
    pl.semaphore_wait(barrier, n - 1 + groups - 1)
    to_mirror(in_a, False).start()
    each(half_n, n, far(in_a), start)
    pack_kv(in_a, 0)
    each(1, half_n, near(in_a), start)
    own_copy(in_a).start()

    seats = (lax.broadcasted_iota(jnp.int32, (LANES, slots), 0) - lax.rem(me * cap, LANES)).astype(f32)
    in_slab = jnp.logical_and(seats >= 0.0, seats < float(cap))
    at_base = jnp.logical_and(direct, seats == rank)
    at_over = jnp.logical_and(in_slab, jnp.logical_and(late >= 0.0, seats - float(base) == late))
    last_dims = (((1,), (1,)), ((), ()))
    sub16 = lax.broadcasted_iota(jnp.int32, (16, slots), 0)
    two = jnp.where(sub16 == 0, local + 1.0, jnp.where(sub16 == 1, owner.astype(f32), 0.0)).astype(bf16)
    tell = lax.dot_general(
        jnp.where(mine, local + 1.0, 0.0).astype(bf16), at_base.astype(f32).astype(bf16), last_dims,
        preferred_element_type=f32,
    )
    tell = jnp.where(tell > 0.0, tell + (lax.broadcasted_iota(jnp.int32, (n, LANES), 0) * tok).astype(f32), 0.0)
    extra = lax.dot_general(two, at_over.astype(f32).astype(bf16), last_dims, preferred_element_type=f32)
    tell = tell + (extra[0:1] + extra[1:2] * float(tok))
    held = jnp.broadcast_to(jnp.sum(beyond, axis=1, keepdims=True), (1, LANES))
    for k in range(n):
        mark_out[k, 0:1, :] = tell[k : k + 1, :]
        mark_out[k, 1:2, :] = held
    mark_in[me] = mark_out[me]
    lax.fori_loop(1, n, start_marks, 0)

    pack_kv(in_b, rows // 2)
    to_mirror(in_b, False).start()
    to_mirror(in_a, True).wait_recv()
    each(1, half_n, spread_over(in_a), start)
    cuts = [half_n]
    for share in FLOW:
        cuts.append(min(n, cuts[-1] + share * half_n // 8))
    early = EARLY * half_n // 8
    each(half_n, half_n + early, far(in_b), start)
    pack_kv(in_b, 0)
    own_copy(in_b).start()
    f_q.wait()
    pack_rows(box_q, rows // 2, tiles, lambda c: c * tile)
    to_mirror(in_q, False).start()
    pack_rows(box_q, 0, tiles, lambda c: c * tile)
    own_copy(in_q).start()
    to_mirror(in_b, True).wait_recv()
    each(1, half_n, spread_over(in_b), start)
    decay[...] = jnp.exp(-rate[...])
    sub = lax.broadcasted_iota(jnp.int32, (ROWS, 1), 0)
    first = jnp.logical_and(sub == 0, me > 0)
    later = ((ROWS - 1 - sub) * steps).astype(f32)
    segment = (sub * steps).astype(f32)
    member, level = me % QUAD, me // QUAD
    levels = n // QUAD
    share = poles // QUAD
    for q in range(QUAD):
        rate4[q] = rate[q * share : (q + 1) * share, :]
    lags = [1, 2, 3] + [QUAD * j for j in range(1, levels - 1)]
    for at, lag in enumerate(lags):
        leaps[at] = jnp.exp(-rate4[member] * float(tok * lag))
    for at, by in enumerate((1, 2, 4)):
        hops[at] = jnp.exp(-rate[...] * float(steps * by))

    def fades_of(k, _):
        r = rate[pl.ds(k, 1), :]
        ending[k] = jnp.exp(-r * later)
        inward[k] = resid[pl.ds(k, 1), :] * jnp.exp(-r * segment)
        return _

    lax.fori_loop(0, poles, fades_of, 0)

    lax.fori_loop(1, n, recv_marks, 0)
    lanes_of = [
        sum(mark_in[k, 0:1, :] for k in range(g * (LANES // cap), (g + 1) * (LANES // cap)))
        for g in range(rows // LANES)
    ]
    came_pos = jnp.concatenate(lanes_of, axis=1) - 1.0
    worst = mark_in[0, 1:2, :]
    for k in range(1, n):
        worst = jnp.maximum(worst, mark_in[k, 1:2, :])
    group_out[...] = jnp.broadcast_to(worst, (ROWS, LANES))

    def group_copy(g, to):
        return pltpu.make_async_remote_copy(
            src_ref=group_out, dst_ref=group_in.at[g], send_sem=send_g.at[g], recv_sem=recv_g.at[g],
            device_id={"groups": to}, device_id_type=MESH,
        )

    for g in range(1, groups):
        group_copy(g, lax.rem(group + g, groups)).start()

    ext = tok + 2 * ROWS
    row = lax.broadcasted_iota(jnp.int32, (ext, 1), 0)
    want = lax.bitwise_and(row, ROWS - 1) * steps + lax.shift_right_logical(row, 3) - 2
    want = jnp.where(want < 0, -100, want + me * tok).astype(f32)
    place_s[...] = (want == came_pos).astype(f32).astype(bf16)
    rim_row = lax.broadcasted_iota(jnp.int32, (16, 1), 0)
    rim_want = jnp.where(rim_row < 2, rim_row + me * tok + tok - 2, -100).astype(f32)
    rim_hot = (rim_want == came_pos).astype(f32).astype(bf16)

    to_mirror(in_q, True).wait_recv()
    each(1, half_n, spread_over(in_q), start)

    def take_then_send(which, then, ahead, first_sent):
        each(half_n, n - ahead, far(which, True), arrive)

        def both(m, c):
            far(which, True)(m).wait_recv()
            far(then)(m - n + ahead + first_sent).start()
            return c

        lax.fori_loop(n - ahead, n, both, 0)

    own_copy(in_a).wait()
    each(1, half_n, near(in_a, True), arrive)
    each(1, half_n, near(in_b), start)
    each(1, half_n, spread_over(in_a, True), arrive)
    take_then_send(in_a, in_b, half_n - early, half_n + early)

    def rim_copy(i, to):
        wide = (2 * (parts[i][1] - parts[i][0]) if i < len(parts) else tiles) * tile
        cols = pl.ds((2 * parts[i][0] if i < len(parts) else 2 * tiles) * tile, wide)
        return pltpu.make_async_remote_copy(
            src_ref=rims_out.at[:, cols], dst_ref=rims_in.at[:, cols], send_sem=rim_sems.at[2 * i],
            recv_sem=rim_sems.at[2 * i + 1], device_id={"ctx": to}, device_id_type=MESH,
        )

    after, before = lax.rem(me + 1, n), lax.rem(me + n - 1, n)

    def rim_send(i):
        count = 2 * (parts[i][1] - parts[i][0]) if i < len(parts) else tiles
        base_tile = 2 * parts[i][0] if i < len(parts) else 2 * tiles

        def fill(c, _):
            src = pl.ds(pl.multiple_of(c * tile, LANES), tile)
            dst = pl.ds(pl.multiple_of((base_tile + c) * tile, LANES), tile)
            rims_out[:, dst] = jnp.dot(rim_hot, arrs[i][:, src], preferred_element_type=f32)[0:ROWS].astype(bf16)
            return _

        lax.fori_loop(0, count, fill, 0)
        rim_copy(i, after).start()

    def featured(arr, at, w_at):
        x = jnp.dot(place_s[...], arr[:, pl.ds(pl.multiple_of(at, LANES), tile)], preferred_element_type=f32)
        w = convw[:, pl.ds(pl.multiple_of(w_at, LANES), tile)]
        return w[0:1] * x[2 * ROWS :] + w[1:2] * x[ROWS : ROWS + tok] + w[2:3] * x[:tok]

    def product(i):
        t0, t1 = parts[i]
        wide = (t1 - t0) * tile

        def product_tile(c, _):
            at = (c - t0) * tile
            k = featured(arrs[i], at, ch + c * tile)
            v = featured(arrs[i], wide + at, 2 * ch + c * tile)
            raw[:, pl.ds(pl.multiple_of(c * tile, LANES), tile)] = k[: 2 * ROWS]
            raw[:, pl.ds(pl.multiple_of(ch + c * tile, LANES), tile)] = v[: 2 * ROWS]
            prod[:, pl.ds(pl.multiple_of(c * tile, LANES), tile)] = k * v
            return _

        lax.fori_loop(t0, t1, product_tile, 0)

    def product_edges(i):
        t0, t1 = parts[i]
        wide = (t1 - t0) * tile
        rim_copy(i, before).wait_recv()

        def edge_tile(c, _):
            def with_edge(at, rim_at):
                cols = pl.ds(pl.multiple_of(at, LANES), tile)
                w = convw[:, pl.ds(pl.multiple_of(ch + at, LANES), tile)]
                edge = rims_in[:, pl.ds(pl.multiple_of(rim_at, LANES), tile)].astype(f32)
                top = jnp.where(first, w[1:2] * edge[1:2] + w[2:3] * edge[0:1], 0.0)
                nxt = jnp.where(first, w[2:3] * edge[1:2], 0.0)
                return jnp.concatenate([raw[0:ROWS, cols] + top, raw[ROWS:, cols] + nxt], axis=0)

            rim_at = (2 * t0 + c - t0) * tile
            prod[0 : 2 * ROWS, pl.ds(pl.multiple_of(c * tile, LANES), tile)] = with_edge(
                c * tile, rim_at
            ) * with_edge(ch + c * tile, rim_at + wide)
            return _

        lax.fori_loop(t0, t1, edge_tile, 0)

    def spread(ref, k, cols):
        return jnp.broadcast_to(ref[k : k + 1, cols], (ROWS, LANES))

    def total(terms):
        while len(terms) > 1:
            terms = [a + b for a, b in zip(terms[::2], terms[1::2])] + terms[len(terms) // 2 * 2 :]
        return terms[0]

    def local_tile(c, _):
        cols = pl.ds(pl.multiple_of(c * LANES, LANES), LANES)
        dec = [spread(decay, k, cols) for k in range(poles)]
        res = [spread(resid, k, cols) for k in range(poles)]
        gain = jnp.broadcast_to(skip[pl.ds(pl.multiple_of(c * LANES, LANES), LANES)].reshape(1, LANES), (ROWS, LANES))

        def step(i, st):
            at = pl.ds(pl.multiple_of(i * ROWS, ROWS), ROWS)
            x = prod[at, cols]
            st = tuple(d * s + x for d, s in zip(dec, st))
            filt[at, cols] = gain * x + total([r * s for r, s in zip(res, st)])
            return st

        zero = jnp.zeros((ROWS, LANES), f32)
        st = lax.fori_loop(0, steps, step, (zero,) * poles, unroll=4)
        for k in range(poles):
            state[k, :, cols] = st[k]
            own[k : k + 1, cols] = jnp.sum(ending[k, :, cols] * st[k], axis=0, keepdims=True)
        return _

    def prefix_tile(c, _):
        cols = pl.ds(pl.multiple_of(c * LANES, LANES), LANES)
        for k in range(poles):
            x = jnp.where(sub == 0, 0.0, pltpu.roll(state[k, :, cols], 1, 0))
            for at, by in enumerate((1, 2, 4)):
                x = x + jnp.where(sub >= by, hops[at, k : k + 1, cols] * pltpu.roll(x, by, 0), 0.0)
            state[k, :, cols] = resid[k : k + 1, cols] * x
        return _

    per = tile // LANES

    def lanes(part):
        return pl.ds(part[0] * tile, (part[1] - part[0]) * tile)

    def scan_copy(part, stage, j, out_way):
        cols = lanes(part)
        here = member if stage != 1 else level
        count = QUAD if stage != 1 else levels
        peer = lax.rem(here + (j if out_way else count - j), count)
        to = level * QUAD + peer if stage != 1 else peer * QUAD + member
        start_at = stage * max(QUAD, levels)
        source, slot = (totals.at[0, :, cols], start_at + here) if stage == 1 else (
            tx.at[stage // 2 * QUAD + peer, :, cols], start_at + here)
        if not out_way:
            slot = start_at + peer
        at = (start_at + j) * len(parts) + parts.index(part)
        return pltpu.make_async_remote_copy(
            src_ref=source, dst_ref=rx.at[slot, :, cols], send_sem=scan_send.at[at],
            recv_sem=scan_recv.at[at], device_id={"ctx": to}, device_id_type=MESH,
        )

    def scan_moves(part, stage, out_way, act):
        for j in range(1, QUAD if stage != 1 else levels):
            act(scan_copy(part, stage, j, out_way))

    def leap(lag, cols):
        return leaps[lags.index(lag), :, cols]

    def scan_open(part):
        cols = lanes(part)
        for q in range(QUAD):
            tx[q, :, cols] = own[q * share : (q + 1) * share, cols]
        rx[member, :, cols] = tx[member, :, cols]
        scan_moves(part, 0, True, start)

    def scan_totals(part):
        cols = lanes(part)
        scan_moves(part, 0, False, arrive)
        t = rx[QUAD - 1, :, cols]
        for i in range(QUAD - 1):
            t = t + leap(QUAD - 1 - i, cols) * rx[i, :, cols]
        totals[0, :, cols] = t
        scan_moves(part, 1, True, start)

    def scan_carries(part):
        cols = lanes(part)
        scan_moves(part, 1, False, arrive)
        carried = jnp.zeros((share, (part[1] - part[0]) * tile), f32)
        for j in range(1, levels):
            got = rx[max(QUAD, levels) + lax.rem(level + levels - j, levels), :, cols]
            got = got if j == 1 else leap(QUAD * (j - 1), cols) * got
            carried = carried + jnp.where(level >= j, got, 0.0)
        for i in range(QUAD):
            tx[QUAD + i, :, cols] = carried
            carried = rx[i, :, cols] + leap(1, cols) * carried
        rx[2 * max(QUAD, levels) + member, :, cols] = tx[QUAD + member, :, cols]
        scan_moves(part, 2, True, start)

    def scan_close(part):
        cols = lanes(part)
        scan_moves(part, 2, False, arrive)
        for q in range(QUAD):
            acc[q * share : (q + 1) * share, cols] = rx[2 * max(QUAD, levels) + q, :, cols]


    def local(part):
        lax.fori_loop(part[0] * per, part[1] * per, local_tile, 0)

    def prefix(part):
        lax.fori_loop(part[0] * per, part[1] * per, prefix_tile, 0)

    part_a, part_b = parts
    def carry_tile(c, _):
        cols = pl.ds(pl.multiple_of(c * LANES, LANES), LANES)
        dec = [spread(decay, k, cols) for k in range(poles)]
        begin = tuple(
            state[k, :, cols] + inward[k, :, cols] * acc[k : k + 1, cols] for k in range(poles)
        )

        def step(i, g):
            at = pl.ds(pl.multiple_of(i * ROWS, ROWS), ROWS)
            g = tuple(d * s for d, s in zip(dec, g))
            filt[at, cols] = filt[at, cols] + total(list(g))
            return g

        lax.fori_loop(0, steps, step, begin, unroll=4)
        return _

    def carry(part):
        scan_close(part)
        lax.fori_loop(part[0] * per, part[1] * per, carry_tile, 0)

    rim_send(in_a)
    product(in_a)
    product_edges(in_a)
    local(part_a)
    scan_open(part_a)
    prefix(part_a)
    own_copy(in_b).wait()
    each(1, half_n, near(in_b, True), arrive)
    each(1, half_n, near(in_q), start)
    each(half_n, cuts[1], far(in_q), start)
    scan_totals(part_a)
    each(1, half_n, spread_over(in_b, True), arrive)
    take_then_send(in_b, in_q, cuts[2] - cuts[1], cuts[1])
    rim_send(in_b)
    scan_carries(part_a)
    product(in_b)
    each(cuts[2], cuts[3], far(in_q), start)
    product_edges(in_b)
    local(part_b)
    scan_open(part_b)
    each(cuts[3], cuts[4], far(in_q), start)
    prefix(part_b)
    scan_totals(part_b)
    carry(part_a)
    each(cuts[4], n, far(in_q), start)
    scan_carries(part_b)
    carry(part_b)
    top_of = worst
    for g in range(1, groups):
        group_copy(g, lax.rem(group + groups - g, groups)).wait_recv()
        top_of = jnp.maximum(top_of, group_in[g, 0:1, :])
    most[0] = jnp.max(top_of).astype(jnp.int32)
    w_copy.wait()

    own_copy(in_q).wait()
    each(1, half_n, near(in_q, True), arrive)
    each(1, half_n, spread_over(in_q, True), arrive)
    each(half_n, n, far(in_q, True), arrive)
    rim_send(in_q)

    def gate_tile(c, _):
        at = c * tile
        cols = pl.ds(pl.multiple_of(at, LANES), tile)
        y = featured(arr_q, at, at)
        raw[:, cols] = y[: 2 * ROWS]
        gated[:, cols] = (y * filt[:, cols]).astype(bf16)
        return _

    lax.fori_loop(0, ch // tile, gate_tile, 0)
    rim_copy(in_q, before).wait_recv()
    edge = rims_in[:, 2 * ch :].astype(f32)
    w1, w2 = convw[1:2, 0:ch], convw[2:3, 0:ch]
    top = jnp.where(first, w1 * edge[1:2] + w2 * edge[0:1], 0.0)
    nxt = jnp.where(first, w2 * edge[1:2], 0.0)
    begun = raw[:, 0:ch] + jnp.concatenate([top, nxt], axis=0)
    gated[0 : 2 * ROWS, :] = (begun * filt[0 : 2 * ROWS, :]).astype(bf16)

    nat = lax.broadcasted_iota(jnp.int32, (tok, 1), 0)
    seat = lax.bitwise_and(nat, steps - 1) * ROWS + lax.shift_right_logical(nat, steps.bit_length() - 1)
    order = (seat == lax.broadcasted_iota(jnp.int32, (tok, tok), 1)).astype(f32).astype(bf16)

    def order_tile(c, _):
        cols = pl.ds(pl.multiple_of(c * tile, LANES), tile)
        natural[:, cols] = jnp.dot(order, gated[:, cols], preferred_element_type=f32).astype(bf16)
        return _

    lax.fori_loop(0, ch // tile, order_tile, 0)

    def out_tile(c, _):
        cols = pl.ds(pl.multiple_of(c * tile, LANES), tile)
        out[:, cols] = jnp.dot(natural[...], w_vmem[:, cols], preferred_element_type=f32).astype(bf16)
        return _

    lax.fori_loop(0, ch // tile, out_tile, 0)

    for which in (in_a, in_b, in_q):
        each(1, half_n, near(which), sent)
        each(half_n, n, far(which), sent)
    for which in (in_a, in_b, in_q):
        to_mirror(which, False).wait_send()
        each(1, half_n, spread_over(which), sent)
    each(1, n, lambda m: marks_to(m, flip(me, m), me), sent)
    for g in range(1, groups):
        group_copy(g, lax.rem(group + g, groups)).wait_send()
    for which in (in_a, in_b, in_q):
        rim_copy(which, after).wait_send()
    for stage in range(3):
        for part in parts:
            scan_moves(part, stage, True, sent)


def swift_call(n, groups, cap, base, tok, args):
    counts, features, positions, conv_weight, pole_rate, pole_residue, skip_gain, out_weight = args
    slots, feat = features.shape
    ch = feat // 3
    poles = pole_rate.shape[0]
    rows = n * cap
    share = poles // QUAD
    wide = max(QUAD, n // QUAD)
    lead = (ch // col_tile(ch) + 1) // 2 * col_tile(ch)
    whole = pl.BlockSpec(memory_space=pltpu.VMEM)
    dma = pltpu.SemaphoreType.DMA
    vmem = pltpu.VMEM
    return pl.pallas_call(
        functools.partial(swift, n, groups, cap, base, tok),
        out_shape=(jax.ShapeDtypeStruct((tok, ch), bf16), jax.ShapeDtypeStruct((1,), jnp.int32)),
        in_specs=[pl.BlockSpec(memory_space=pltpu.SMEM), pl.BlockSpec(memory_space=pl.ANY)]
        + [whole] * 5 + [pl.BlockSpec(memory_space=pl.ANY)],
        out_specs=(whole, pl.BlockSpec(memory_space=pltpu.SMEM)),
        scratch_shapes=[
            vmem((rows, 2 * lead), bf16),
            vmem((rows, 2 * (ch - lead)), bf16),
            vmem((rows, ch), bf16),
            vmem((rows, 2 * lead), bf16),
            vmem((rows, 2 * (ch - lead)), bf16),
            vmem((rows, ch), bf16),
            vmem((n, 2, LANES), f32),
            vmem((n, 2, LANES), f32),
            vmem((ROWS, LANES), f32),
            vmem((groups, ROWS, LANES), f32),
            vmem((rows, slots), bf16),
            vmem((tok + 2 * ROWS, rows), bf16),
            vmem((tok, ch), f32),
            vmem((tok, ch), f32),
            vmem((tok, ch), bf16),
            vmem((tok, ch), bf16),
            vmem((poles, ROWS, ch), f32),
            vmem((slots, feat), bf16),
            vmem((poles, ch), f32),
            vmem((ROWS, feat), bf16),
            vmem((ROWS, feat), bf16),
            vmem((poles, ch), f32),
            vmem((poles, ch), f32),
            vmem((1, share, ch), f32),
            vmem((QUAD, share, ch), f32),
            vmem((2 * QUAD, share, ch), f32),
            vmem((3 * wide, share, ch), f32),
            vmem(out_weight.shape, bf16),
            dma((3, n)), dma((3, n)), dma((3, n)), dma((3, n)), dma((n,)), dma((n,)), dma((groups,)), dma((groups,)),
            vmem((2 * ROWS, 2 * ch), f32),
            vmem((poles, ROWS, ch), f32),
            vmem((poles, ROWS, ch), f32),
            vmem((3, poles, ch), f32),
            vmem((2 + n // QUAD, share, ch), f32),
            dma((6,)), dma((6 * wide,)), dma((6 * wide,)), dma((3,)), dma, dma((2,)),
        ],
        compiler_params=pltpu.CompilerParams(
            collective_id=1, has_side_effects=True, vmem_limit_bytes=60 << 20
        ),
        name="hyena_direct",
    )(*args)


def mega_call(n, cap, tok, args):
    counts, features, positions, conv_weight, pole_rate, pole_residue, skip_gain, out_weight = args
    slots, feat = features.shape
    ch = feat // 3
    poles = pole_rate.shape[0]
    rows = n * cap
    stages = len(scan_spans(n))
    whole = pl.BlockSpec(memory_space=pltpu.VMEM)
    dma = pltpu.SemaphoreType.DMA
    return pl.pallas_call(
        functools.partial(mega, n, cap, tok, PACE[0] * (n - 1) // 15),
        out_shape=jax.ShapeDtypeStruct((tok, ch), bf16),
        in_specs=[pl.BlockSpec(memory_space=pltpu.SMEM), pl.BlockSpec(memory_space=pl.ANY)]
        + [whole] * 5 + [pl.BlockSpec(memory_space=pl.ANY)],
        out_specs=whole,
        scratch_shapes=[
            pltpu.VMEM((rows, 2 * ch + LANES), bf16),
            pltpu.VMEM((rows, ch), bf16),
            pltpu.VMEM((rows, 2 * ch + LANES), bf16),
            pltpu.VMEM((rows, ch), bf16),
            pltpu.VMEM((rows, slots), bf16),
            pltpu.VMEM((tok + 2 * ROWS, rows), bf16),
            pltpu.VMEM((tok, ch), f32),
            pltpu.VMEM((tok, ch), f32),
            pltpu.VMEM((16, LANES), bf16),
            pltpu.VMEM((tok, ch), bf16),
            pltpu.VMEM((poles, ROWS, ch), f32),
            pltpu.VMEM((slots, feat), bf16),
            pltpu.VMEM((poles, ch), f32),
            pltpu.VMEM((16, 2 * ch), bf16),
            pltpu.VMEM((16, 2 * ch), bf16),
            pltpu.VMEM((16, ch), bf16),
            pltpu.VMEM((16, ch), bf16),
            pltpu.VMEM((poles, ch), f32),
            pltpu.VMEM((1, poles, ch), f32),
            pltpu.VMEM((stages, poles, ch), bf16),
            pltpu.VMEM((3 * stages, poles, ch), bf16),
            pltpu.VMEM(out_weight.shape, bf16),
            dma((n,)), dma((n,)), dma((n,)), dma((n,)), dma((4,)), dma((3 * stages,)), dma((3 * stages,)),
            dma((2,)), dma, dma((2,)),
        ],
        compiler_params=pltpu.CompilerParams(
            collective_id=0, has_side_effects=True, vmem_limit_bytes=60 << 20
        ),
        name="hyena",
    )(*args)


def on_device(
    features, positions, counts, conv_weight, pole_rate, pole_residue, skip_gain, out_weight
):
    n = lax.axis_size("ctx")
    groups = lax.axis_size("groups")
    slots, feat = features.shape
    ch = feat // 3
    tok = 2 * slots // 3
    cap = 2 * tok // n
    poles = pole_rate.shape[0]
    if cap % 16 or tok & (tok - 1) or tok > 256 or conv_weight.shape[0] != 3 or ch % LANES or n & (n - 1) or n < 4:
        return plain_on_device(
            features, positions, counts, conv_weight, pole_rate, pole_residue, skip_gain, out_weight
        )
    args = (counts, features, positions, conv_weight, pole_rate, pole_residue, skip_gain, out_weight)
    base = slots // n
    if poles % QUAD or base % ROWS or cap - base > 16 or LANES % cap:
        return mega_call(n, cap, tok, args)
    done, most = swift_call(n, groups, cap, base, tok, args)
    return lax.cond(most[0] > cap - base, lambda d: mega_call(n, cap, tok, args), lambda d: d, done)


PACE = (2, 1, 1, 2, 2)
FLOW = (3, 2, 1, 1)
EARLY = 0
QUAD = 4


def solution(mesh):
    return jax.shard_map(
        on_device,
        mesh=mesh,
        in_specs=(
            P(("groups", "ctx"), None),
            P(("groups", "ctx")),
            P(("groups", "ctx")),
            P(),
            P(),
            P(),
            P(),
            P(),
        ),
        out_specs=P(("groups", "ctx"), None),
        check_vma=False,
    )
```

```python
import functools

import jax
import jax.numpy as jnp
from jax import lax
from jax.experimental import pallas as pl
from jax.experimental.pallas import tpu as pltpu
from jax.sharding import PartitionSpec as P

LANES = 128
ROWS = 8
MESH = pl.DeviceIdType.MESH
f32, bf16 = jnp.float32, jnp.bfloat16

block_len = 32


def from_behind(array, axis, by):
    count = lax.axis_size(axis)
    pairs = [(i, i + by) for i in range(count) if 0 <= i + by < count]
    return lax.ppermute(array, axis, pairs)


def plain_on_device(
    features, positions, counts, conv_weight, pole_rate, pole_residue, skip_gain, out_weight
):
    devices = lax.axis_size("ctx")
    slot_count = features.shape[0]
    feat_width = features.shape[1]
    channels = feat_width // 3
    tok_rows = 2 * slot_count // 3
    pair_cap = 2 * tok_rows // devices
    taps = conv_weight.shape[0]
    poles = pole_rate.shape[0]
    slot_ids = jnp.arange(slot_count, dtype=jnp.int32)
    is_live = slot_ids < counts[0]
    owners = jnp.where(is_live, positions // tok_rows, devices)
    same = jnp.logical_and(owners[:, None] == owners[None, :], slot_ids[None, :] < slot_ids[:, None])
    within = jnp.sum(same.astype(jnp.int32), axis=1)
    flat_index = jnp.where(is_live, owners * pair_cap + within, devices * pair_cap)
    outbox = (
        jnp.zeros((devices * pair_cap + 1, feat_width), features.dtype)
        .at[flat_index]
        .set(features)[:-1]
    )
    local_pos = (
        jnp.full((devices * pair_cap + 1,), -1, jnp.int32)
        .at[flat_index]
        .set(positions % tok_rows)[:-1]
    )
    outbox = outbox.reshape(devices, pair_cap, feat_width)
    local_pos = local_pos.reshape(devices, pair_cap)
    arrived, arrived_pos = (
        lax.all_to_all(outbox, "ctx", split_axis=0, concat_axis=0, tiled=True),
        lax.all_to_all(local_pos, "ctx", split_axis=0, concat_axis=0, tiled=True),
    )
    target = jnp.where(arrived_pos >= 0, arrived_pos, tok_rows).reshape(-1)
    placed = (
        jnp.zeros((tok_rows + 1, feat_width), features.dtype)
        .at[target]
        .set(arrived.reshape(-1, feat_width))[:-1]
    )
    rim_rows = from_behind(placed[tok_rows - (taps - 1) :], "ctx", 1)
    extended = jnp.concatenate([rim_rows, placed], axis=0)
    featured = jnp.zeros((tok_rows, feat_width), jnp.float32)
    for tap in range(taps):
        start = taps - 1 - tap
        featured = featured + conv_weight[tap][None, :] * extended[start : start + tok_rows].astype(
            jnp.float32
        )
    query_feat = featured[:, :channels]
    product = featured[:, channels : 2 * channels] * featured[:, 2 * channels :]
    num_blocks = tok_rows // block_len
    lag_steps = jnp.arange(block_len + 1).astype(jnp.float32)
    powers = jnp.exp(-pole_rate[None] * lag_steps[:, None, None])
    filter_taps = jnp.sum(powers[:block_len] * pole_residue[None], axis=1)
    blocked = product.reshape(num_blocks, block_len, channels)
    padded_blk = jnp.pad(blocked, ((0, 0), (block_len - 1, 0), (0, 0)))
    inside = jnp.zeros((num_blocks, block_len, channels), jnp.float32)
    for lag in range(block_len):
        first = block_len - 1 - lag
        inside = inside + filter_taps[lag][None, None, :] * padded_blk[:, first : first + block_len]
    blk_sums = jnp.zeros((num_blocks, poles, channels), jnp.float32)
    for row in range(block_len):
        blk_sums = blk_sums + powers[block_len - 1 - row][None] * blocked[:, row][:, None, :]
    decay_blk = powers[block_len]

    def advance(running, block_sum):
        return (decay_blk * running + block_sum, running)

    local_end, starts = lax.scan(advance, jnp.zeros((poles, channels), jnp.float32), blk_sums)
    decay_dev = jnp.exp(-pole_rate * float(tok_rows))

    def relay_step(counter, incoming):
        return from_behind(decay_dev * incoming + local_end, "ctx", 1)

    carry_in = lax.fori_loop(0, devices - 1, relay_step, jnp.zeros_like(local_end))
    block_starts = (jnp.arange(num_blocks) * block_len).astype(jnp.float32)
    block_decay = jnp.exp(-pole_rate[None] * block_starts[:, None, None])
    incoming = starts + block_decay * carry_in[None]
    inward = pole_residue[None] * powers[1:]
    from_state = jnp.zeros((num_blocks, block_len, channels), jnp.float32)
    for pole in range(poles):
        from_state = from_state + inward[:, pole][None] * incoming[:, pole][:, None, :]
    convolved = (inside + from_state).reshape(tok_rows, channels)
    filtered = skip_gain[None, :] * product + convolved
    gated_rows = (query_feat * filtered).astype(jnp.bfloat16)
    return jnp.dot(gated_rows, out_weight, preferred_element_type=jnp.float32).astype(jnp.bfloat16)

def col_tile(width):
    for tile in (384, 256, 128):
        if width % tile == 0:
            return tile
    return width


def scan_spans(n):
    spans, span = [], 1
    while span < n:
        spans.append(span)
        span *= 4
    return spans


def mega(
    n, cap, tok, up_front,
    counts, feats_hbm, pos, convw, rate, resid, skip, w_hbm, out,
    box_kv, box_q, arr_kv, arr_q, hot_s, place_s, prod, filt, gated, natural, state,
    feats, decay, rim_kv_out, rim_kv_in, rim_q_out, rim_q_in, own, acc, tx, rx, w_vmem,
    send_kv, recv_kv, send_q, recv_q, rim_sems, scan_send, scan_recv, self_sems, w_sem, f_sems,
):
    me = lax.axis_index("ctx")
    slots, feat = feats_hbm.shape
    ch = feat // 3
    poles = rate.shape[0]
    steps = tok // ROWS
    tile = col_tile(ch)
    rows = n * cap
    barrier = pltpu.get_barrier_semaphore()

    bits = (n - 1).bit_length()

    def mask_of(d):
        return sum(((d // (1 << b)) % 2) * (1 << (bits - 1 - b)) for b in range(bits))

    def peer_of(d):
        m = mask_of(d)
        return sum(((me // (1 << b) + m // (1 << b)) % 2) * (1 << b) for b in range(bits))

    def greet(d, c):
        pl.semaphore_signal(barrier, inc=1, device_id={"ctx": peer_of(d)}, device_id_type=MESH)
        return c

    lax.fori_loop(1, n, greet, 0)
    kv_cols = pl.ds(ch, 2 * ch)
    f_kv = pltpu.make_async_copy(feats_hbm.at[:, kv_cols], feats.at[:, kv_cols], f_sems.at[0])
    f_q = pltpu.make_async_copy(feats_hbm.at[:, pl.ds(0, ch)], feats.at[:, pl.ds(0, ch)], f_sems.at[1])
    f_kv.start()
    f_q.start()
    w_copy = pltpu.make_async_copy(w_hbm, w_vmem, w_sem)
    w_copy.start()

    p = pos[...].reshape(1, slots)
    shift = tok.bit_length() - 1
    live = lax.broadcasted_iota(jnp.int32, (1, slots), 1) < counts[0]
    owner = jnp.where(live, lax.shift_right_logical(p, shift), -1)
    local = lax.bitwise_and(p, tok - 1).astype(f32)
    mine = owner == lax.broadcasted_iota(jnp.int32, (n, slots), 0)
    tri = lax.broadcasted_iota(jnp.int32, (slots, slots), 0) <= lax.broadcasted_iota(
        jnp.int32, (slots, slots), 1
    )
    cum = jnp.dot(mine.astype(f32).astype(bf16), tri.astype(f32).astype(bf16), preferred_element_type=f32)
    rank = jnp.sum(jnp.where(mine, cum, 0.0), axis=0, keepdims=True) - 1.0
    flat = owner.astype(f32) * float(cap) + rank
    hit = lax.broadcasted_iota(jnp.int32, (rows, slots), 0).astype(f32) == flat
    hot_s[...] = hit.astype(f32).astype(bf16)
    marks = jnp.sum(jnp.where(hit, local + 1.0, 0.0), axis=1, keepdims=True) - 1.0
    box_kv[:, 2 * ch :] = jnp.broadcast_to(marks, (rows, LANES)).astype(bf16)

    def pack_kv(c, _):
        src = pl.ds(pl.multiple_of(ch + c * tile, LANES), tile)
        dst = pl.ds(pl.multiple_of(c * tile, LANES), tile)
        box_kv[:, dst] = jnp.dot(hot_s[...], feats[:, src], preferred_element_type=f32).astype(bf16)
        return _

    def pack_q(c, _):
        dst = pl.ds(pl.multiple_of(c * tile, LANES), tile)
        box_q[:, dst] = jnp.dot(hot_s[...], feats[:, dst], preferred_element_type=f32).astype(bf16)
        return _

    f_kv.wait()
    lax.fori_loop(0, 2 * ch // tile, pack_kv, 0)

    def slab(ref, k):
        return ref.at[pl.ds(pl.multiple_of(k * cap, cap), cap), :]

    def outgoing(box, arr, send, recv, d):
        to = peer_of(d)
        return pltpu.make_async_remote_copy(
            src_ref=slab(box, to), dst_ref=slab(arr, me), send_sem=send.at[d], recv_sem=recv.at[d],
            device_id={"ctx": to}, device_id_type=MESH,
        )

    def incoming(box, arr, send, recv, d):
        came = peer_of(d)
        return pltpu.make_async_remote_copy(
            src_ref=slab(box, came), dst_ref=slab(arr, came), send_sem=send.at[d], recv_sem=recv.at[d],
            device_id={"ctx": came}, device_id_type=MESH,
        )

    def start_kv(d, c):
        outgoing(box_kv, arr_kv, send_kv, recv_kv, d).start()
        return c

    def start_q(d, c):
        outgoing(box_q, arr_q, send_q, recv_q, d).start()
        return c

    def recv_kv_wait(d, c):
        incoming(box_kv, arr_kv, send_kv, recv_kv, d).wait_recv()
        return c

    def recv_q_wait(d, c):
        incoming(box_q, arr_q, send_q, recv_q, d).wait_recv()
        return c

    def send_waits(d, c):
        outgoing(box_kv, arr_kv, send_kv, recv_kv, d).wait_send()
        outgoing(box_q, arr_q, send_q, recv_q, d).wait_send()
        return c

    pl.semaphore_wait(barrier, n - 1)
    lax.fori_loop(1, n, start_kv, 0)
    own_kv = pltpu.make_async_copy(slab(box_kv, me), slab(arr_kv, me), self_sems.at[0])
    own_kv.start()
    f_q.wait()
    lax.fori_loop(0, ch // tile, pack_q, 0)
    own_q = pltpu.make_async_copy(slab(box_q, me), slab(arr_q, me), self_sems.at[1])
    own_q.start()
    lax.fori_loop(1, 1 + up_front, start_q, 0)
    decay[...] = jnp.exp(-rate[...])

    own_kv.wait()
    lax.fori_loop(1, n, recv_kv_wait, 0)

    ext = tok + 2 * ROWS
    came_pos = jnp.transpose(arr_kv[:, 2 * ch :].astype(f32))[0:1, :]
    row = lax.broadcasted_iota(jnp.int32, (ext, 1), 0)
    want = lax.bitwise_and(row, ROWS - 1) * steps + lax.shift_right_logical(row, 3) - 2
    want = jnp.where(want < 0, -100, want).astype(f32)
    place_s[...] = (want == came_pos).astype(f32).astype(bf16)
    rim_row = lax.broadcasted_iota(jnp.int32, (16, 1), 0)
    rim_want = jnp.where(rim_row < 2, rim_row + tok - 2, -100).astype(f32)
    rim_hot = (rim_want == came_pos).astype(f32).astype(bf16)

    def rim_copy(src, dst, k, to):
        return pltpu.make_async_remote_copy(
            src_ref=src, dst_ref=dst, send_sem=rim_sems.at[2 * k], recv_sem=rim_sems.at[2 * k + 1],
            device_id={"ctx": to}, device_id_type=MESH,
        )

    after, before = lax.rem(me + 1, n), lax.rem(me + n - 1, n)

    def rim_kv_tile(c, _):
        cols = pl.ds(pl.multiple_of(c * tile, LANES), tile)
        rim_kv_out[:, cols] = jnp.dot(rim_hot, arr_kv[:, cols], preferred_element_type=f32).astype(bf16)
        return _

    def rim_q_tile(c, _):
        cols = pl.ds(pl.multiple_of(c * tile, LANES), tile)
        rim_q_out[:, cols] = jnp.dot(rim_hot, arr_q[:, cols], preferred_element_type=f32).astype(bf16)
        return _

    lax.fori_loop(0, 2 * ch // tile, rim_kv_tile, 0)
    rim_kv = rim_copy(rim_kv_out, rim_kv_in, 0, after)
    rim_kv.start()
    spans = scan_spans(n)
    cuts = [1]
    for share in PACE:
        cuts.append(min(n, cuts[-1] + share * (n - 1) // 15))
    lax.fori_loop(cuts[1], cuts[2], start_q, 0)
    rim_copy(rim_kv_out, rim_kv_in, 0, before).wait_recv()

    sub = lax.broadcasted_iota(jnp.int32, (ROWS, 1), 0)
    first = jnp.logical_and(sub == 0, me > 0)

    def featured(arr, at, w_at, rim, rim_at):
        x = jnp.dot(place_s[...], arr[:, pl.ds(pl.multiple_of(at, LANES), tile)], preferred_element_type=f32)
        w = convw[:, pl.ds(pl.multiple_of(w_at, LANES), tile)]
        y = w[0:1] * x[2 * ROWS :] + w[1:2] * x[ROWS : ROWS + tok] + w[2:3] * x[:tok]
        if rim is None:
            return y
        edge = rim[:, pl.ds(pl.multiple_of(rim_at, LANES), tile)].astype(f32)
        top = jnp.where(first, w[1:2] * edge[1:2] + w[2:3] * edge[0:1], 0.0)
        nxt = jnp.where(first, w[2:3] * edge[1:2], 0.0)
        return jnp.concatenate([y[:ROWS] + top, y[ROWS : 2 * ROWS] + nxt, y[2 * ROWS :]], axis=0)

    def product_tile(c, _):
        at = c * tile
        k = featured(arr_kv, at, ch + at, rim_kv_in, at)
        v = featured(arr_kv, ch + at, 2 * ch + at, rim_kv_in, ch + at)
        prod[:, pl.ds(pl.multiple_of(at, LANES), tile)] = k * v
        return _

    lax.fori_loop(0, ch // tile, product_tile, 0)
    lax.fori_loop(cuts[2], cuts[3], start_q, 0)

    def spread(ref, k, cols):
        return jnp.broadcast_to(ref[k : k + 1, cols], (ROWS, LANES))

    later = ((ROWS - 1 - sub) * steps).astype(f32)

    def total(terms):
        while len(terms) > 1:
            terms = [a + b for a, b in zip(terms[::2], terms[1::2])] + terms[len(terms) // 2 * 2 :]
        return terms[0]

    def local_tile(c, _):
        cols = pl.ds(pl.multiple_of(c * LANES, LANES), LANES)
        dec = [spread(decay, k, cols) for k in range(poles)]
        res = [spread(resid, k, cols) for k in range(poles)]
        gain = jnp.broadcast_to(skip[pl.ds(pl.multiple_of(c * LANES, LANES), LANES)].reshape(1, LANES), (ROWS, LANES))

        def step(i, st):
            at = pl.ds(pl.multiple_of(i * ROWS, ROWS), ROWS)
            x = prod[at, cols]
            st = tuple(d * s + x for d, s in zip(dec, st))
            filt[at, cols] = gain * x + total([r * s for r, s in zip(res, st)])
            return st

        zero = jnp.zeros((ROWS, LANES), f32)
        st = lax.fori_loop(0, steps, step, (zero,) * poles, unroll=2)
        for k in range(poles):
            state[k, :, cols] = st[k]
            fade = jnp.exp(-rate[k : k + 1, cols] * later)
            own[k : k + 1, cols] = jnp.sum(fade * st[k], axis=0, keepdims=True)
        return _

    half = ch // LANES // 2
    lax.fori_loop(0, half, local_tile, 0)
    lax.fori_loop(cuts[3], cuts[4], start_q, 0)
    lax.fori_loop(half, ch // LANES, local_tile, 0)

    def scan_copy(k, j, to):
        return pltpu.make_async_remote_copy(
            src_ref=tx.at[k], dst_ref=rx.at[3 * k + j - 1], send_sem=scan_send.at[3 * k + j - 1],
            recv_sem=scan_recv.at[3 * k + j - 1], device_id={"ctx": to}, device_id_type=MESH,
        )

    def scan_moves(k, send, act):
        span = spans[k]
        for j in range(1, 4):
            if j * span < n:
                to = me + j * span if send else me - j * span
                act(scan_copy(k, j, lax.rem(to + n, n)))

    acc[0] = jnp.zeros((poles, ch), f32)
    for k, span in enumerate(spans):
        tx[k] = own[...].astype(bf16)
        scan_moves(k, True, lambda copy: copy.start())
        stop = n if k == len(spans) - 1 or 5 + k >= len(cuts) else cuts[5 + k]
        lax.fori_loop(cuts[4 + k] if 4 + k < len(cuts) else n, stop, start_q, 0)
        scan_moves(k, False, lambda copy: copy.wait_recv())
        for j in range(1, 4):
            if j * span < n:
                got = jnp.where(me >= j * span, rx[3 * k + j - 1].astype(f32), 0.0)
                acc[0] = acc[0] + jnp.exp(-rate[...] * float(tok * (j * span - 1))) * got
                if k < len(spans) - 1:
                    own[...] = own[...] + jnp.exp(-rate[...] * float(tok * j * span)) * got

    def carry_tile(c, _):
        cols = pl.ds(pl.multiple_of(c * LANES, LANES), LANES)
        dec = [spread(decay, k, cols) for k in range(poles)]
        start = []
        for k in range(poles):
            r = rate[k : k + 1, cols]
            x = jnp.where(sub == 0, acc[0, k : k + 1, cols], pltpu.roll(state[k, :, cols], 1, 0))
            for by in (1, 2, 4):
                fade = jnp.exp(-r * float(steps * by))
                x = x + jnp.where(sub >= by, fade * pltpu.roll(x, by, 0), 0.0)
            start.append(resid[k : k + 1, cols] * x)

        def step(i, g):
            at = pl.ds(pl.multiple_of(i * ROWS, ROWS), ROWS)
            g = tuple(d * s for d, s in zip(dec, g))
            filt[at, cols] = filt[at, cols] + total(list(g))
            return g

        lax.fori_loop(0, steps, step, tuple(start), unroll=2)
        return _

    lax.fori_loop(0, ch // LANES, carry_tile, 0)

    own_q.wait()
    lax.fori_loop(1, n, recv_q_wait, 0)
    lax.fori_loop(0, ch // tile, rim_q_tile, 0)
    rim_q = rim_copy(rim_q_out, rim_q_in, 1, after)
    rim_q.start()

    def query_tile(c, _):
        at = c * tile
        prod[:, pl.ds(pl.multiple_of(at, LANES), tile)] = featured(arr_q, at, at, None, at)
        return _

    lax.fori_loop(0, ch // tile, query_tile, 0)
    rim_copy(rim_q_out, rim_q_in, 1, before).wait_recv()
    edge = rim_q_in[...].astype(f32)
    w1, w2 = convw[1:2, 0:ch], convw[2:3, 0:ch]
    prod[0:ROWS, :] = prod[0:ROWS, :] + jnp.where(first, w1 * edge[1:2] + w2 * edge[0:1], 0.0)
    prod[ROWS : 2 * ROWS, :] = prod[ROWS : 2 * ROWS, :] + jnp.where(first, w2 * edge[1:2], 0.0)

    nat = lax.broadcasted_iota(jnp.int32, (tok, 1), 0)
    seat = lax.bitwise_and(nat, steps - 1) * ROWS + lax.shift_right_logical(nat, steps.bit_length() - 1)
    order = (seat == lax.broadcasted_iota(jnp.int32, (tok, tok), 1)).astype(f32).astype(bf16)

    def gate_tile(c, _):
        cols = pl.ds(pl.multiple_of(c * tile, LANES), tile)
        rows_g = (prod[:, cols] * filt[:, cols]).astype(bf16)
        natural[:, cols] = jnp.dot(order, rows_g, preferred_element_type=f32).astype(bf16)
        return _

    lax.fori_loop(0, ch // tile, gate_tile, 0)
    w_copy.wait()

    def out_tile(c, _):
        cols = pl.ds(pl.multiple_of(c * tile, LANES), tile)
        out[:, cols] = jnp.dot(natural[...], w_vmem[:, cols], preferred_element_type=f32).astype(bf16)
        return _

    lax.fori_loop(0, ch // tile, out_tile, 0)

    lax.fori_loop(1, n, send_waits, 0)
    rim_kv.wait_send()
    rim_q.wait_send()
    for k in range(len(spans)):
        scan_moves(k, True, lambda copy: copy.wait_send())


def swift(
    n, groups, cap, base, tok,
    counts, feats_hbm, pos, convw, rate, resid, skip, w_hbm, out, most,
    box_a, box_b, box_q, arr_a, arr_b, arr_q, mark_out, mark_in, group_out, group_in,
    hot_s, place_s, prod, filt, gated, natural, state,
    feats, decay, rims_out, rims_in, own, acc, totals, rate4, tx, rx, w_vmem,
    sends, recvs, over_sends, over_recvs, send_m, recv_m, send_g, recv_g, raw, ending, inward, hops, leaps,
    rim_sems, scan_send, scan_recv, self_sems, w_sem, f_sems,
):
    me = lax.axis_index("ctx")
    group = lax.axis_index("groups")
    slots, feat = feats_hbm.shape
    ch = feat // 3
    poles = rate.shape[0]
    steps = tok // ROWS
    tile = col_tile(ch)
    rows = n * cap
    over = cap - base
    half_n = n // 2
    tiles = ch // tile
    lead = (tiles + 1) // 2
    parts = [(0, lead), (lead, tiles)]
    barrier = pltpu.get_barrier_semaphore()
    bits = (n - 1).bit_length()

    def flip(a, m):
        return sum(((a // (1 << b) + m // (1 << b)) % 2) * (1 << b) for b in range(bits))

    def greet(m, c):
        pl.semaphore_signal(barrier, inc=1, device_id={"ctx": flip(me, m)}, device_id_type=MESH)
        return c

    lax.fori_loop(1, n, greet, 0)
    for g in range(1, groups):
        pl.semaphore_signal(barrier, inc=1, device_id={"groups": lax.rem(group + g, groups)}, device_id_type=MESH)
    kv_cols = pl.ds(ch, 2 * ch)
    f_kv = pltpu.make_async_copy(feats_hbm.at[:, kv_cols], feats.at[:, kv_cols], f_sems.at[0])
    f_q = pltpu.make_async_copy(feats_hbm.at[:, pl.ds(0, ch)], feats.at[:, pl.ds(0, ch)], f_sems.at[1])
    f_kv.start()
    f_q.start()
    w_copy = pltpu.make_async_copy(w_hbm, w_vmem, w_sem)
    w_copy.start()

    p = pos[...].reshape(1, slots)
    shift = tok.bit_length() - 1
    live = lax.broadcasted_iota(jnp.int32, (1, slots), 1) < counts[0]
    owner = jnp.where(live, lax.shift_right_logical(p, shift), -1)
    local = lax.bitwise_and(p, tok - 1).astype(f32)
    mine = owner == lax.broadcasted_iota(jnp.int32, (n, slots), 0)
    tri = lax.broadcasted_iota(jnp.int32, (slots, slots), 0) <= lax.broadcasted_iota(
        jnp.int32, (slots, slots), 1
    )
    tri = tri.astype(f32).astype(bf16)
    cum = jnp.dot(mine.astype(f32).astype(bf16), tri, preferred_element_type=f32)
    rank = jnp.sum(jnp.where(mine, cum, 0.0), axis=0, keepdims=True) - 1.0
    direct = jnp.logical_and(live, rank < float(base))
    beyond = jnp.logical_and(live, rank >= float(base)).astype(f32)
    bump = jnp.dot(jnp.broadcast_to(beyond, (16, slots)).astype(bf16), tri, preferred_element_type=f32)[0:1]
    late = jnp.where(beyond > 0.0, bump - 1.0, -1.0)
    apart = lax.bitwise_xor(owner, me)
    flat = jnp.where(direct, apart.astype(f32) * float(cap) + rank, -1.0)
    spare = jnp.where(late >= 0.0, late + float(base), -1.0)
    hot_row = lax.broadcasted_iota(jnp.int32, (rows, slots), 0)
    hit = jnp.logical_or(hot_row.astype(f32) == flat, lax.bitwise_and(hot_row, cap - 1).astype(f32) == spare)
    hot_s[...] = hit.astype(f32).astype(bf16)

    def pack_rows(box, first, count, source):
        def pack(c, _):
            at = pl.ds(first, rows // 2)
            src = pl.ds(pl.multiple_of(source(c), LANES), tile)
            dst = pl.ds(pl.multiple_of(c * tile, LANES), tile)
            box[at, dst] = jnp.dot(hot_s[at, :], feats[:, src], preferred_element_type=f32).astype(bf16)
            return _

        lax.fori_loop(0, count, pack, 0)

    def pack_kv(i, first):
        t0, t1 = parts[i]
        count = t1 - t0
        pack_rows(boxes[i], first, 2 * count, lambda c: ch + (c // count) * ch + (t0 + c % count) * tile)

    boxes = (box_a, box_b, box_q)
    arrs = (arr_a, arr_b, arr_q)

    def slab(ref, k, size):
        return ref.at[pl.ds(pl.multiple_of(k * cap, cap), size), :]

    def over_rows(ref, k):
        return ref.at[pl.ds(pl.multiple_of(k * cap + base, ROWS), over), :]

    def direct_copy(which, m, size, came):
        box, arr, send, recv = boxes[which], arrs[which], sends.at[which], recvs.at[which]
        to = flip(me, m)
        return pltpu.make_async_remote_copy(
            src_ref=slab(box, m, size), dst_ref=slab(arr, to if came else me, size), send_sem=send.at[m],
            recv_sem=recv.at[m], device_id={"ctx": to}, device_id_type=MESH,
        )

    def to_mirror(which, came):
        box, arr, send, recv = boxes[which], arrs[which], over_sends.at[which], over_recvs.at[which]
        to = flip(me, half_n)
        return pltpu.make_async_remote_copy(
            src_ref=over_rows(box, half_n), dst_ref=over_rows(arr, to if came else me), send_sem=send.at[0],
            recv_sem=recv.at[0], device_id={"ctx": to}, device_id_type=MESH,
        )

    def forward(which, m, came):
        arr, send, recv = arrs[which], over_sends.at[which], over_recvs.at[which]
        to = flip(me, m)
        rows_of = over_rows(arr, flip(to if came else me, half_n))
        return pltpu.make_async_remote_copy(
            src_ref=rows_of, dst_ref=rows_of, send_sem=send.at[m], recv_sem=recv.at[m],
            device_id={"ctx": to}, device_id_type=MESH,
        )

    in_a, in_b, in_q = 0, 1, 2

    def each(first, last, make, act):
        def one(m, c):
            act(make(m))
            return c

        lax.fori_loop(first, last, one, 0)

    def start(copy):
        copy.start()

    def arrive(copy):
        copy.wait_recv()

    def sent(copy):
        copy.wait_send()

    def near(which, came=False):
        return lambda m: direct_copy(which, m, cap, came)

    def far(which, came=False):
        return lambda m: direct_copy(which, m, base, came)

    def spread_over(which, came=False):
        return lambda m: forward(which, m, came)

    def marks_to(m, to, came):
        return pltpu.make_async_remote_copy(
            src_ref=mark_out.at[to], dst_ref=mark_in.at[came], send_sem=send_m.at[m], recv_sem=recv_m.at[m],
            device_id={"ctx": to}, device_id_type=MESH,
        )

    def start_marks(m, c):
        marks_to(m, flip(me, m), me).start()
        return c

    def recv_marks(m, c):
        marks_to(m, flip(me, m), flip(me, m)).wait_recv()
        return c

    def own_copy(i):
        return pltpu.make_async_copy(slab(boxes[i], 0, cap), slab(arrs[i], me, cap), self_sems.at[i])

    f_kv.wait()
    pack_kv(in_a, rows // 2)
    pl.semaphore_wait(barrier, n - 1 + groups - 1)
    to_mirror(in_a, False).start()
    each(half_n, n, far(in_a), start)
    pack_kv(in_a, 0)
    each(1, half_n, near(in_a), start)
    own_copy(in_a).start()

    seats = (lax.broadcasted_iota(jnp.int32, (LANES, slots), 0) - lax.rem(me * cap, LANES)).astype(f32)
    in_slab = jnp.logical_and(seats >= 0.0, seats < float(cap))
    at_base = jnp.logical_and(direct, seats == rank)
    at_over = jnp.logical_and(in_slab, jnp.logical_and(late >= 0.0, seats - float(base) == late))
    last_dims = (((1,), (1,)), ((), ()))
    sub16 = lax.broadcasted_iota(jnp.int32, (16, slots), 0)
    two = jnp.where(sub16 == 0, local + 1.0, jnp.where(sub16 == 1, owner.astype(f32), 0.0)).astype(bf16)
    tell = lax.dot_general(
        jnp.where(mine, local + 1.0, 0.0).astype(bf16), at_base.astype(f32).astype(bf16), last_dims,
        preferred_element_type=f32,
    )
    tell = jnp.where(tell > 0.0, tell + (lax.broadcasted_iota(jnp.int32, (n, LANES), 0) * tok).astype(f32), 0.0)
    extra = lax.dot_general(two, at_over.astype(f32).astype(bf16), last_dims, preferred_element_type=f32)
    tell = tell + (extra[0:1] + extra[1:2] * float(tok))
    held = jnp.broadcast_to(jnp.sum(beyond, axis=1, keepdims=True), (1, LANES))
    for k in range(n):
        mark_out[k, 0:1, :] = tell[k : k + 1, :]
        mark_out[k, 1:2, :] = held
    mark_in[me] = mark_out[me]
    lax.fori_loop(1, n, start_marks, 0)

    pack_kv(in_b, rows // 2)
    to_mirror(in_b, False).start()
    to_mirror(in_a, True).wait_recv()
    each(1, half_n, spread_over(in_a), start)
    cuts = [half_n]
    for share in FLOW:
        cuts.append(min(n, cuts[-1] + share * half_n // 8))
    early = EARLY * half_n // 8
    each(half_n, half_n + early, far(in_b), start)
    pack_kv(in_b, 0)
    own_copy(in_b).start()
    f_q.wait()
    pack_rows(box_q, rows // 2, tiles, lambda c: c * tile)
    to_mirror(in_q, False).start()
    pack_rows(box_q, 0, tiles, lambda c: c * tile)
    own_copy(in_q).start()
    to_mirror(in_b, True).wait_recv()
    each(1, half_n, spread_over(in_b), start)
    decay[...] = jnp.exp(-rate[...])
    sub = lax.broadcasted_iota(jnp.int32, (ROWS, 1), 0)
    first = jnp.logical_and(sub == 0, me > 0)
    later = ((ROWS - 1 - sub) * steps).astype(f32)
    segment = (sub * steps).astype(f32)
    member, level = me % QUAD, me // QUAD
    levels = n // QUAD
    share = poles // QUAD
    for q in range(QUAD):
        rate4[q] = rate[q * share : (q + 1) * share, :]
    lags = [1, 2, 3] + [QUAD * j for j in range(1, levels - 1)]
    for at, lag in enumerate(lags):
        leaps[at] = jnp.exp(-rate4[member] * float(tok * lag))
    for at, by in enumerate((1, 2, 4)):
        hops[at] = jnp.exp(-rate[...] * float(steps * by))

    def fades_of(k, _):
        r = rate[pl.ds(k, 1), :]
        ending[k] = jnp.exp(-r * later)
        inward[k] = resid[pl.ds(k, 1), :] * jnp.exp(-r * segment)
        return _

    lax.fori_loop(0, poles, fades_of, 0)

    lax.fori_loop(1, n, recv_marks, 0)
    lanes_of = [
        sum(mark_in[k, 0:1, :] for k in range(g * (LANES // cap), (g + 1) * (LANES // cap)))
        for g in range(rows // LANES)
    ]
    came_pos = jnp.concatenate(lanes_of, axis=1) - 1.0
    worst = mark_in[0, 1:2, :]
    for k in range(1, n):
        worst = jnp.maximum(worst, mark_in[k, 1:2, :])
    group_out[...] = jnp.broadcast_to(worst, (ROWS, LANES))

    def group_copy(g, to):
        return pltpu.make_async_remote_copy(
            src_ref=group_out, dst_ref=group_in.at[g], send_sem=send_g.at[g], recv_sem=recv_g.at[g],
            device_id={"groups": to}, device_id_type=MESH,
        )

    for g in range(1, groups):
        group_copy(g, lax.rem(group + g, groups)).start()

    ext = tok + 2 * ROWS
    row = lax.broadcasted_iota(jnp.int32, (ext, 1), 0)
    want = lax.bitwise_and(row, ROWS - 1) * steps + lax.shift_right_logical(row, 3) - 2
    want = jnp.where(want < 0, -100, want + me * tok).astype(f32)
    place_s[...] = (want == came_pos).astype(f32).astype(bf16)
    rim_row = lax.broadcasted_iota(jnp.int32, (16, 1), 0)
    rim_want = jnp.where(rim_row < 2, rim_row + me * tok + tok - 2, -100).astype(f32)
    rim_hot = (rim_want == came_pos).astype(f32).astype(bf16)

    to_mirror(in_q, True).wait_recv()
    each(1, half_n, spread_over(in_q), start)

    def take_then_send(which, then, ahead, first_sent):
        each(half_n, n - ahead, far(which, True), arrive)

        def both(m, c):
            far(which, True)(m).wait_recv()
            far(then)(m - n + ahead + first_sent).start()
            return c

        lax.fori_loop(n - ahead, n, both, 0)

    own_copy(in_a).wait()
    each(1, half_n, near(in_a, True), arrive)
    each(1, half_n, near(in_b), start)
    each(1, half_n, spread_over(in_a, True), arrive)
    take_then_send(in_a, in_b, half_n - early, half_n + early)

    def rim_copy(i, to):
        wide = (2 * (parts[i][1] - parts[i][0]) if i < len(parts) else tiles) * tile
        cols = pl.ds((2 * parts[i][0] if i < len(parts) else 2 * tiles) * tile, wide)
        return pltpu.make_async_remote_copy(
            src_ref=rims_out.at[:, cols], dst_ref=rims_in.at[:, cols], send_sem=rim_sems.at[2 * i],
            recv_sem=rim_sems.at[2 * i + 1], device_id={"ctx": to}, device_id_type=MESH,
        )

    after, before = lax.rem(me + 1, n), lax.rem(me + n - 1, n)

    def rim_send(i):
        count = 2 * (parts[i][1] - parts[i][0]) if i < len(parts) else tiles
        base_tile = 2 * parts[i][0] if i < len(parts) else 2 * tiles

        def fill(c, _):
            src = pl.ds(pl.multiple_of(c * tile, LANES), tile)
            dst = pl.ds(pl.multiple_of((base_tile + c) * tile, LANES), tile)
            rims_out[:, dst] = jnp.dot(rim_hot, arrs[i][:, src], preferred_element_type=f32)[0:ROWS].astype(bf16)
            return _

        lax.fori_loop(0, count, fill, 0)
        rim_copy(i, after).start()

    def featured(arr, at, w_at):
        x = jnp.dot(place_s[...], arr[:, pl.ds(pl.multiple_of(at, LANES), tile)], preferred_element_type=f32)
        w = convw[:, pl.ds(pl.multiple_of(w_at, LANES), tile)]
        return w[0:1] * x[2 * ROWS :] + w[1:2] * x[ROWS : ROWS + tok] + w[2:3] * x[:tok]

    def product(i):
        t0, t1 = parts[i]
        wide = (t1 - t0) * tile

        def product_tile(c, _):
            at = (c - t0) * tile
            k = featured(arrs[i], at, ch + c * tile)
            v = featured(arrs[i], wide + at, 2 * ch + c * tile)
            raw[:, pl.ds(pl.multiple_of(c * tile, LANES), tile)] = k[: 2 * ROWS]
            raw[:, pl.ds(pl.multiple_of(ch + c * tile, LANES), tile)] = v[: 2 * ROWS]
            prod[:, pl.ds(pl.multiple_of(c * tile, LANES), tile)] = k * v
            return _

        lax.fori_loop(t0, t1, product_tile, 0)

    def product_edges(i):
        t0, t1 = parts[i]
        wide = (t1 - t0) * tile
        rim_copy(i, before).wait_recv()

        def edge_tile(c, _):
            def with_edge(at, rim_at):
                cols = pl.ds(pl.multiple_of(at, LANES), tile)
                w = convw[:, pl.ds(pl.multiple_of(ch + at, LANES), tile)]
                edge = rims_in[:, pl.ds(pl.multiple_of(rim_at, LANES), tile)].astype(f32)
                top = jnp.where(first, w[1:2] * edge[1:2] + w[2:3] * edge[0:1], 0.0)
                nxt = jnp.where(first, w[2:3] * edge[1:2], 0.0)
                return jnp.concatenate([raw[0:ROWS, cols] + top, raw[ROWS:, cols] + nxt], axis=0)

            rim_at = (2 * t0 + c - t0) * tile
            prod[0 : 2 * ROWS, pl.ds(pl.multiple_of(c * tile, LANES), tile)] = with_edge(
                c * tile, rim_at
            ) * with_edge(ch + c * tile, rim_at + wide)
            return _

        lax.fori_loop(t0, t1, edge_tile, 0)

    def spread(ref, k, cols):
        return jnp.broadcast_to(ref[k : k + 1, cols], (ROWS, LANES))

    def total(terms):
        while len(terms) > 1:
            terms = [a + b for a, b in zip(terms[::2], terms[1::2])] + terms[len(terms) // 2 * 2 :]
        return terms[0]

    def local_tile(c, _):
        cols = pl.ds(pl.multiple_of(c * LANES, LANES), LANES)
        dec = [spread(decay, k, cols) for k in range(poles)]
        res = [spread(resid, k, cols) for k in range(poles)]
        gain = jnp.broadcast_to(skip[pl.ds(pl.multiple_of(c * LANES, LANES), LANES)].reshape(1, LANES), (ROWS, LANES))

        def step(i, st):
            at = pl.ds(pl.multiple_of(i * ROWS, ROWS), ROWS)
            x = prod[at, cols]
            st = tuple(d * s + x for d, s in zip(dec, st))
            filt[at, cols] = gain * x + total([r * s for r, s in zip(res, st)])
            return st

        zero = jnp.zeros((ROWS, LANES), f32)
        st = lax.fori_loop(0, steps, step, (zero,) * poles, unroll=4)
        for k in range(poles):
            state[k, :, cols] = st[k]
            own[k : k + 1, cols] = jnp.sum(ending[k, :, cols] * st[k], axis=0, keepdims=True)
        return _

    def prefix_tile(c, _):
        cols = pl.ds(pl.multiple_of(c * LANES, LANES), LANES)
        for k in range(poles):
            x = jnp.where(sub == 0, 0.0, pltpu.roll(state[k, :, cols], 1, 0))
            for at, by in enumerate((1, 2, 4)):
                x = x + jnp.where(sub >= by, hops[at, k : k + 1, cols] * pltpu.roll(x, by, 0), 0.0)
            state[k, :, cols] = resid[k : k + 1, cols] * x
        return _

    per = tile // LANES

    def lanes(part):
        return pl.ds(part[0] * tile, (part[1] - part[0]) * tile)

    def scan_copy(part, stage, j, out_way):
        cols = lanes(part)
        here = member if stage != 1 else level
        count = QUAD if stage != 1 else levels
        peer = lax.rem(here + (j if out_way else count - j), count)
        to = level * QUAD + peer if stage != 1 else peer * QUAD + member
        start_at = stage * max(QUAD, levels)
        source, slot = (totals.at[0, :, cols], start_at + here) if stage == 1 else (
            tx.at[stage // 2 * QUAD + peer, :, cols], start_at + here)
        if not out_way:
            slot = start_at + peer
        at = (start_at + j) * len(parts) + parts.index(part)
        return pltpu.make_async_remote_copy(
            src_ref=source, dst_ref=rx.at[slot, :, cols], send_sem=scan_send.at[at],
            recv_sem=scan_recv.at[at], device_id={"ctx": to}, device_id_type=MESH,
        )

    def scan_moves(part, stage, out_way, act):
        for j in range(1, QUAD if stage != 1 else levels):
            act(scan_copy(part, stage, j, out_way))

    def leap(lag, cols):
        return leaps[lags.index(lag), :, cols]

    def scan_open(part):
        cols = lanes(part)
        for q in range(QUAD):
            tx[q, :, cols] = own[q * share : (q + 1) * share, cols]
        rx[member, :, cols] = tx[member, :, cols]
        scan_moves(part, 0, True, start)

    def scan_totals(part):
        cols = lanes(part)
        scan_moves(part, 0, False, arrive)
        t = rx[QUAD - 1, :, cols]
        for i in range(QUAD - 1):
            t = t + leap(QUAD - 1 - i, cols) * rx[i, :, cols]
        totals[0, :, cols] = t
        scan_moves(part, 1, True, start)

    def scan_carries(part):
        cols = lanes(part)
        scan_moves(part, 1, False, arrive)
        carried = jnp.zeros((share, (part[1] - part[0]) * tile), f32)
        for j in range(1, levels):
            got = rx[max(QUAD, levels) + lax.rem(level + levels - j, levels), :, cols]
            got = got if j == 1 else leap(QUAD * (j - 1), cols) * got
            carried = carried + jnp.where(level >= j, got, 0.0)
        for i in range(QUAD):
            tx[QUAD + i, :, cols] = carried
            carried = rx[i, :, cols] + leap(1, cols) * carried
        rx[2 * max(QUAD, levels) + member, :, cols] = tx[QUAD + member, :, cols]
        scan_moves(part, 2, True, start)

    def scan_close(part):
        cols = lanes(part)
        scan_moves(part, 2, False, arrive)
        for q in range(QUAD):
            acc[q * share : (q + 1) * share, cols] = rx[2 * max(QUAD, levels) + q, :, cols]


    def local(part):
        lax.fori_loop(part[0] * per, part[1] * per, local_tile, 0)

    def prefix(part):
        lax.fori_loop(part[0] * per, part[1] * per, prefix_tile, 0)

    part_a, part_b = parts
    def carry_tile(c, _):
        cols = pl.ds(pl.multiple_of(c * LANES, LANES), LANES)
        dec = [spread(decay, k, cols) for k in range(poles)]
        begin = tuple(
            state[k, :, cols] + inward[k, :, cols] * acc[k : k + 1, cols] for k in range(poles)
        )

        def step(i, g):
            at = pl.ds(pl.multiple_of(i * ROWS, ROWS), ROWS)
            g = tuple(d * s for d, s in zip(dec, g))
            filt[at, cols] = filt[at, cols] + total(list(g))
            return g

        lax.fori_loop(0, steps, step, begin, unroll=4)
        return _

    def carry(part):
        scan_close(part)
        lax.fori_loop(part[0] * per, part[1] * per, carry_tile, 0)

    rim_send(in_a)
    product(in_a)
    product_edges(in_a)
    local(part_a)
    scan_open(part_a)
    prefix(part_a)
    own_copy(in_b).wait()
    each(1, half_n, near(in_b, True), arrive)
    each(1, half_n, near(in_q), start)
    each(half_n, cuts[1], far(in_q), start)
    each(1, half_n, spread_over(in_b, True), arrive)
    take_then_send(in_b, in_q, cuts[2] - cuts[1], cuts[1])
    rim_send(in_b)
    scan_totals(part_a)
    product(in_b)
    each(cuts[2], cuts[3], far(in_q), start)
    product_edges(in_b)
    local(part_b)
    scan_open(part_b)
    each(cuts[3], cuts[4], far(in_q), start)
    prefix(part_b)
    scan_carries(part_a)
    scan_totals(part_b)
    each(cuts[4], n, far(in_q), start)
    carry(part_a)
    scan_carries(part_b)
    carry(part_b)
    top_of = worst
    for g in range(1, groups):
        group_copy(g, lax.rem(group + groups - g, groups)).wait_recv()
        top_of = jnp.maximum(top_of, group_in[g, 0:1, :])
    most[0] = jnp.max(top_of).astype(jnp.int32)
    w_copy.wait()

    own_copy(in_q).wait()
    each(1, half_n, near(in_q, True), arrive)
    each(1, half_n, spread_over(in_q, True), arrive)
    each(half_n, n, far(in_q, True), arrive)
    rim_send(in_q)

    def gate_tile(c, _):
        at = c * tile
        cols = pl.ds(pl.multiple_of(at, LANES), tile)
        y = featured(arr_q, at, at)
        raw[:, cols] = y[: 2 * ROWS]
        gated[:, cols] = (y * filt[:, cols]).astype(bf16)
        return _

    lax.fori_loop(0, ch // tile, gate_tile, 0)
    rim_copy(in_q, before).wait_recv()
    edge = rims_in[:, 2 * ch :].astype(f32)
    w1, w2 = convw[1:2, 0:ch], convw[2:3, 0:ch]
    top = jnp.where(first, w1 * edge[1:2] + w2 * edge[0:1], 0.0)
    nxt = jnp.where(first, w2 * edge[1:2], 0.0)
    begun = raw[:, 0:ch] + jnp.concatenate([top, nxt], axis=0)
    gated[0 : 2 * ROWS, :] = (begun * filt[0 : 2 * ROWS, :]).astype(bf16)

    nat = lax.broadcasted_iota(jnp.int32, (tok, 1), 0)
    seat = lax.bitwise_and(nat, steps - 1) * ROWS + lax.shift_right_logical(nat, steps.bit_length() - 1)
    order = (seat == lax.broadcasted_iota(jnp.int32, (tok, tok), 1)).astype(f32).astype(bf16)

    def order_tile(c, _):
        cols = pl.ds(pl.multiple_of(c * tile, LANES), tile)
        natural[:, cols] = jnp.dot(order, gated[:, cols], preferred_element_type=f32).astype(bf16)
        return _

    lax.fori_loop(0, ch // tile, order_tile, 0)

    wide = 640 if ch % 640 == 0 else tile

    def out_tile(c, _):
        cols = pl.ds(pl.multiple_of(c * wide, LANES), wide)
        out[:, cols] = jnp.dot(natural[...], w_vmem[:, cols], preferred_element_type=f32).astype(bf16)
        return _

    lax.fori_loop(0, ch // wide, out_tile, 0)

    for which in (in_a, in_b, in_q):
        each(1, half_n, near(which), sent)
        each(half_n, n, far(which), sent)
    for which in (in_a, in_b, in_q):
        to_mirror(which, False).wait_send()
        each(1, half_n, spread_over(which), sent)
    each(1, n, lambda m: marks_to(m, flip(me, m), me), sent)
    for g in range(1, groups):
        group_copy(g, lax.rem(group + g, groups)).wait_send()
    for which in (in_a, in_b, in_q):
        rim_copy(which, after).wait_send()
    for stage in range(3):
        for part in parts:
            scan_moves(part, stage, True, sent)


def swift_call(n, groups, cap, base, tok, args):
    counts, features, positions, conv_weight, pole_rate, pole_residue, skip_gain, out_weight = args
    slots, feat = features.shape
    ch = feat // 3
    poles = pole_rate.shape[0]
    rows = n * cap
    share = poles // QUAD
    wide = max(QUAD, n // QUAD)
    lead = (ch // col_tile(ch) + 1) // 2 * col_tile(ch)
    whole = pl.BlockSpec(memory_space=pltpu.VMEM)
    dma = pltpu.SemaphoreType.DMA
    vmem = pltpu.VMEM
    return pl.pallas_call(
        functools.partial(swift, n, groups, cap, base, tok),
        out_shape=(jax.ShapeDtypeStruct((tok, ch), bf16), jax.ShapeDtypeStruct((1,), jnp.int32)),
        in_specs=[pl.BlockSpec(memory_space=pltpu.SMEM), pl.BlockSpec(memory_space=pl.ANY)]
        + [whole] * 5 + [pl.BlockSpec(memory_space=pl.ANY)],
        out_specs=(whole, pl.BlockSpec(memory_space=pltpu.SMEM)),
        scratch_shapes=[
            vmem((rows, 2 * lead), bf16),
            vmem((rows, 2 * (ch - lead)), bf16),
            vmem((rows, ch), bf16),
            vmem((rows, 2 * lead), bf16),
            vmem((rows, 2 * (ch - lead)), bf16),
            vmem((rows, ch), bf16),
            vmem((n, 2, LANES), f32),
            vmem((n, 2, LANES), f32),
            vmem((ROWS, LANES), f32),
            vmem((groups, ROWS, LANES), f32),
            vmem((rows, slots), bf16),
            vmem((tok + 2 * ROWS, rows), bf16),
            vmem((tok, ch), f32),
            vmem((tok, ch), f32),
            vmem((tok, ch), bf16),
            vmem((tok, ch), bf16),
            vmem((poles, ROWS, ch), f32),
            vmem((slots, feat), bf16),
            vmem((poles, ch), f32),
            vmem((ROWS, feat), bf16),
            vmem((ROWS, feat), bf16),
            vmem((poles, ch), f32),
            vmem((poles, ch), f32),
            vmem((1, share, ch), f32),
            vmem((QUAD, share, ch), f32),
            vmem((2 * QUAD, share, ch), f32),
            vmem((3 * wide, share, ch), f32),
            vmem(out_weight.shape, bf16),
            dma((3, n)), dma((3, n)), dma((3, n)), dma((3, n)), dma((n,)), dma((n,)), dma((groups,)), dma((groups,)),
            vmem((2 * ROWS, 2 * ch), f32),
            vmem((poles, ROWS, ch), f32),
            vmem((poles, ROWS, ch), f32),
            vmem((3, poles, ch), f32),
            vmem((2 + n // QUAD, share, ch), f32),
            dma((6,)), dma((6 * wide,)), dma((6 * wide,)), dma((3,)), dma, dma((2,)),
        ],
        compiler_params=pltpu.CompilerParams(
            collective_id=1, has_side_effects=True, vmem_limit_bytes=60 << 20
        ),
        name="hyena_direct",
    )(*args)


def mega_call(n, cap, tok, args):
    counts, features, positions, conv_weight, pole_rate, pole_residue, skip_gain, out_weight = args
    slots, feat = features.shape
    ch = feat // 3
    poles = pole_rate.shape[0]
    rows = n * cap
    stages = len(scan_spans(n))
    whole = pl.BlockSpec(memory_space=pltpu.VMEM)
    dma = pltpu.SemaphoreType.DMA
    return pl.pallas_call(
        functools.partial(mega, n, cap, tok, PACE[0] * (n - 1) // 15),
        out_shape=jax.ShapeDtypeStruct((tok, ch), bf16),
        in_specs=[pl.BlockSpec(memory_space=pltpu.SMEM), pl.BlockSpec(memory_space=pl.ANY)]
        + [whole] * 5 + [pl.BlockSpec(memory_space=pl.ANY)],
        out_specs=whole,
        scratch_shapes=[
            pltpu.VMEM((rows, 2 * ch + LANES), bf16),
            pltpu.VMEM((rows, ch), bf16),
            pltpu.VMEM((rows, 2 * ch + LANES), bf16),
            pltpu.VMEM((rows, ch), bf16),
            pltpu.VMEM((rows, slots), bf16),
            pltpu.VMEM((tok + 2 * ROWS, rows), bf16),
            pltpu.VMEM((tok, ch), f32),
            pltpu.VMEM((tok, ch), f32),
            pltpu.VMEM((16, LANES), bf16),
            pltpu.VMEM((tok, ch), bf16),
            pltpu.VMEM((poles, ROWS, ch), f32),
            pltpu.VMEM((slots, feat), bf16),
            pltpu.VMEM((poles, ch), f32),
            pltpu.VMEM((16, 2 * ch), bf16),
            pltpu.VMEM((16, 2 * ch), bf16),
            pltpu.VMEM((16, ch), bf16),
            pltpu.VMEM((16, ch), bf16),
            pltpu.VMEM((poles, ch), f32),
            pltpu.VMEM((1, poles, ch), f32),
            pltpu.VMEM((stages, poles, ch), bf16),
            pltpu.VMEM((3 * stages, poles, ch), bf16),
            pltpu.VMEM(out_weight.shape, bf16),
            dma((n,)), dma((n,)), dma((n,)), dma((n,)), dma((4,)), dma((3 * stages,)), dma((3 * stages,)),
            dma((2,)), dma, dma((2,)),
        ],
        compiler_params=pltpu.CompilerParams(
            collective_id=0, has_side_effects=True, vmem_limit_bytes=60 << 20
        ),
        name="hyena",
    )(*args)


def on_device(
    features, positions, counts, conv_weight, pole_rate, pole_residue, skip_gain, out_weight
):
    n = lax.axis_size("ctx")
    groups = lax.axis_size("groups")
    slots, feat = features.shape
    ch = feat // 3
    tok = 2 * slots // 3
    cap = 2 * tok // n
    poles = pole_rate.shape[0]
    if cap % 16 or tok & (tok - 1) or tok > 256 or conv_weight.shape[0] != 3 or ch % LANES or n & (n - 1) or n < 4:
        return plain_on_device(
            features, positions, counts, conv_weight, pole_rate, pole_residue, skip_gain, out_weight
        )
    args = (counts, features, positions, conv_weight, pole_rate, pole_residue, skip_gain, out_weight)
    base = slots // n
    if poles % QUAD or base % ROWS or cap - base > 16 or LANES % cap:
        return mega_call(n, cap, tok, args)
    done, most = swift_call(n, groups, cap, base, tok, args)
    return lax.cond(most[0] > cap - base, lambda d: mega_call(n, cap, tok, args), lambda d: d, done)


PACE = (2, 1, 1, 2, 2)
FLOW = (0, 2, 1, 1)
EARLY = 0
QUAD = 4


def solution(mesh):
    return jax.shard_map(
        on_device,
        mesh=mesh,
        in_specs=(
            P(("groups", "ctx"), None),
            P(("groups", "ctx")),
            P(("groups", "ctx")),
            P(),
            P(),
            P(),
            P(),
            P(),
        ),
        out_specs=P(("groups", "ctx"), None),
        check_vma=False,
    )
```

```python
import functools

import jax
import jax.numpy as jnp
from jax import lax
from jax.experimental import pallas as pl
from jax.experimental.pallas import tpu as pltpu
from jax.sharding import PartitionSpec as P

LANES = 128
ROWS = 8
MESH = pl.DeviceIdType.MESH
f32, bf16 = jnp.float32, jnp.bfloat16

block_len = 32


def from_behind(array, axis, by):
    count = lax.axis_size(axis)
    pairs = [(i, i + by) for i in range(count) if 0 <= i + by < count]
    return lax.ppermute(array, axis, pairs)


def plain_on_device(
    features, positions, counts, conv_weight, pole_rate, pole_residue, skip_gain, out_weight
):
    devices = lax.axis_size("ctx")
    slot_count = features.shape[0]
    feat_width = features.shape[1]
    channels = feat_width // 3
    tok_rows = 2 * slot_count // 3
    pair_cap = 2 * tok_rows // devices
    taps = conv_weight.shape[0]
    poles = pole_rate.shape[0]
    slot_ids = jnp.arange(slot_count, dtype=jnp.int32)
    is_live = slot_ids < counts[0]
    owners = jnp.where(is_live, positions // tok_rows, devices)
    same = jnp.logical_and(owners[:, None] == owners[None, :], slot_ids[None, :] < slot_ids[:, None])
    within = jnp.sum(same.astype(jnp.int32), axis=1)
    flat_index = jnp.where(is_live, owners * pair_cap + within, devices * pair_cap)
    outbox = (
        jnp.zeros((devices * pair_cap + 1, feat_width), features.dtype)
        .at[flat_index]
        .set(features)[:-1]
    )
    local_pos = (
        jnp.full((devices * pair_cap + 1,), -1, jnp.int32)
        .at[flat_index]
        .set(positions % tok_rows)[:-1]
    )
    outbox = outbox.reshape(devices, pair_cap, feat_width)
    local_pos = local_pos.reshape(devices, pair_cap)
    arrived, arrived_pos = (
        lax.all_to_all(outbox, "ctx", split_axis=0, concat_axis=0, tiled=True),
        lax.all_to_all(local_pos, "ctx", split_axis=0, concat_axis=0, tiled=True),
    )
    target = jnp.where(arrived_pos >= 0, arrived_pos, tok_rows).reshape(-1)
    placed = (
        jnp.zeros((tok_rows + 1, feat_width), features.dtype)
        .at[target]
        .set(arrived.reshape(-1, feat_width))[:-1]
    )
    rim_rows = from_behind(placed[tok_rows - (taps - 1) :], "ctx", 1)
    extended = jnp.concatenate([rim_rows, placed], axis=0)
    featured = jnp.zeros((tok_rows, feat_width), jnp.float32)
    for tap in range(taps):
        start = taps - 1 - tap
        featured = featured + conv_weight[tap][None, :] * extended[start : start + tok_rows].astype(
            jnp.float32
        )
    query_feat = featured[:, :channels]
    product = featured[:, channels : 2 * channels] * featured[:, 2 * channels :]
    num_blocks = tok_rows // block_len
    lag_steps = jnp.arange(block_len + 1).astype(jnp.float32)
    powers = jnp.exp(-pole_rate[None] * lag_steps[:, None, None])
    filter_taps = jnp.sum(powers[:block_len] * pole_residue[None], axis=1)
    blocked = product.reshape(num_blocks, block_len, channels)
    padded_blk = jnp.pad(blocked, ((0, 0), (block_len - 1, 0), (0, 0)))
    inside = jnp.zeros((num_blocks, block_len, channels), jnp.float32)
    for lag in range(block_len):
        first = block_len - 1 - lag
        inside = inside + filter_taps[lag][None, None, :] * padded_blk[:, first : first + block_len]
    blk_sums = jnp.zeros((num_blocks, poles, channels), jnp.float32)
    for row in range(block_len):
        blk_sums = blk_sums + powers[block_len - 1 - row][None] * blocked[:, row][:, None, :]
    decay_blk = powers[block_len]

    def advance(running, block_sum):
        return (decay_blk * running + block_sum, running)

    local_end, starts = lax.scan(advance, jnp.zeros((poles, channels), jnp.float32), blk_sums)
    decay_dev = jnp.exp(-pole_rate * float(tok_rows))

    def relay_step(counter, incoming):
        return from_behind(decay_dev * incoming + local_end, "ctx", 1)

    carry_in = lax.fori_loop(0, devices - 1, relay_step, jnp.zeros_like(local_end))
    block_starts = (jnp.arange(num_blocks) * block_len).astype(jnp.float32)
    block_decay = jnp.exp(-pole_rate[None] * block_starts[:, None, None])
    incoming = starts + block_decay * carry_in[None]
    inward = pole_residue[None] * powers[1:]
    from_state = jnp.zeros((num_blocks, block_len, channels), jnp.float32)
    for pole in range(poles):
        from_state = from_state + inward[:, pole][None] * incoming[:, pole][:, None, :]
    convolved = (inside + from_state).reshape(tok_rows, channels)
    filtered = skip_gain[None, :] * product + convolved
    gated_rows = (query_feat * filtered).astype(jnp.bfloat16)
    return jnp.dot(gated_rows, out_weight, preferred_element_type=jnp.float32).astype(jnp.bfloat16)

def col_tile(width):
    for tile in (384, 256, 128):
        if width % tile == 0:
            return tile
    return width


def scan_spans(n):
    spans, span = [], 1
    while span < n:
        spans.append(span)
        span *= 4
    return spans


def mega(
    n, cap, tok, up_front,
    counts, feats_hbm, pos, convw, rate, resid, skip, w_hbm, out,
    box_kv, box_q, arr_kv, arr_q, hot_s, place_s, prod, filt, gated, natural, state,
    feats, decay, rim_kv_out, rim_kv_in, rim_q_out, rim_q_in, own, acc, tx, rx, w_vmem,
    send_kv, recv_kv, send_q, recv_q, rim_sems, scan_send, scan_recv, self_sems, w_sem, f_sems,
):
    me = lax.axis_index("ctx")
    slots, feat = feats_hbm.shape
    ch = feat // 3
    poles = rate.shape[0]
    steps = tok // ROWS
    tile = col_tile(ch)
    rows = n * cap
    barrier = pltpu.get_barrier_semaphore()

    bits = (n - 1).bit_length()

    def mask_of(d):
        return sum(((d // (1 << b)) % 2) * (1 << (bits - 1 - b)) for b in range(bits))

    def peer_of(d):
        m = mask_of(d)
        return sum(((me // (1 << b) + m // (1 << b)) % 2) * (1 << b) for b in range(bits))

    def greet(d, c):
        pl.semaphore_signal(barrier, inc=1, device_id={"ctx": peer_of(d)}, device_id_type=MESH)
        return c

    lax.fori_loop(1, n, greet, 0)
    kv_cols = pl.ds(ch, 2 * ch)
    f_kv = pltpu.make_async_copy(feats_hbm.at[:, kv_cols], feats.at[:, kv_cols], f_sems.at[0])
    f_q = pltpu.make_async_copy(feats_hbm.at[:, pl.ds(0, ch)], feats.at[:, pl.ds(0, ch)], f_sems.at[1])
    f_kv.start()
    f_q.start()
    w_copy = pltpu.make_async_copy(w_hbm, w_vmem, w_sem)
    w_copy.start()

    p = pos[...].reshape(1, slots)
    shift = tok.bit_length() - 1
    live = lax.broadcasted_iota(jnp.int32, (1, slots), 1) < counts[0]
    owner = jnp.where(live, lax.shift_right_logical(p, shift), -1)
    local = lax.bitwise_and(p, tok - 1).astype(f32)
    mine = owner == lax.broadcasted_iota(jnp.int32, (n, slots), 0)
    tri = lax.broadcasted_iota(jnp.int32, (slots, slots), 0) <= lax.broadcasted_iota(
        jnp.int32, (slots, slots), 1
    )
    cum = jnp.dot(mine.astype(f32).astype(bf16), tri.astype(f32).astype(bf16), preferred_element_type=f32)
    rank = jnp.sum(jnp.where(mine, cum, 0.0), axis=0, keepdims=True) - 1.0
    flat = owner.astype(f32) * float(cap) + rank
    hit = lax.broadcasted_iota(jnp.int32, (rows, slots), 0).astype(f32) == flat
    hot_s[...] = hit.astype(f32).astype(bf16)
    marks = jnp.sum(jnp.where(hit, local + 1.0, 0.0), axis=1, keepdims=True) - 1.0
    box_kv[:, 2 * ch :] = jnp.broadcast_to(marks, (rows, LANES)).astype(bf16)

    def pack_kv(c, _):
        src = pl.ds(pl.multiple_of(ch + c * tile, LANES), tile)
        dst = pl.ds(pl.multiple_of(c * tile, LANES), tile)
        box_kv[:, dst] = jnp.dot(hot_s[...], feats[:, src], preferred_element_type=f32).astype(bf16)
        return _

    def pack_q(c, _):
        dst = pl.ds(pl.multiple_of(c * tile, LANES), tile)
        box_q[:, dst] = jnp.dot(hot_s[...], feats[:, dst], preferred_element_type=f32).astype(bf16)
        return _

    f_kv.wait()
    lax.fori_loop(0, 2 * ch // tile, pack_kv, 0)

    def slab(ref, k):
        return ref.at[pl.ds(pl.multiple_of(k * cap, cap), cap), :]

    def outgoing(box, arr, send, recv, d):
        to = peer_of(d)
        return pltpu.make_async_remote_copy(
            src_ref=slab(box, to), dst_ref=slab(arr, me), send_sem=send.at[d], recv_sem=recv.at[d],
            device_id={"ctx": to}, device_id_type=MESH,
        )

    def incoming(box, arr, send, recv, d):
        came = peer_of(d)
        return pltpu.make_async_remote_copy(
            src_ref=slab(box, came), dst_ref=slab(arr, came), send_sem=send.at[d], recv_sem=recv.at[d],
            device_id={"ctx": came}, device_id_type=MESH,
        )

    def start_kv(d, c):
        outgoing(box_kv, arr_kv, send_kv, recv_kv, d).start()
        return c

    def start_q(d, c):
        outgoing(box_q, arr_q, send_q, recv_q, d).start()
        return c

    def recv_kv_wait(d, c):
        incoming(box_kv, arr_kv, send_kv, recv_kv, d).wait_recv()
        return c

    def recv_q_wait(d, c):
        incoming(box_q, arr_q, send_q, recv_q, d).wait_recv()
        return c

    def send_waits(d, c):
        outgoing(box_kv, arr_kv, send_kv, recv_kv, d).wait_send()
        outgoing(box_q, arr_q, send_q, recv_q, d).wait_send()
        return c

    pl.semaphore_wait(barrier, n - 1)
    lax.fori_loop(1, n, start_kv, 0)
    own_kv = pltpu.make_async_copy(slab(box_kv, me), slab(arr_kv, me), self_sems.at[0])
    own_kv.start()
    f_q.wait()
    lax.fori_loop(0, ch // tile, pack_q, 0)
    own_q = pltpu.make_async_copy(slab(box_q, me), slab(arr_q, me), self_sems.at[1])
    own_q.start()
    lax.fori_loop(1, 1 + up_front, start_q, 0)
    decay[...] = jnp.exp(-rate[...])

    own_kv.wait()
    lax.fori_loop(1, n, recv_kv_wait, 0)

    ext = tok + 2 * ROWS
    came_pos = jnp.transpose(arr_kv[:, 2 * ch :].astype(f32))[0:1, :]
    row = lax.broadcasted_iota(jnp.int32, (ext, 1), 0)
    want = lax.bitwise_and(row, ROWS - 1) * steps + lax.shift_right_logical(row, 3) - 2
    want = jnp.where(want < 0, -100, want).astype(f32)
    place_s[...] = (want == came_pos).astype(f32).astype(bf16)
    rim_row = lax.broadcasted_iota(jnp.int32, (16, 1), 0)
    rim_want = jnp.where(rim_row < 2, rim_row + tok - 2, -100).astype(f32)
    rim_hot = (rim_want == came_pos).astype(f32).astype(bf16)

    def rim_copy(src, dst, k, to):
        return pltpu.make_async_remote_copy(
            src_ref=src, dst_ref=dst, send_sem=rim_sems.at[2 * k], recv_sem=rim_sems.at[2 * k + 1],
            device_id={"ctx": to}, device_id_type=MESH,
        )

    after, before = lax.rem(me + 1, n), lax.rem(me + n - 1, n)

    def rim_kv_tile(c, _):
        cols = pl.ds(pl.multiple_of(c * tile, LANES), tile)
        rim_kv_out[:, cols] = jnp.dot(rim_hot, arr_kv[:, cols], preferred_element_type=f32).astype(bf16)
        return _

    def rim_q_tile(c, _):
        cols = pl.ds(pl.multiple_of(c * tile, LANES), tile)
        rim_q_out[:, cols] = jnp.dot(rim_hot, arr_q[:, cols], preferred_element_type=f32).astype(bf16)
        return _

    lax.fori_loop(0, 2 * ch // tile, rim_kv_tile, 0)
    rim_kv = rim_copy(rim_kv_out, rim_kv_in, 0, after)
    rim_kv.start()
    spans = scan_spans(n)
    cuts = [1]
    for share in PACE:
        cuts.append(min(n, cuts[-1] + share * (n - 1) // 15))
    lax.fori_loop(cuts[1], cuts[2], start_q, 0)
    rim_copy(rim_kv_out, rim_kv_in, 0, before).wait_recv()

    sub = lax.broadcasted_iota(jnp.int32, (ROWS, 1), 0)
    first = jnp.logical_and(sub == 0, me > 0)

    def featured(arr, at, w_at, rim, rim_at):
        x = jnp.dot(place_s[...], arr[:, pl.ds(pl.multiple_of(at, LANES), tile)], preferred_element_type=f32)
        w = convw[:, pl.ds(pl.multiple_of(w_at, LANES), tile)]
        y = w[0:1] * x[2 * ROWS :] + w[1:2] * x[ROWS : ROWS + tok] + w[2:3] * x[:tok]
        if rim is None:
            return y
        edge = rim[:, pl.ds(pl.multiple_of(rim_at, LANES), tile)].astype(f32)
        top = jnp.where(first, w[1:2] * edge[1:2] + w[2:3] * edge[0:1], 0.0)
        nxt = jnp.where(first, w[2:3] * edge[1:2], 0.0)
        return jnp.concatenate([y[:ROWS] + top, y[ROWS : 2 * ROWS] + nxt, y[2 * ROWS :]], axis=0)

    def product_tile(c, _):
        at = c * tile
        k = featured(arr_kv, at, ch + at, rim_kv_in, at)
        v = featured(arr_kv, ch + at, 2 * ch + at, rim_kv_in, ch + at)
        prod[:, pl.ds(pl.multiple_of(at, LANES), tile)] = k * v
        return _

    lax.fori_loop(0, ch // tile, product_tile, 0)
    lax.fori_loop(cuts[2], cuts[3], start_q, 0)

    def spread(ref, k, cols):
        return jnp.broadcast_to(ref[k : k + 1, cols], (ROWS, LANES))

    later = ((ROWS - 1 - sub) * steps).astype(f32)

    def total(terms):
        while len(terms) > 1:
            terms = [a + b for a, b in zip(terms[::2], terms[1::2])] + terms[len(terms) // 2 * 2 :]
        return terms[0]

    def local_tile(c, _):
        cols = pl.ds(pl.multiple_of(c * LANES, LANES), LANES)
        dec = [spread(decay, k, cols) for k in range(poles)]
        res = [spread(resid, k, cols) for k in range(poles)]
        gain = jnp.broadcast_to(skip[pl.ds(pl.multiple_of(c * LANES, LANES), LANES)].reshape(1, LANES), (ROWS, LANES))

        def step(i, st):
            at = pl.ds(pl.multiple_of(i * ROWS, ROWS), ROWS)
            x = prod[at, cols]
            st = tuple(d * s + x for d, s in zip(dec, st))
            filt[at, cols] = gain * x + total([r * s for r, s in zip(res, st)])
            return st

        zero = jnp.zeros((ROWS, LANES), f32)
        st = lax.fori_loop(0, steps, step, (zero,) * poles, unroll=2)
        for k in range(poles):
            state[k, :, cols] = st[k]
            fade = jnp.exp(-rate[k : k + 1, cols] * later)
            own[k : k + 1, cols] = jnp.sum(fade * st[k], axis=0, keepdims=True)
        return _

    half = ch // LANES // 2
    lax.fori_loop(0, half, local_tile, 0)
    lax.fori_loop(cuts[3], cuts[4], start_q, 0)
    lax.fori_loop(half, ch // LANES, local_tile, 0)

    def scan_copy(k, j, to):
        return pltpu.make_async_remote_copy(
            src_ref=tx.at[k], dst_ref=rx.at[3 * k + j - 1], send_sem=scan_send.at[3 * k + j - 1],
            recv_sem=scan_recv.at[3 * k + j - 1], device_id={"ctx": to}, device_id_type=MESH,
        )

    def scan_moves(k, send, act):
        span = spans[k]
        for j in range(1, 4):
            if j * span < n:
                to = me + j * span if send else me - j * span
                act(scan_copy(k, j, lax.rem(to + n, n)))

    acc[0] = jnp.zeros((poles, ch), f32)
    for k, span in enumerate(spans):
        tx[k] = own[...].astype(bf16)
        scan_moves(k, True, lambda copy: copy.start())
        stop = n if k == len(spans) - 1 or 5 + k >= len(cuts) else cuts[5 + k]
        lax.fori_loop(cuts[4 + k] if 4 + k < len(cuts) else n, stop, start_q, 0)
        scan_moves(k, False, lambda copy: copy.wait_recv())
        for j in range(1, 4):
            if j * span < n:
                got = jnp.where(me >= j * span, rx[3 * k + j - 1].astype(f32), 0.0)
                acc[0] = acc[0] + jnp.exp(-rate[...] * float(tok * (j * span - 1))) * got
                if k < len(spans) - 1:
                    own[...] = own[...] + jnp.exp(-rate[...] * float(tok * j * span)) * got

    def carry_tile(c, _):
        cols = pl.ds(pl.multiple_of(c * LANES, LANES), LANES)
        dec = [spread(decay, k, cols) for k in range(poles)]
        start = []
        for k in range(poles):
            r = rate[k : k + 1, cols]
            x = jnp.where(sub == 0, acc[0, k : k + 1, cols], pltpu.roll(state[k, :, cols], 1, 0))
            for by in (1, 2, 4):
                fade = jnp.exp(-r * float(steps * by))
                x = x + jnp.where(sub >= by, fade * pltpu.roll(x, by, 0), 0.0)
            start.append(resid[k : k + 1, cols] * x)

        def step(i, g):
            at = pl.ds(pl.multiple_of(i * ROWS, ROWS), ROWS)
            g = tuple(d * s for d, s in zip(dec, g))
            filt[at, cols] = filt[at, cols] + total(list(g))
            return g

        lax.fori_loop(0, steps, step, tuple(start), unroll=2)
        return _

    lax.fori_loop(0, ch // LANES, carry_tile, 0)

    own_q.wait()
    lax.fori_loop(1, n, recv_q_wait, 0)
    lax.fori_loop(0, ch // tile, rim_q_tile, 0)
    rim_q = rim_copy(rim_q_out, rim_q_in, 1, after)
    rim_q.start()

    def query_tile(c, _):
        at = c * tile
        prod[:, pl.ds(pl.multiple_of(at, LANES), tile)] = featured(arr_q, at, at, None, at)
        return _

    lax.fori_loop(0, ch // tile, query_tile, 0)
    rim_copy(rim_q_out, rim_q_in, 1, before).wait_recv()
    edge = rim_q_in[...].astype(f32)
    w1, w2 = convw[1:2, 0:ch], convw[2:3, 0:ch]
    prod[0:ROWS, :] = prod[0:ROWS, :] + jnp.where(first, w1 * edge[1:2] + w2 * edge[0:1], 0.0)
    prod[ROWS : 2 * ROWS, :] = prod[ROWS : 2 * ROWS, :] + jnp.where(first, w2 * edge[1:2], 0.0)

    nat = lax.broadcasted_iota(jnp.int32, (tok, 1), 0)
    seat = lax.bitwise_and(nat, steps - 1) * ROWS + lax.shift_right_logical(nat, steps.bit_length() - 1)
    order = (seat == lax.broadcasted_iota(jnp.int32, (tok, tok), 1)).astype(f32).astype(bf16)

    def gate_tile(c, _):
        cols = pl.ds(pl.multiple_of(c * tile, LANES), tile)
        rows_g = (prod[:, cols] * filt[:, cols]).astype(bf16)
        natural[:, cols] = jnp.dot(order, rows_g, preferred_element_type=f32).astype(bf16)
        return _

    lax.fori_loop(0, ch // tile, gate_tile, 0)
    w_copy.wait()

    def out_tile(c, _):
        cols = pl.ds(pl.multiple_of(c * tile, LANES), tile)
        out[:, cols] = jnp.dot(natural[...], w_vmem[:, cols], preferred_element_type=f32).astype(bf16)
        return _

    lax.fori_loop(0, ch // tile, out_tile, 0)

    lax.fori_loop(1, n, send_waits, 0)
    rim_kv.wait_send()
    rim_q.wait_send()
    for k in range(len(spans)):
        scan_moves(k, True, lambda copy: copy.wait_send())


def swift(
    n, groups, cap, base, tok,
    counts, feats_hbm, pos, convw, rate, resid, skip, w_hbm, out, most,
    box_a, box_b, box_q, arr_a, arr_b, arr_q, mark_out, mark_in, group_out, group_in,
    hot_s, place_s, prod, filt, gated, natural, state,
    feats, decay, rims_out, rims_in, own, acc, totals, rate4, tx, rx, w_vmem,
    sends, recvs, over_sends, over_recvs, send_m, recv_m, send_g, recv_g, raw, ending, inward, hops, leaps,
    rim_sems, scan_send, scan_recv, self_sems, w_sem, f_sems,
):
    me = lax.axis_index("ctx")
    group = lax.axis_index("groups")
    slots, feat = feats_hbm.shape
    ch = feat // 3
    poles = rate.shape[0]
    steps = tok // ROWS
    tile = col_tile(ch)
    rows = n * cap
    over = cap - base
    half_n = n // 2
    tiles = ch // tile
    lead = (tiles + 1) // 2
    parts = [(0, lead), (lead, tiles)]
    barrier = pltpu.get_barrier_semaphore()
    bits = (n - 1).bit_length()

    def flip(a, m):
        return sum(((a // (1 << b) + m // (1 << b)) % 2) * (1 << b) for b in range(bits))

    def greet(m, c):
        pl.semaphore_signal(barrier, inc=1, device_id={"ctx": flip(me, m)}, device_id_type=MESH)
        return c

    lax.fori_loop(1, n, greet, 0)
    for g in range(1, groups):
        pl.semaphore_signal(barrier, inc=1, device_id={"groups": lax.rem(group + g, groups)}, device_id_type=MESH)
    kv_cols = pl.ds(ch, 2 * ch)
    f_kv = pltpu.make_async_copy(feats_hbm.at[:, kv_cols], feats.at[:, kv_cols], f_sems.at[0])
    f_q = pltpu.make_async_copy(feats_hbm.at[:, pl.ds(0, ch)], feats.at[:, pl.ds(0, ch)], f_sems.at[1])
    f_kv.start()
    f_q.start()
    w_copy = pltpu.make_async_copy(w_hbm, w_vmem, w_sem)
    w_copy.start()

    p = pos[...].reshape(1, slots)
    shift = tok.bit_length() - 1
    live = lax.broadcasted_iota(jnp.int32, (1, slots), 1) < counts[0]
    owner = jnp.where(live, lax.shift_right_logical(p, shift), -1)
    local = lax.bitwise_and(p, tok - 1).astype(f32)
    mine = owner == lax.broadcasted_iota(jnp.int32, (n, slots), 0)
    tri = lax.broadcasted_iota(jnp.int32, (slots, slots), 0) <= lax.broadcasted_iota(
        jnp.int32, (slots, slots), 1
    )
    tri = tri.astype(f32).astype(bf16)
    cum = jnp.dot(mine.astype(f32).astype(bf16), tri, preferred_element_type=f32)
    rank = jnp.sum(jnp.where(mine, cum, 0.0), axis=0, keepdims=True) - 1.0
    direct = jnp.logical_and(live, rank < float(base))
    beyond = jnp.logical_and(live, rank >= float(base)).astype(f32)
    bump = jnp.dot(jnp.broadcast_to(beyond, (16, slots)).astype(bf16), tri, preferred_element_type=f32)[0:1]
    late = jnp.where(beyond > 0.0, bump - 1.0, -1.0)
    apart = lax.bitwise_xor(owner, me)
    flat = jnp.where(direct, apart.astype(f32) * float(cap) + rank, -1.0)
    spare = jnp.where(late >= 0.0, late + float(base), -1.0)
    hot_row = lax.broadcasted_iota(jnp.int32, (rows, slots), 0)
    hit = jnp.logical_or(hot_row.astype(f32) == flat, lax.bitwise_and(hot_row, cap - 1).astype(f32) == spare)
    hot_s[...] = hit.astype(f32).astype(bf16)

    def pack_rows(box, first, count, source):
        def pack(c, _):
            at = pl.ds(first, rows // 2)
            src = pl.ds(pl.multiple_of(source(c), LANES), tile)
            dst = pl.ds(pl.multiple_of(c * tile, LANES), tile)
            box[at, dst] = jnp.dot(hot_s[at, :], feats[:, src], preferred_element_type=f32).astype(bf16)
            return _

        lax.fori_loop(0, count, pack, 0)

    def pack_kv(i, first):
        t0, t1 = parts[i]
        count = t1 - t0
        pack_rows(boxes[i], first, 2 * count, lambda c: ch + (c // count) * ch + (t0 + c % count) * tile)

    boxes = (box_a, box_b, box_q)
    arrs = (arr_a, arr_b, arr_q)

    def slab(ref, k, size):
        return ref.at[pl.ds(pl.multiple_of(k * cap, cap), size), :]

    def over_rows(ref, k):
        return ref.at[pl.ds(pl.multiple_of(k * cap + base, ROWS), over), :]

    def direct_copy(which, m, size, came):
        box, arr, send, recv = boxes[which], arrs[which], sends.at[which], recvs.at[which]
        to = flip(me, m)
        return pltpu.make_async_remote_copy(
            src_ref=slab(box, m, size), dst_ref=slab(arr, to if came else me, size), send_sem=send.at[m],
            recv_sem=recv.at[m], device_id={"ctx": to}, device_id_type=MESH,
        )

    def to_mirror(which, came):
        box, arr, send, recv = boxes[which], arrs[which], over_sends.at[which], over_recvs.at[which]
        to = flip(me, half_n)
        return pltpu.make_async_remote_copy(
            src_ref=over_rows(box, half_n), dst_ref=over_rows(arr, to if came else me), send_sem=send.at[0],
            recv_sem=recv.at[0], device_id={"ctx": to}, device_id_type=MESH,
        )

    def forward(which, m, came):
        arr, send, recv = arrs[which], over_sends.at[which], over_recvs.at[which]
        to = flip(me, m)
        rows_of = over_rows(arr, flip(to if came else me, half_n))
        return pltpu.make_async_remote_copy(
            src_ref=rows_of, dst_ref=rows_of, send_sem=send.at[m], recv_sem=recv.at[m],
            device_id={"ctx": to}, device_id_type=MESH,
        )

    in_a, in_b, in_q = 0, 1, 2

    def each(first, last, make, act):
        def one(m, c):
            act(make(m))
            return c

        lax.fori_loop(first, last, one, 0)

    def start(copy):
        copy.start()

    def arrive(copy):
        copy.wait_recv()

    def sent(copy):
        copy.wait_send()

    def near(which, came=False):
        return lambda m: direct_copy(which, m, cap, came)

    def far(which, came=False):
        return lambda m: direct_copy(which, m, base, came)

    def spread_over(which, came=False):
        return lambda m: forward(which, m, came)

    def marks_to(m, to, came):
        return pltpu.make_async_remote_copy(
            src_ref=mark_out.at[to], dst_ref=mark_in.at[came], send_sem=send_m.at[m], recv_sem=recv_m.at[m],
            device_id={"ctx": to}, device_id_type=MESH,
        )

    def start_marks(m, c):
        marks_to(m, flip(me, m), me).start()
        return c

    def recv_marks(m, c):
        marks_to(m, flip(me, m), flip(me, m)).wait_recv()
        return c

    def own_copy(i):
        return pltpu.make_async_copy(slab(boxes[i], 0, cap), slab(arrs[i], me, cap), self_sems.at[i])

    f_kv.wait()
    pack_kv(in_a, rows // 2)
    pl.semaphore_wait(barrier, n - 1 + groups - 1)
    to_mirror(in_a, False).start()
    each(half_n, n, far(in_a), start)
    pack_kv(in_a, 0)
    each(1, half_n, near(in_a), start)
    own_copy(in_a).start()

    seats = (lax.broadcasted_iota(jnp.int32, (LANES, slots), 0) - lax.rem(me * cap, LANES)).astype(f32)
    in_slab = jnp.logical_and(seats >= 0.0, seats < float(cap))
    at_base = jnp.logical_and(direct, seats == rank)
    at_over = jnp.logical_and(in_slab, jnp.logical_and(late >= 0.0, seats - float(base) == late))
    last_dims = (((1,), (1,)), ((), ()))
    sub16 = lax.broadcasted_iota(jnp.int32, (16, slots), 0)
    two = jnp.where(sub16 == 0, local + 1.0, jnp.where(sub16 == 1, owner.astype(f32), 0.0)).astype(bf16)
    tell = lax.dot_general(
        jnp.where(mine, local + 1.0, 0.0).astype(bf16), at_base.astype(f32).astype(bf16), last_dims,
        preferred_element_type=f32,
    )
    tell = jnp.where(tell > 0.0, tell + (lax.broadcasted_iota(jnp.int32, (n, LANES), 0) * tok).astype(f32), 0.0)
    extra = lax.dot_general(two, at_over.astype(f32).astype(bf16), last_dims, preferred_element_type=f32)
    tell = tell + (extra[0:1] + extra[1:2] * float(tok))
    held = jnp.broadcast_to(jnp.sum(beyond, axis=1, keepdims=True), (1, LANES))
    for k in range(n):
        mark_out[k, 0:1, :] = tell[k : k + 1, :]
        mark_out[k, 1:2, :] = held
    mark_in[me] = mark_out[me]
    lax.fori_loop(1, n, start_marks, 0)

    pack_kv(in_b, rows // 2)
    to_mirror(in_b, False).start()
    to_mirror(in_a, True).wait_recv()
    each(1, half_n, spread_over(in_a), start)
    cuts = [half_n]
    for share in FLOW:
        cuts.append(min(n, cuts[-1] + share * half_n // 8))
    early = EARLY * half_n // 8
    each(half_n, half_n + early, far(in_b), start)
    pack_kv(in_b, 0)
    own_copy(in_b).start()
    f_q.wait()
    pack_rows(box_q, rows // 2, tiles, lambda c: c * tile)
    to_mirror(in_q, False).start()
    pack_rows(box_q, 0, tiles, lambda c: c * tile)
    own_copy(in_q).start()
    to_mirror(in_b, True).wait_recv()
    each(1, half_n, spread_over(in_b), start)
    decay[...] = jnp.exp(-rate[...])
    sub = lax.broadcasted_iota(jnp.int32, (ROWS, 1), 0)
    first = jnp.logical_and(sub == 0, me > 0)
    later = ((ROWS - 1 - sub) * steps).astype(f32)
    segment = (sub * steps).astype(f32)
    member, level = me % QUAD, me // QUAD
    levels = n // QUAD
    share = poles // QUAD
    for q in range(QUAD):
        rate4[q] = rate[q * share : (q + 1) * share, :]
    lags = [1, 2, 3] + [QUAD * j for j in range(1, levels - 1)]
    for at, lag in enumerate(lags):
        leaps[at] = jnp.exp(-rate4[member] * float(tok * lag))
    for at, by in enumerate((1, 2, 4)):
        hops[at] = jnp.exp(-rate[...] * float(steps * by))

    def fades_of(k, _):
        r = rate[pl.ds(k, 1), :]
        ending[k] = jnp.exp(-r * later)
        inward[k] = resid[pl.ds(k, 1), :] * jnp.exp(-r * segment)
        return _

    lax.fori_loop(0, poles, fades_of, 0)

    lax.fori_loop(1, n, recv_marks, 0)
    lanes_of = [
        sum(mark_in[k, 0:1, :] for k in range(g * (LANES // cap), (g + 1) * (LANES // cap)))
        for g in range(rows // LANES)
    ]
    came_pos = jnp.concatenate(lanes_of, axis=1) - 1.0
    worst = mark_in[0, 1:2, :]
    for k in range(1, n):
        worst = jnp.maximum(worst, mark_in[k, 1:2, :])
    group_out[...] = jnp.broadcast_to(worst, (ROWS, LANES))

    def group_copy(g, to):
        return pltpu.make_async_remote_copy(
            src_ref=group_out, dst_ref=group_in.at[g], send_sem=send_g.at[g], recv_sem=recv_g.at[g],
            device_id={"groups": to}, device_id_type=MESH,
        )

    for g in range(1, groups):
        group_copy(g, lax.rem(group + g, groups)).start()

    ext = tok + 2 * ROWS
    row = lax.broadcasted_iota(jnp.int32, (ext, 1), 0)
    want = lax.bitwise_and(row, ROWS - 1) * steps + lax.shift_right_logical(row, 3) - 2
    want = jnp.where(want < 0, -100, want + me * tok).astype(f32)
    place_s[...] = (want == came_pos).astype(f32).astype(bf16)
    rim_row = lax.broadcasted_iota(jnp.int32, (16, 1), 0)
    rim_want = jnp.where(rim_row < 2, rim_row + me * tok + tok - 2, -100).astype(f32)
    rim_hot = (rim_want == came_pos).astype(f32).astype(bf16)

    to_mirror(in_q, True).wait_recv()
    each(1, half_n, spread_over(in_q), start)

    def take_then_send(which, then, ahead, first_sent):
        each(half_n, n - ahead, far(which, True), arrive)

        def both(m, c):
            far(which, True)(m).wait_recv()
            far(then)(m - n + ahead + first_sent).start()
            return c

        lax.fori_loop(n - ahead, n, both, 0)

    own_copy(in_a).wait()
    each(1, half_n, near(in_b), start)
    each(1, half_n, near(in_a, True), arrive)
    each(1, half_n, spread_over(in_a, True), arrive)
    take_then_send(in_a, in_b, half_n - early, half_n + early)

    def rim_copy(i, to):
        wide = (2 * (parts[i][1] - parts[i][0]) if i < len(parts) else tiles) * tile
        cols = pl.ds((2 * parts[i][0] if i < len(parts) else 2 * tiles) * tile, wide)
        return pltpu.make_async_remote_copy(
            src_ref=rims_out.at[:, cols], dst_ref=rims_in.at[:, cols], send_sem=rim_sems.at[2 * i],
            recv_sem=rim_sems.at[2 * i + 1], device_id={"ctx": to}, device_id_type=MESH,
        )

    after, before = lax.rem(me + 1, n), lax.rem(me + n - 1, n)

    def rim_send(i):
        count = 2 * (parts[i][1] - parts[i][0]) if i < len(parts) else tiles
        base_tile = 2 * parts[i][0] if i < len(parts) else 2 * tiles

        def fill(c, _):
            src = pl.ds(pl.multiple_of(c * tile, LANES), tile)
            dst = pl.ds(pl.multiple_of((base_tile + c) * tile, LANES), tile)
            rims_out[:, dst] = jnp.dot(rim_hot, arrs[i][:, src], preferred_element_type=f32)[0:ROWS].astype(bf16)
            return _

        lax.fori_loop(0, count, fill, 0)
        rim_copy(i, after).start()

    def featured(arr, at, w_at):
        x = jnp.dot(place_s[...], arr[:, pl.ds(pl.multiple_of(at, LANES), tile)], preferred_element_type=f32)
        w = convw[:, pl.ds(pl.multiple_of(w_at, LANES), tile)]
        return w[0:1] * x[2 * ROWS :] + w[1:2] * x[ROWS : ROWS + tok] + w[2:3] * x[:tok]

    def product(i):
        t0, t1 = parts[i]
        wide = (t1 - t0) * tile

        def product_tile(c, _):
            at = (c - t0) * tile
            k = featured(arrs[i], at, ch + c * tile)
            v = featured(arrs[i], wide + at, 2 * ch + c * tile)
            raw[:, pl.ds(pl.multiple_of(c * tile, LANES), tile)] = k[: 2 * ROWS]
            raw[:, pl.ds(pl.multiple_of(ch + c * tile, LANES), tile)] = v[: 2 * ROWS]
            prod[:, pl.ds(pl.multiple_of(c * tile, LANES), tile)] = k * v
            return _

        lax.fori_loop(t0, t1, product_tile, 0)

    def product_edges(i):
        t0, t1 = parts[i]
        wide = (t1 - t0) * tile
        rim_copy(i, before).wait_recv()

        def edge_tile(c, _):
            def with_edge(at, rim_at):
                cols = pl.ds(pl.multiple_of(at, LANES), tile)
                w = convw[:, pl.ds(pl.multiple_of(ch + at, LANES), tile)]
                edge = rims_in[:, pl.ds(pl.multiple_of(rim_at, LANES), tile)].astype(f32)
                top = jnp.where(first, w[1:2] * edge[1:2] + w[2:3] * edge[0:1], 0.0)
                nxt = jnp.where(first, w[2:3] * edge[1:2], 0.0)
                return jnp.concatenate([raw[0:ROWS, cols] + top, raw[ROWS:, cols] + nxt], axis=0)

            rim_at = (2 * t0 + c - t0) * tile
            prod[0 : 2 * ROWS, pl.ds(pl.multiple_of(c * tile, LANES), tile)] = with_edge(
                c * tile, rim_at
            ) * with_edge(ch + c * tile, rim_at + wide)
            return _

        lax.fori_loop(t0, t1, edge_tile, 0)

    def spread(ref, k, cols):
        return jnp.broadcast_to(ref[k : k + 1, cols], (ROWS, LANES))

    def total(terms):
        while len(terms) > 1:
            terms = [a + b for a, b in zip(terms[::2], terms[1::2])] + terms[len(terms) // 2 * 2 :]
        return terms[0]

    def local_tile(c, _):
        cols = pl.ds(pl.multiple_of(c * LANES, LANES), LANES)
        dec = [spread(decay, k, cols) for k in range(poles)]
        res = [spread(resid, k, cols) for k in range(poles)]
        gain = jnp.broadcast_to(skip[pl.ds(pl.multiple_of(c * LANES, LANES), LANES)].reshape(1, LANES), (ROWS, LANES))

        def step(i, st):
            at = pl.ds(pl.multiple_of(i * ROWS, ROWS), ROWS)
            x = prod[at, cols]
            st = tuple(d * s + x for d, s in zip(dec, st))
            filt[at, cols] = gain * x + total([r * s for r, s in zip(res, st)])
            return st

        zero = jnp.zeros((ROWS, LANES), f32)
        st = lax.fori_loop(0, steps, step, (zero,) * poles, unroll=4)
        for k in range(poles):
            state[k, :, cols] = st[k]
            own[k : k + 1, cols] = jnp.sum(ending[k, :, cols] * st[k], axis=0, keepdims=True)
        return _

    def prefix_tile(c, _):
        cols = pl.ds(pl.multiple_of(c * LANES, LANES), LANES)
        for k in range(poles):
            x = jnp.where(sub == 0, 0.0, pltpu.roll(state[k, :, cols], 1, 0))
            for at, by in enumerate((1, 2, 4)):
                x = x + jnp.where(sub >= by, hops[at, k : k + 1, cols] * pltpu.roll(x, by, 0), 0.0)
            state[k, :, cols] = resid[k : k + 1, cols] * x
        return _

    per = tile // LANES

    def lanes(part):
        return pl.ds(part[0] * tile, (part[1] - part[0]) * tile)

    def scan_copy(part, stage, j, out_way):
        cols = lanes(part)
        here = member if stage != 1 else level
        count = QUAD if stage != 1 else levels
        peer = lax.rem(here + (j if out_way else count - j), count)
        to = level * QUAD + peer if stage != 1 else peer * QUAD + member
        start_at = stage * max(QUAD, levels)
        source, slot = (totals.at[0, :, cols], start_at + here) if stage == 1 else (
            tx.at[stage // 2 * QUAD + peer, :, cols], start_at + here)
        if not out_way:
            slot = start_at + peer
        at = (start_at + j) * len(parts) + parts.index(part)
        return pltpu.make_async_remote_copy(
            src_ref=source, dst_ref=rx.at[slot, :, cols], send_sem=scan_send.at[at],
            recv_sem=scan_recv.at[at], device_id={"ctx": to}, device_id_type=MESH,
        )

    def scan_moves(part, stage, out_way, act):
        for j in range(1, QUAD if stage != 1 else levels):
            act(scan_copy(part, stage, j, out_way))

    def leap(lag, cols):
        return leaps[lags.index(lag), :, cols]

    def scan_open(part):
        cols = lanes(part)
        for q in range(QUAD):
            tx[q, :, cols] = own[q * share : (q + 1) * share, cols]
        rx[member, :, cols] = tx[member, :, cols]
        scan_moves(part, 0, True, start)

    def scan_totals(part):
        cols = lanes(part)
        scan_moves(part, 0, False, arrive)
        t = rx[QUAD - 1, :, cols]
        for i in range(QUAD - 1):
            t = t + leap(QUAD - 1 - i, cols) * rx[i, :, cols]
        totals[0, :, cols] = t
        scan_moves(part, 1, True, start)

    def scan_carries(part):
        cols = lanes(part)
        scan_moves(part, 1, False, arrive)
        carried = jnp.zeros((share, (part[1] - part[0]) * tile), f32)
        for j in range(1, levels):
            got = rx[max(QUAD, levels) + lax.rem(level + levels - j, levels), :, cols]
            got = got if j == 1 else leap(QUAD * (j - 1), cols) * got
            carried = carried + jnp.where(level >= j, got, 0.0)
        for i in range(QUAD):
            tx[QUAD + i, :, cols] = carried
            carried = rx[i, :, cols] + leap(1, cols) * carried
        rx[2 * max(QUAD, levels) + member, :, cols] = tx[QUAD + member, :, cols]
        scan_moves(part, 2, True, start)

    def scan_close(part):
        cols = lanes(part)
        scan_moves(part, 2, False, arrive)
        for q in range(QUAD):
            acc[q * share : (q + 1) * share, cols] = rx[2 * max(QUAD, levels) + q, :, cols]


    def local(part):
        lax.fori_loop(part[0] * per, part[1] * per, local_tile, 0)

    def prefix(part):
        lax.fori_loop(part[0] * per, part[1] * per, prefix_tile, 0)

    part_a, part_b = parts
    def carry_tile(c, _):
        cols = pl.ds(pl.multiple_of(c * LANES, LANES), LANES)
        dec = [spread(decay, k, cols) for k in range(poles)]
        begin = tuple(
            state[k, :, cols] + inward[k, :, cols] * acc[k : k + 1, cols] for k in range(poles)
        )

        def step(i, g):
            at = pl.ds(pl.multiple_of(i * ROWS, ROWS), ROWS)
            g = tuple(d * s for d, s in zip(dec, g))
            filt[at, cols] = filt[at, cols] + total(list(g))
            return g

        lax.fori_loop(0, steps, step, begin, unroll=4)
        return _

    def carry(part):
        scan_close(part)
        lax.fori_loop(part[0] * per, part[1] * per, carry_tile, 0)

    rim_send(in_a)
    product(in_a)
    product_edges(in_a)
    local(part_a)
    scan_open(part_a)
    prefix(part_a)
    own_copy(in_b).wait()
    each(1, half_n, near(in_b, True), arrive)
    each(1, half_n, near(in_q), start)
    each(half_n, cuts[1], far(in_q), start)
    each(1, half_n, spread_over(in_b, True), arrive)
    take_then_send(in_b, in_q, cuts[2] - cuts[1], cuts[1])
    rim_send(in_b)
    scan_totals(part_a)
    product(in_b)
    each(cuts[2], cuts[3], far(in_q), start)
    product_edges(in_b)
    local(part_b)
    scan_open(part_b)
    each(cuts[3], cuts[4], far(in_q), start)
    prefix(part_b)
    scan_carries(part_a)
    scan_totals(part_b)
    each(cuts[4], cuts[5], far(in_q), start)
    carry(part_a)
    scan_carries(part_b)
    each(cuts[5], n, far(in_q), start)
    carry(part_b)
    top_of = worst
    for g in range(1, groups):
        group_copy(g, lax.rem(group + groups - g, groups)).wait_recv()
        top_of = jnp.maximum(top_of, group_in[g, 0:1, :])
    most[0] = jnp.max(top_of).astype(jnp.int32)
    w_copy.wait()

    own_copy(in_q).wait()
    each(1, half_n, near(in_q, True), arrive)
    each(1, half_n, spread_over(in_q, True), arrive)
    each(half_n, n, far(in_q, True), arrive)
    rim_send(in_q)

    def gate_tile(c, _):
        at = c * tile
        cols = pl.ds(pl.multiple_of(at, LANES), tile)
        y = featured(arr_q, at, at)
        raw[:, cols] = y[: 2 * ROWS]
        gated[:, cols] = (y * filt[:, cols]).astype(bf16)
        return _

    lax.fori_loop(0, ch // tile, gate_tile, 0)
    rim_copy(in_q, before).wait_recv()
    edge = rims_in[:, 2 * ch :].astype(f32)
    w1, w2 = convw[1:2, 0:ch], convw[2:3, 0:ch]
    top = jnp.where(first, w1 * edge[1:2] + w2 * edge[0:1], 0.0)
    nxt = jnp.where(first, w2 * edge[1:2], 0.0)
    begun = raw[:, 0:ch] + jnp.concatenate([top, nxt], axis=0)
    gated[0 : 2 * ROWS, :] = (begun * filt[0 : 2 * ROWS, :]).astype(bf16)

    nat = lax.broadcasted_iota(jnp.int32, (tok, 1), 0)
    seat = lax.bitwise_and(nat, steps - 1) * ROWS + lax.shift_right_logical(nat, steps.bit_length() - 1)
    order = (seat == lax.broadcasted_iota(jnp.int32, (tok, tok), 1)).astype(f32).astype(bf16)

    def order_tile(c, _):
        cols = pl.ds(pl.multiple_of(c * tile, LANES), tile)
        natural[:, cols] = jnp.dot(order, gated[:, cols], preferred_element_type=f32).astype(bf16)
        return _

    lax.fori_loop(0, ch // tile, order_tile, 0)

    wide = 640 if ch % 640 == 0 else tile

    def out_tile(c, _):
        cols = pl.ds(pl.multiple_of(c * wide, LANES), wide)
        out[:, cols] = jnp.dot(natural[...], w_vmem[:, cols], preferred_element_type=f32).astype(bf16)
        return _

    lax.fori_loop(0, ch // wide, out_tile, 0)

    for which in (in_a, in_b, in_q):
        each(1, half_n, near(which), sent)
        each(half_n, n, far(which), sent)
    for which in (in_a, in_b, in_q):
        to_mirror(which, False).wait_send()
        each(1, half_n, spread_over(which), sent)
    each(1, n, lambda m: marks_to(m, flip(me, m), me), sent)
    for g in range(1, groups):
        group_copy(g, lax.rem(group + g, groups)).wait_send()
    for which in (in_a, in_b, in_q):
        rim_copy(which, after).wait_send()
    for stage in range(3):
        for part in parts:
            scan_moves(part, stage, True, sent)


def swift_call(n, groups, cap, base, tok, args):
    counts, features, positions, conv_weight, pole_rate, pole_residue, skip_gain, out_weight = args
    slots, feat = features.shape
    ch = feat // 3
    poles = pole_rate.shape[0]
    rows = n * cap
    share = poles // QUAD
    wide = max(QUAD, n // QUAD)
    lead = (ch // col_tile(ch) + 1) // 2 * col_tile(ch)
    whole = pl.BlockSpec(memory_space=pltpu.VMEM)
    dma = pltpu.SemaphoreType.DMA
    vmem = pltpu.VMEM
    return pl.pallas_call(
        functools.partial(swift, n, groups, cap, base, tok),
        out_shape=(jax.ShapeDtypeStruct((tok, ch), bf16), jax.ShapeDtypeStruct((1,), jnp.int32)),
        in_specs=[pl.BlockSpec(memory_space=pltpu.SMEM), pl.BlockSpec(memory_space=pl.ANY)]
        + [whole] * 5 + [pl.BlockSpec(memory_space=pl.ANY)],
        out_specs=(whole, pl.BlockSpec(memory_space=pltpu.SMEM)),
        scratch_shapes=[
            vmem((rows, 2 * lead), bf16),
            vmem((rows, 2 * (ch - lead)), bf16),
            vmem((rows, ch), bf16),
            vmem((rows, 2 * lead), bf16),
            vmem((rows, 2 * (ch - lead)), bf16),
            vmem((rows, ch), bf16),
            vmem((n, 2, LANES), f32),
            vmem((n, 2, LANES), f32),
            vmem((ROWS, LANES), f32),
            vmem((groups, ROWS, LANES), f32),
            vmem((rows, slots), bf16),
            vmem((tok + 2 * ROWS, rows), bf16),
            vmem((tok, ch), f32),
            vmem((tok, ch), f32),
            vmem((tok, ch), bf16),
            vmem((tok, ch), bf16),
            vmem((poles, ROWS, ch), f32),
            vmem((slots, feat), bf16),
            vmem((poles, ch), f32),
            vmem((ROWS, feat), bf16),
            vmem((ROWS, feat), bf16),
            vmem((poles, ch), f32),
            vmem((poles, ch), f32),
            vmem((1, share, ch), f32),
            vmem((QUAD, share, ch), f32),
            vmem((2 * QUAD, share, ch), f32),
            vmem((3 * wide, share, ch), f32),
            vmem(out_weight.shape, bf16),
            dma((3, n)), dma((3, n)), dma((3, n)), dma((3, n)), dma((n,)), dma((n,)), dma((groups,)), dma((groups,)),
            vmem((2 * ROWS, 2 * ch), f32),
            vmem((poles, ROWS, ch), f32),
            vmem((poles, ROWS, ch), f32),
            vmem((3, poles, ch), f32),
            vmem((2 + n // QUAD, share, ch), f32),
            dma((6,)), dma((6 * wide,)), dma((6 * wide,)), dma((3,)), dma, dma((2,)),
        ],
        compiler_params=pltpu.CompilerParams(
            collective_id=1, has_side_effects=True, vmem_limit_bytes=60 << 20
        ),
        name="hyena_direct",
    )(*args)


def mega_call(n, cap, tok, args):
    counts, features, positions, conv_weight, pole_rate, pole_residue, skip_gain, out_weight = args
    slots, feat = features.shape
    ch = feat // 3
    poles = pole_rate.shape[0]
    rows = n * cap
    stages = len(scan_spans(n))
    whole = pl.BlockSpec(memory_space=pltpu.VMEM)
    dma = pltpu.SemaphoreType.DMA
    return pl.pallas_call(
        functools.partial(mega, n, cap, tok, PACE[0] * (n - 1) // 15),
        out_shape=jax.ShapeDtypeStruct((tok, ch), bf16),
        in_specs=[pl.BlockSpec(memory_space=pltpu.SMEM), pl.BlockSpec(memory_space=pl.ANY)]
        + [whole] * 5 + [pl.BlockSpec(memory_space=pl.ANY)],
        out_specs=whole,
        scratch_shapes=[
            pltpu.VMEM((rows, 2 * ch + LANES), bf16),
            pltpu.VMEM((rows, ch), bf16),
            pltpu.VMEM((rows, 2 * ch + LANES), bf16),
            pltpu.VMEM((rows, ch), bf16),
            pltpu.VMEM((rows, slots), bf16),
            pltpu.VMEM((tok + 2 * ROWS, rows), bf16),
            pltpu.VMEM((tok, ch), f32),
            pltpu.VMEM((tok, ch), f32),
            pltpu.VMEM((16, LANES), bf16),
            pltpu.VMEM((tok, ch), bf16),
            pltpu.VMEM((poles, ROWS, ch), f32),
            pltpu.VMEM((slots, feat), bf16),
            pltpu.VMEM((poles, ch), f32),
            pltpu.VMEM((16, 2 * ch), bf16),
            pltpu.VMEM((16, 2 * ch), bf16),
            pltpu.VMEM((16, ch), bf16),
            pltpu.VMEM((16, ch), bf16),
            pltpu.VMEM((poles, ch), f32),
            pltpu.VMEM((1, poles, ch), f32),
            pltpu.VMEM((stages, poles, ch), bf16),
            pltpu.VMEM((3 * stages, poles, ch), bf16),
            pltpu.VMEM(out_weight.shape, bf16),
            dma((n,)), dma((n,)), dma((n,)), dma((n,)), dma((4,)), dma((3 * stages,)), dma((3 * stages,)),
            dma((2,)), dma, dma((2,)),
        ],
        compiler_params=pltpu.CompilerParams(
            collective_id=0, has_side_effects=True, vmem_limit_bytes=60 << 20
        ),
        name="hyena",
    )(*args)


def on_device(
    features, positions, counts, conv_weight, pole_rate, pole_residue, skip_gain, out_weight
):
    n = lax.axis_size("ctx")
    groups = lax.axis_size("groups")
    slots, feat = features.shape
    ch = feat // 3
    tok = 2 * slots // 3
    cap = 2 * tok // n
    poles = pole_rate.shape[0]
    if cap % 16 or tok & (tok - 1) or tok > 256 or conv_weight.shape[0] != 3 or ch % LANES or n & (n - 1) or n < 4:
        return plain_on_device(
            features, positions, counts, conv_weight, pole_rate, pole_residue, skip_gain, out_weight
        )
    args = (counts, features, positions, conv_weight, pole_rate, pole_residue, skip_gain, out_weight)
    base = slots // n
    if poles % QUAD or base % ROWS or cap - base > 16 or LANES % cap:
        return mega_call(n, cap, tok, args)
    done, most = swift_call(n, groups, cap, base, tok, args)
    return lax.cond(most[0] > cap - base, lambda d: mega_call(n, cap, tok, args), lambda d: d, done)


PACE = (2, 1, 1, 2, 2)
FLOW = (0, 2, 1, 1, 2)
EARLY = 0
QUAD = 4


def solution(mesh):
    return jax.shard_map(
        on_device,
        mesh=mesh,
        in_specs=(
            P(("groups", "ctx"), None),
            P(("groups", "ctx")),
            P(("groups", "ctx")),
            P(),
            P(),
            P(),
            P(),
            P(),
        ),
        out_specs=P(("groups", "ctx"), None),
        check_vma=False,
    )
```
